32 devices in a mesh: gx: 16 (over z, y, core), gy: 2 (over x).
Axes of the slice: x: 2, y: 2, z: 4, core: 2. Of those that a mesh axis runs over, the one named last changes fastest.
Arguments:
- cell_bin: int32 [524288], P(('gx', 'gy')), may hold values from 0 to 8191
- cell_layer: int32 [524288], P(('gx', 'gy')), may hold values from 0 to 7
- cell_offset: int32 [524288], P(('gx', 'gy')), may hold values from 0 to 8, as said below
- cell_power: float32 [524288], P(('gx', 'gy')), may hold values from 1 to 10
- spill_weight: float32 [524288], P(('gx', 'gy')), may hold values from 0.05 to 0.5
- conductivity: float32 [8, 512, 512], P(None, 'gx', 'gy'), may hold values from 0.5 to 2
- layer_coupling: float32 [7], replicated, may hold values from 0.5 to 2
Outputs:
- final_warmth: float32 [8, 512, 512], P(None, 'gx', 'gy')
- warmth_driven_pull: float32 [2, 524288], P(None, ('gx', 'gy'))
The draws below stay inside these ranges and needn't reach their ends.
Inputs may be any that keep to these rules, and one draw needn't show every extreme that they name: `cell_offset`: an offset never points outside the grid of tiles; among the cells held by one tile at most 2048 have any one offset other than 4, and in every draw each tile has some offset held by exactly 2048 of its cells, and some tile receives exactly 2048 cells from each of its neighbouring tiles.
All inputs are finite; a program needn't handle non-finite values.
Results may differ from the reference program's by a relative error of at most 0.00002.
Values sent between devices are 32-bit elements; how exact they have to be, the bound alone decides.
No kernel may reach another device: no remote copies, remote signals or barrier semaphores. Data moves between devices by JAX's collectives and lax.ppermute only.
A program may use at most 64 MiB of HBM per device.

```python
import math
import jax
import jax.numpy as jnp

LAYERS = 8
TC = 32
TR = 256
C_DEV = 16384
ITERS = 4
CAP = 2048
NC = 512
NR = 512
CELLS = 524288
N_GX = 16
N_GY = 2


def draw_cell_offset(key, part):
    device_count = N_GX * N_GY
    device_ids = jnp.arange(device_count, dtype=jnp.int32)
    offset_codes = jnp.arange(9, dtype=jnp.int32)
    target_column = (device_ids // N_GY)[:, None] + offset_codes[None, :] // 3 - 1
    target_row = (device_ids % N_GY)[:, None] + offset_codes[None, :] % 3 - 1
    allowed = (target_column >= 0) & (target_column < N_GX) & (target_row >= 0) & (target_row < N_GY) & (offset_codes[None, :] != 4)
    key_count, key_pick, key_focus_col, key_focus_row, key_shuffle = jax.random.split(jax.random.fold_in(key, 11), 5)
    counts = jax.random.randint(key_count, (device_count, 9), 0, CAP + 1)
    scores = jax.random.randint(key_pick, (device_count, 9), 0, 1024) * 16 + offset_codes[None, :]
    scores = jnp.where(allowed, scores, -1)
    forced = offset_codes[None, :] == jnp.argmax(scores, axis=1)[:, None]
    focus_column = jax.random.randint(key_focus_col, (), 0, N_GX)
    focus_row = jax.random.randint(key_focus_row, (), 0, N_GY)
    toward_focus = (target_column == focus_column) & (target_row == focus_row)
    counts = jnp.where(allowed, jnp.where(forced | toward_focus, CAP, counts), 0)
    bounds = jnp.cumsum(counts, axis=1)
    positions = jnp.arange(C_DEV, dtype=jnp.int32)
    chosen = jax.vmap(lambda row_bounds: jnp.searchsorted(row_bounds, positions, side='right'))(bounds).astype(jnp.int32)
    chosen = jnp.where(chosen >= 9, 4, chosen)
    shuffle_keys = jax.random.randint(key_shuffle, (device_count, C_DEV), 0, 2 ** 31 // C_DEV) * C_DEV + positions[None, :]
    order_ids = jnp.argsort(shuffle_keys, axis=1, stable=True)
    return jnp.take_along_axis(chosen, order_ids, axis=1).reshape(-1).astype(jnp.int32)


def place_ends(drawn, stream_key, low, top_value):
    extent = drawn.shape
    place = [jax.random.randint(jax.random.fold_in(stream_key, axis), (), 0, extent[axis]) for axis in range(len(extent))]
    drawn = drawn.at[tuple(place)].set(low)
    longest = extent.index(max(extent))
    place[longest] = (place[longest] + 1) % extent[longest]
    return drawn.at[tuple(place)].set(top_value)


def shard_levels(rng, extent, cuts, least, top_value):
    loudness, own = 1.0, jax.random.fold_in(rng, 6)
    for dim, shards_of in cuts:
        draws = jnp.exp(jax.random.uniform(jax.random.fold_in(own, dim), (shards_of,), jnp.float32, least / len(cuts), top_value / len(cuts)))
        loudness = loudness * jnp.repeat(draws, extent[dim] // shards_of).reshape([-1 if axis == dim else 1 for axis in range(len(extent))])
    return loudness


def setup_inputs(seed: int = 0) -> dict:
    keys = jax.random.split(jax.random.key(seed), 8)
    return {
        "cell_bin": place_ends(jax.random.randint(keys[0], (CELLS,), 0, TC * TR), jax.random.fold_in(keys[0], 1), 0, (TC * TR) - 1).astype(jnp.int32),
        "cell_layer": place_ends(jax.random.randint(keys[1], (CELLS,), 0, LAYERS), jax.random.fold_in(keys[1], 1), 0, LAYERS - 1).astype(jnp.int32),
        "cell_offset": draw_cell_offset(jax.random.fold_in(keys[7], 71), 0),
        "cell_power": jnp.clip(jnp.exp(math.log(10.0) - 2.3025851 * jax.random.uniform(keys[3], (CELLS,), jnp.float32) ** shard_levels(keys[3], (CELLS,), ((0, 32),), -0.2, 0.2)), 1.0, 10.0),
        "spill_weight": jnp.clip(0.05 + 0.45 * jax.random.uniform(keys[4], (CELLS,), jnp.float32) ** shard_levels(keys[4], (CELLS,), ((0, 32),), -0.2, 0.2), 0.05, 0.5),
        "conductivity": jnp.clip(jnp.exp(math.log(2.0) - 1.3862944 * jax.random.uniform(keys[5], (LAYERS, NC, NR), jnp.float32) ** shard_levels(keys[5], (LAYERS, NC, NR), ((1, 16), (2, 2)), -0.2, 0.2)), 0.5, 2.0),
        "layer_coupling": jnp.clip(jnp.exp(jax.random.uniform(keys[6], (LAYERS - 1,), jnp.float32, math.log(0.5), math.log(2.0))), 0.5, 2.0),
    }


SINK_RATE = 0.5
LOW_BOUND = 0.5
HIGH_BOUND = 33.0


def operator_core(padded_values, padded_conduct, coupling):
    vertical_count = padded_values.shape[1] - 2
    horizontal_count = padded_values.shape[2] - 2
    centre_values = padded_values[:, 1:1 + vertical_count, 1:1 + horizontal_count]
    centre_conduct = padded_conduct[:, 1:1 + vertical_count, 1:1 + horizontal_count]
    result = SINK_RATE * centre_values
    for column_start, row_start in ((2, 1), (0, 1), (1, 2), (1, 0)):
        beside_values = padded_values[:, column_start:column_start + vertical_count, row_start:row_start + horizontal_count]
        beside_conduct = padded_conduct[:, column_start:column_start + vertical_count, row_start:row_start + horizontal_count]
        result = result + 0.5 * (centre_conduct + beside_conduct) * (centre_values - beside_values)
    face_conduct = coupling[:, None, None] * (0.5 * (centre_conduct[:-1] + centre_conduct[1:]))
    vertical_flow = face_conduct * (centre_values[:-1] - centre_values[1:])
    zero_layer = jnp.zeros_like(vertical_flow[:1])
    return result + jnp.concatenate([vertical_flow, zero_layer], 0) - jnp.concatenate([zero_layer, vertical_flow], 0)


def reference(cell_bin, cell_layer, cell_offset, cell_power, spill_weight, conductivity, layer_coupling):
    holder = jnp.arange(CELLS, dtype=jnp.int32) // C_DEV
    tile_column = holder // N_GY + cell_offset // 3 - 1
    tile_row = holder % N_GY + cell_offset % 3 - 1
    grid_column = tile_column * TC + cell_bin // TR
    grid_row = tile_row * TR + cell_bin % TR
    spill_layer = jnp.where(cell_layer == LAYERS - 1, LAYERS - 2, cell_layer + 1)
    plane_cells = NC * NR
    plane_index = grid_column * NR + grid_row
    main_index = cell_layer * plane_cells + plane_index
    spill_index = spill_layer * plane_cells + plane_index
    main_power = cell_power * (1.0 - spill_weight)
    spill_power = cell_power * spill_weight
    flat_power = jnp.zeros((LAYERS * plane_cells,), jnp.float32)
    flat_power = flat_power.at[main_index].add(main_power).at[spill_index].add(spill_power)
    dissipation_map = flat_power.reshape(LAYERS, NC, NR)
    padded_conduct = jnp.pad(conductivity, ((0, 0), (1, 1), (1, 1)))

    def diffusion_matrix_product(values):
        return operator_core(jnp.pad(values, ((0, 0), (1, 1), (1, 1))), padded_conduct, layer_coupling)

    middle_window = 0.5 * (HIGH_BOUND + LOW_BOUND)
    spread = 0.5 * (HIGH_BOUND - LOW_BOUND)
    sigma_value = middle_window / spread
    ratio_now = 1.0 / sigma_value
    final_warmth = dissipation_map / middle_window
    iterate_advance = dissipation_map / middle_window
    for sweep_index in range(ITERS):
        leftover_error_map = dissipation_map - diffusion_matrix_product(final_warmth)
        ratio_next = 1.0 / (2.0 * sigma_value - ratio_now)
        iterate_advance = (ratio_next * ratio_now) * iterate_advance + (2.0 * ratio_next / spread) * leftover_error_map
        final_warmth = final_warmth + iterate_advance
        ratio_now = ratio_next
    bordered_warmth = jnp.pad(final_warmth, ((0, 0), (1, 1), (1, 1)))
    vertical_slope = 0.5 * (bordered_warmth[:, 2:, 1:-1] - bordered_warmth[:, :-2, 1:-1])
    horizontal_slope = 0.5 * (bordered_warmth[:, 1:-1, 2:] - bordered_warmth[:, 1:-1, :-2])
    vertical_pull_share = -cell_power * vertical_slope.reshape(-1)[main_index]
    horizontal_pull_share = -cell_power * horizontal_slope.reshape(-1)[main_index]
    return final_warmth, jnp.stack([vertical_pull_share, horizontal_pull_share])
```

```python
import functools

import jax
import jax.numpy as jnp
from jax import lax
from jax.experimental import pallas as pl
from jax.experimental.pallas import tpu as pltpu
from jax.sharding import PartitionSpec as P

ITERS = 4
CAP = 2048
SINK_RATE = 0.5
LOW_BOUND = 0.5
HIGH_BOUND = 33.0

WIDE = 256
GROUP = CAP // WIDE
HALO = 8
F32, BF16 = jnp.float32, jnp.bfloat16


def partner(place, kind, count):
    if kind == 0:
        return place
    if kind == 1:
        return place ^ 1
    return (place - 1 if place % 2 == 0 else place + 1) % count


def exchange(value, x_kind, y_kind):
    nx, ny = lax.axis_size("gx"), lax.axis_size("gy")
    pairs = [
        (a * ny + b, partner(a, x_kind, nx) * ny + partner(b, y_kind, ny))
        for a in range(nx)
        for b in range(ny)
    ]
    return lax.ppermute(value, ("gx", "gy"), pairs)


def pieces(value):
    high = value.astype(BF16).astype(F32)
    return high, value - high


def row_iota(count, width=128):
    return lax.broadcasted_iota(jnp.int32, (count, width), 0).astype(F32)


def onehot(row, count):
    return jnp.where(row_iota(count, row.shape[1]) == row, 1.0, 0.0).astype(BF16)


def lanes(parts):
    return jnp.concatenate(parts, axis=1) if len(parts) > 1 else parts[0]


def transposed_dot(left, right):
    return lax.dot_general(left, right, (((1,), (1,)), ((), ())), preferred_element_type=F32)


def dot(left, right):
    return lax.dot_general(left, right, (((1,), (0,)), ((), ())), preferred_element_type=F32)


def kind_of(step, place):
    ahead = 1 - 2 * lax.rem(place, 2)
    return jnp.where(step == 0, 0, jnp.where(step == ahead, 1, 2))


def pack_kernel(
    nyc, cols, rows,
    bin_ref, layer_ref, off_ref, power_ref, spill_ref, cond_ref,
    msga_ref, msgb_ref, owny_ref, slot_ref,
    q_ref, lam_ref, field_ref, acc_ref,
):
    a, b = lax.axis_index("gx"), lax.axis_index("gy")
    groups = 3 * nyc - 1
    table = groups * GROUP
    off = off_ref[...]
    col_code = (off >= 3).astype(jnp.int32) + (off >= 6).astype(jnp.int32)
    x_kind = kind_of(col_code - 1, a)
    y_kind = kind_of(off - 3 * col_code - 1, b)
    group = jnp.where(x_kind > 0, (x_kind - 1) * nyc + y_kind, 2 * nyc - 1 + y_kind)
    group = jnp.where(off == 4, -1, group)
    size = off.shape[0]
    r_i = lax.broadcasted_iota(jnp.int32, (size, size), 0)
    c_i = lax.broadcasted_iota(jnp.int32, (size, size), 1)
    upper = jnp.where(r_i < c_i, 1.0, 0.0).astype(BF16)
    lower = jnp.where(r_i > c_i, 1.0, 0.0).astype(BF16)
    ones = jnp.ones((size, size), BF16)
    slot = jnp.full(off.shape, -1.0, F32)
    for g in range(groups):
        mine = group == g
        mask = jnp.where(mine, 1.0, 0.0).astype(BF16)
        totals = dot(mask, ones).astype(BF16)
        rank = dot(mask, upper) + dot(lower, totals)
        slot = jnp.where(mine, rank + float(g * CAP), slot)
    slot_ref[...] = slot
    q = jnp.floor(slot * (1.0 / WIDE))
    q_ref[...] = q
    lam_ref[...] = slot - q * WIDE
    code = layer_ref[...] * (cols * rows) + bin_ref[...]
    field_ref[0] = (code // rows).astype(F32)
    field_ref[1] = (code % rows).astype(F32)
    power = power_ref[...]
    spill = spill_ref[...]
    field_ref[2], field_ref[3] = pieces(power * (1.0 - spill))
    field_ref[4], field_ref[5] = pieces(power * spill)
    acc_ref[...] = jnp.zeros_like(acc_ref)
    step = 8

    def body(j, carry):
        base = pl.multiple_of(j * step, step)
        q8 = q_ref[pl.ds(base, step), :]
        lam8 = lam_ref[pl.ds(base, step), :]
        vals = [field_ref[f, pl.ds(base, step), :] for f in range(6)]
        picks, marks = [], []
        for i in range(step):
            hit = row_iota(table) == q8[i : i + 1]
            picks.append(
                jnp.concatenate([jnp.where(hit, v[i : i + 1], 0.0) for v in vals], axis=0)
            )
            marks.append(onehot(lam8[i : i + 1], WIDE))
        acc_ref[...] += transposed_dot(lanes(picks).astype(BF16), lanes(marks))
        return carry

    lax.fori_loop(0, size // step, body, 0)
    out = [acc_ref[f * table : (f + 1) * table, :] for f in range(6)]
    sent = [out[0] * float(rows) + out[1], out[2] + out[3], out[4] + out[5]]

    def put(ref, at, g):
        for f in range(3):
            ref[(at * 3 + f) * GROUP : (at * 3 + f + 1) * GROUP, :] = sent[f][
                g * GROUP : (g + 1) * GROUP
            ]

    for y in range(nyc):
        put(msga_ref, y, y)
        put(msgb_ref, y, nyc + y)
        if y:
            put(owny_ref, y - 1, 2 * nyc + y - 1)
    first, last = cond_ref[:, :HALO, :], cond_ref[:, cols - HALO :, :]
    even = lax.rem(a, 2) == 0
    top = nyc * 3 * GROUP
    flat = (-1, cond_ref.shape[2])
    msga_ref[top:, :] = jnp.where(even, last, first).reshape(flat)
    msgb_ref[top:, :] = jnp.where(even, first, last).reshape(flat)


def deposit_block(lc, r, main, spill, cols, cells):
    count = cells
    picks, marks = [], []
    for lc_i, r_i, (mh, ml), (sh, sl) in zip(lc, r, main, spill):
        spot = row_iota(count, lc_i.shape[1])
        other = jnp.where(lc_i >= float(count - cols), lc_i - cols, lc_i + cols)
        here, there = spot == lc_i, spot == other
        high = jnp.where(here, mh, jnp.where(there, sh, 0.0))
        low = jnp.where(here, ml, jnp.where(there, sl, 0.0))
        picks.append(jnp.concatenate([high.astype(BF16), low.astype(BF16)], axis=0))
        marks.append(onehot(r_i, WIDE))
    return transposed_dot(lanes(picks), lanes(marks))


def stay_deposit_kernel(
    cols, bin_ref, layer_ref, off_ref, power_ref, spill_ref, grid_ref, lc_ref, r_ref, val_ref
):
    count, rows = grid_ref.shape[0] // 2, grid_ref.shape[1]
    code = layer_ref[...] * (cols * rows) + bin_ref[...]
    lc_ref[...] = (code // rows).astype(F32)
    r_ref[...] = (code % rows).astype(F32)
    power = jnp.where(off_ref[...] == 4, power_ref[...], 0.0)
    spill = spill_ref[...]
    val_ref[0], val_ref[1] = pieces(power * (1.0 - spill))
    val_ref[2], val_ref[3] = pieces(power * spill)
    grid_ref[...] = jnp.zeros_like(grid_ref)
    step = 8

    def body(j, carry):
        base = pl.multiple_of(j * step, step)
        lc8, r8 = lc_ref[pl.ds(base, step), :], r_ref[pl.ds(base, step), :]
        v = [val_ref[f, pl.ds(base, step), :] for f in range(4)]
        rows_of = lambda x: [x[i : i + 1] for i in range(step)]
        parts = [rows_of(x) for x in v]
        grid_ref[...] += deposit_block(
            rows_of(lc8), rows_of(r8), list(zip(parts[0], parts[1])),
            list(zip(parts[2], parts[3])), cols, count,
        )
        return carry

    lax.fori_loop(0, lc_ref.shape[0] // step, body, 0)


def deposit_groups(grid_ref, sources, cols):
    count, rows = grid_ref.shape[0] // 2, grid_ref.shape[1]
    step = 4
    for ref, at in sources:
        for half in range(GROUP // step):
            lc, r, main, spill = [], [], [], []
            for i in range(step):
                row = at + half * step + i
                code = ref[row : row + 1, :]
                lc_i = jnp.floor(code * (1.0 / rows))
                lc.append(lc_i)
                r.append(code - lc_i * rows)
                main.append(pieces(ref[row + GROUP : row + GROUP + 1, :]))
                spill.append(pieces(ref[row + 2 * GROUP : row + 2 * GROUP + 1, :]))
            grid_ref[...] += deposit_block(lc, r, main, spill, cols, count)


def near_deposit_kernel(cols, stay_ref, recva_ref, recvb_ref, grid_ref):
    grid_ref[...] = stay_ref[...]
    deposit_groups(grid_ref, [(recva_ref, 0), (recvb_ref, 0)], cols)


def far_deposit_kernel(cols, nyc, *refs):
    near_ref, recvy = refs[0], refs[1:nyc]
    grid_ref, edgea_ref, edgeb_ref, acc_ref = refs[nyc:]
    acc_ref[...] = near_ref[...]
    sources = [(ref, 3 * GROUP * i) for ref in recvy for i in range(3)]
    deposit_groups(acc_ref, sources, cols)
    count = acc_ref.shape[0] // 2
    grid = (acc_ref[:count, :] + acc_ref[count:, :]).reshape(grid_ref.shape)
    grid_ref[...] = grid
    first, last = grid[:, :HALO, :], grid[:, cols - HALO :, :]
    even = lax.rem(lax.axis_index("gx"), 2) == 0
    edgea_ref[...] = jnp.where(even, last, first)
    edgeb_ref[...] = jnp.where(even, first, last)


def with_columns(own, from_a, from_b):
    a = lax.axis_index("gx")
    even = lax.rem(a, 2) == 0
    right = jnp.where(even, from_a, from_b)
    left = jnp.where(even, from_b, from_a)
    right = jnp.where(a < lax.axis_size("gx") - 1, right, 0.0)
    left = jnp.where(a > 0, left, 0.0)
    return jnp.concatenate([left, own, right], axis=1)


def row_edge(wide, last):
    rows = wide.shape[1]
    tile = jnp.where(last, wide[:, rows - 128 :], wide[:, :128]).T
    return jnp.where(last, tile[128 - HALO :], tile[:HALO])


def put_edges(ref, at, edge):
    extra = edge.shape[1] - WIDE
    ref[at : at + HALO, :] = edge[:, :WIDE]
    ref[at + HALO : at + 2 * HALO, :] = jnp.concatenate(
        [edge[:, WIDE:], jnp.zeros((HALO, WIDE - extra), F32)], axis=1
    )


def get_edges(ref, at, count):
    return jnp.concatenate(
        [ref[at : at + HALO, :], ref[at + HALO : at + 2 * HALO, : count - WIDE]], axis=1
    )


def y_edges(refs, at, wide):
    even = lax.rem(lax.axis_index("gy"), 2) == 0
    for kind, ref in enumerate(refs):
        put_edges(ref, at, row_edge(wide, even if kind == 0 else jnp.logical_not(even)))


def halo_of(ref, cols, layers, top):
    return ref[top:, :].reshape(layers, HALO, ref.shape[1])


def forward_kernel(nyc, recva_ref, recvb_ref, owny_ref, cond_ref, *msgy_refs):
    layers, cols, rows = cond_ref.shape
    size, top = 3 * GROUP, nyc * 3 * GROUP
    for y, ref in enumerate(msgy_refs):
        ref[:size, :] = owny_ref[y * size : (y + 1) * size, :]
        ref[size : 2 * size, :] = recva_ref[(y + 1) * size : (y + 2) * size, :]
        ref[2 * size : 3 * size, :] = recvb_ref[(y + 1) * size : (y + 2) * size, :]
    wide = with_columns(
        cond_ref[...], halo_of(recva_ref, cols, layers, top), halo_of(recvb_ref, cols, layers, top)
    )
    y_edges(msgy_refs, 3 * size, wide.reshape(-1, rows))


def power_edge_kernel(grid_ref, froma_ref, fromb_ref, *edge_refs):
    wide = with_columns(grid_ref[...], froma_ref[...], fromb_ref[...])
    y_edges(edge_refs, 0, wide.reshape(-1, grid_ref.shape[2]))


def with_rows(wide, edges):
    b, ny = lax.axis_index("gy"), lax.axis_size("gy")
    layers, span, rows = wide.shape
    count = layers * span
    even = lax.rem(b, 2) == 0
    one = edges[0]
    two = edges[1] if len(edges) > 1 else jnp.zeros_like(one)
    after = jnp.where(b < ny - 1, jnp.where(even, one, two), 0.0)
    before = jnp.where(b > 0, jnp.where(even, two, one), 0.0)
    tile = jnp.concatenate([after, jnp.zeros((128 - 2 * HALO, count), F32), before], axis=0).T
    return jnp.concatenate([wide, tile.reshape(layers, span, 128)], axis=2)


def solve_kernel(nyc, *refs):
    grid_ref, froma_ref, fromb_ref, cond_ref, recva_ref, recvb_ref, coupling_ref = refs[:7]
    edge_refs, recvy_refs = refs[7 : 6 + nyc], refs[6 + nyc : 5 + 2 * nyc]
    warmth_ref, slope_ref, k_ref, p_ref, v_ref, u_ref, fc_ref, fr_ref, fl_ref, e_ref = refs[
        5 + 2 * nyc :
    ]
    layers, cols, rows = cond_ref.shape
    span, wide_rows = cols + 2 * HALO, rows + 128
    count = layers * span
    top = nyc * 3 * GROUP
    a, b = lax.axis_index("gx"), lax.axis_index("gy")
    nx, ny = lax.axis_size("gx"), lax.axis_size("gy")
    k_ref[...] = with_rows(
        with_columns(
            cond_ref[...],
            halo_of(recva_ref, cols, layers, top),
            halo_of(recvb_ref, cols, layers, top),
        ),
        [get_edges(ref, 9 * GROUP, count) for ref in recvy_refs],
    )
    p_ref[...] = with_rows(
        with_columns(grid_ref[...], froma_ref[...], fromb_ref[...]),
        [get_edges(ref, 0, count) for ref in edge_refs],
    )
    shape = (span, wide_rows)
    c_i = lax.broadcasted_iota(jnp.int32, shape, 0)
    r_i = lax.broadcasted_iota(jnp.int32, shape, 1)
    c_low = jnp.where(a > 0, 0, HALO)
    c_high = jnp.where(a < nx - 1, span, span - HALO)
    r_high = jnp.where(b < ny - 1, rows + HALO, rows)
    r_low = jnp.where(b > 0, wide_rows - HALO, wide_rows)
    inside = jnp.where((c_i >= c_low) & (c_i < c_high) & ((r_i < r_high) | (r_i >= r_low)), 1.0, 0.0)
    next_c = lambda x: pltpu.roll(x, span - 1, 0)
    prev_c = lambda x: pltpu.roll(x, 1, 0)
    next_r = lambda x: pltpu.roll(x, wide_rows - 1, 1)
    prev_r = lambda x: pltpu.roll(x, 1, 1)
    both_c, both_r = inside * next_c(inside), inside * next_r(inside)
    for l in range(layers):
        k = k_ref[l]
        face_c, face_r = 0.5 * (k + next_c(k)), 0.5 * (k + next_r(k))
        kept_c, kept_r = face_c * both_c, face_r * both_r
        fc_ref[l], fr_ref[l] = kept_c, kept_r
        lost_c, lost_r = face_c - kept_c, face_r - kept_r
        e_ref[l] = SINK_RATE + ((lost_c + prev_c(lost_c)) + (lost_r + prev_r(lost_r)))
        if l + 1 < layers:
            fl_ref[l] = coupling_ref[l] * (0.5 * (k + k_ref[l + 1])) * inside
    middle = 0.5 * (HIGH_BOUND + LOW_BOUND)
    spread = 0.5 * (HIGH_BOUND - LOW_BOUND)
    sigma = middle / spread
    now = 1.0 / sigma
    for l in range(layers):
        start = p_ref[l] / middle
        v_ref[0, l] = start
        u_ref[l] = start
    for sweep in range(ITERS):
        later = 1.0 / (2.0 * sigma - now)
        keep, gain = later * now, 2.0 * later / spread
        old, new = sweep % 2, (sweep + 1) % 2
        below = None
        for l in range(layers):
            v = v_ref[old, l]
            flow_c = fc_ref[l] * (v - next_c(v))
            flow_r = fr_ref[l] * (v - next_r(v))
            result = e_ref[l] * v + (flow_c - prev_c(flow_c)) + (flow_r - prev_r(flow_r))
            if below is not None:
                result = result - below
            if l + 1 < layers:
                below = fl_ref[l] * (v - v_ref[old, l + 1])
                result = result + below
            advance = keep * u_ref[l] + gain * (p_ref[l] - result)
            u_ref[l] = advance
            v_ref[new, l] = v + advance
        now = later
    final = ITERS % 2
    cells = layers * cols
    for l in range(layers):
        v = v_ref[final, l]
        warmth_ref[l] = v[HALO : HALO + cols, :rows]
        for f, slope in enumerate((0.5 * (next_c(v) - prev_c(v)), 0.5 * (next_r(v) - prev_r(v)))):
            high, low = pieces(slope[HALO : HALO + cols, :rows])
            at = f * cells + l * cols
            slope_ref[at : at + cols, :rows] = high.astype(BF16)
            slope_ref[at : at + cols, rows:] = low.astype(BF16)


def gather_block(slope, lc, r):
    cells = slope.shape[0] // 2
    mark = onehot(r, slope.shape[1] // 2)
    found = dot(slope, jnp.concatenate([mark, mark], axis=0))
    here = row_iota(cells, lc.shape[1]) == lc
    return [
        jnp.sum(jnp.where(here, found[f * cells : (f + 1) * cells], 0.0), axis=0, keepdims=True)
        for f in range(2)
    ]


def gather_kernel(sources, slope_ref, *refs):
    ins, out_ref = refs[:-1], refs[-1]
    rows = slope_ref.shape[1] // 2
    for g, (which, at) in enumerate(sources):
        for t in range(GROUP):
            code = ins[which][at + t : at + t + 1, :]
            lc = jnp.floor(code * (1.0 / rows))
            for f, value in enumerate(gather_block(slope_ref[...], lc, code - lc * rows)):
                row = (g * 2 + f) * GROUP + t
                out_ref[row : row + 1, :] = value


def stay_gather_kernel(cols, slope_ref, bin_ref, layer_ref, out_ref, lc_ref, r_ref):
    rows = slope_ref.shape[1] // 2
    code = layer_ref[...] * (cols * rows) + bin_ref[...]
    lc_ref[...] = (code // rows).astype(F32)
    r_ref[...] = (code % rows).astype(F32)
    step = 8

    def body(j, carry):
        base = pl.multiple_of(j * step, step)
        lc8, r8 = lc_ref[pl.ds(base, step), :], r_ref[pl.ds(base, step), :]
        for i in range(0, step, 2):
            two = lambda x: jnp.concatenate([x[i : i + 1], x[i + 1 : i + 2]], axis=1)
            at = pl.multiple_of(base * 128 + i * 128, 256)
            for f, value in enumerate(gather_block(slope_ref[...], two(lc8), two(r8))):
                out_ref[f : f + 1, pl.ds(at, 256)] = value
        return carry

    lax.fori_loop(0, lc_ref.shape[0] // step, body, 0)


def reply_kernel(nyc, near_ref, *refs):
    size = 2 * GROUP
    backs, (a_ref, b_ref) = refs[: nyc - 1], refs[nyc - 1 :]
    a_ref[:size, :] = near_ref[:size, :]
    b_ref[:size, :] = near_ref[size:, :]
    for y, ref in enumerate(backs):
        a_ref[(y + 1) * size : (y + 2) * size, :] = ref[size : 2 * size, :]
        b_ref[(y + 1) * size : (y + 2) * size, :] = ref[2 * size : 3 * size, :]


def unpack_kernel(nyc, backa_ref, backb_ref, *refs):
    backy, (stay_ref, slot_ref, power_ref, out_ref, q_ref, lam_ref, table_ref) = (
        refs[: nyc - 1], refs[nyc - 1 :],
    )
    groups = [(backa_ref, y) for y in range(nyc)] + [(backb_ref, y) for y in range(nyc)]
    groups += [(ref, 0) for ref in backy]
    table = len(groups) * GROUP
    for f in range(2):
        whole = jnp.concatenate(
            [ref[(2 * at + f) * GROUP : (2 * at + f + 1) * GROUP, :] for ref, at in groups], axis=0
        )
        high, low = pieces(whole)
        table_ref[f * table : (f + 1) * table, :WIDE] = high
        table_ref[f * table : (f + 1) * table, WIDE:] = low
    slot = slot_ref[...]
    q = jnp.floor(slot * (1.0 / WIDE))
    q_ref[...] = q
    lam_ref[...] = slot - q * WIDE
    source = table_ref[...].astype(BF16)
    step = 8

    def body(j, carry):
        base = pl.multiple_of(j * step, step)
        q8, lam8 = q_ref[pl.ds(base, step), :], lam_ref[pl.ds(base, step), :]
        power8 = power_ref[pl.ds(base, step), :]
        for i in range(0, step, 2):
            two = lambda x: jnp.concatenate([x[i : i + 1], x[i + 1 : i + 2]], axis=1)
            at = pl.multiple_of(base * 128 + i * 128, 256)
            mark = onehot(two(lam8), WIDE)
            found = dot(source, jnp.concatenate([mark, mark], axis=0))
            place = two(q8)
            here = row_iota(table, 256) == place
            for f in range(2):
                value = jnp.sum(
                    jnp.where(here, found[f * table : (f + 1) * table], 0.0), axis=0, keepdims=True
                )
                value = jnp.where(place >= 0.0, value, stay_ref[f : f + 1, pl.ds(at, 256)])
                out_ref[f : f + 1, pl.ds(at, 256)] = -two(power8) * value
        return carry

    lax.fori_loop(0, q_ref.shape[0] // step, body, 0)


def call(kernel, outs, scratch, *args, scalars=()):
    space = pl.BlockSpec(memory_space=pltpu.VMEM)
    specs = [
        pl.BlockSpec(memory_space=pltpu.SMEM) if i in scalars else space for i in range(len(args))
    ]
    shapes = [jax.ShapeDtypeStruct(shape, dtype) for shape, dtype in outs]
    return pl.pallas_call(
        kernel,
        out_shape=shapes,
        in_specs=specs,
        out_specs=[space] * len(shapes),
        scratch_shapes=scratch,
        compiler_params=pltpu.CompilerParams(vmem_limit_bytes=48 * 1024 * 1024),
    )(*args)


def shards(
    cell_bin, cell_layer, cell_offset, cell_power, spill_weight, conductivity, layer_coupling
):
    layers, cols, rows = conductivity.shape
    cells = cell_bin.shape[0]
    nyc = 2 if lax.axis_size("gy") == 2 else 3
    count = layers * cols
    groups = 3 * nyc - 1
    flat = lambda x: x.reshape(cells // 128, 128)
    bins, layer, off = flat(cell_bin), flat(cell_layer), flat(cell_offset)
    power, spill = flat(cell_power), flat(spill_weight)
    square = bins.shape
    own = 3 * GROUP
    message = (nyc * own + layers * HALO, WIDE)
    vmem = lambda *shape: pltpu.VMEM(shape, F32)
    partial = functools.partial

    msg_a, msg_b, own_y, slot = call(
        partial(pack_kernel, nyc, cols, rows),
        [(message, F32), (message, F32), (((nyc - 1) * own, WIDE), F32), (square, F32)],
        [vmem(*square), vmem(*square), vmem(6, *square), vmem(6 * groups * GROUP, WIDE)],
        bins, layer, off, power, spill, conductivity,
    )
    recv_a, recv_b = exchange(msg_a, 1, 0), exchange(msg_b, 2, 0)
    (stay_grid,) = call(
        partial(stay_deposit_kernel, cols),
        [((2 * count, rows), F32)],
        [vmem(*square), vmem(*square), vmem(4, *square)],
        bins, layer, off, power, spill,
    )
    msg_y = call(
        partial(forward_kernel, nyc),
        [((3 * own + 2 * HALO, WIDE), F32)] * (nyc - 1),
        [],
        recv_a, recv_b, own_y, conductivity,
    )
    recv_y = [exchange(m, 0, i + 1) for i, m in enumerate(msg_y)]
    (near_grid,) = call(
        partial(near_deposit_kernel, cols),
        [((2 * count, rows), F32)],
        [],
        stay_grid, recv_a, recv_b,
    )
    edge = (layers, HALO, rows)
    grid, edge_a, edge_b = call(
        partial(far_deposit_kernel, cols, nyc),
        [(conductivity.shape, F32), (edge, F32), (edge, F32)],
        [vmem(2 * count, rows)],
        near_grid, *recv_y,
    )
    from_a, from_b = exchange(edge_a, 1, 0), exchange(edge_b, 2, 0)
    edges = call(
        power_edge_kernel, [((2 * HALO, WIDE), F32)] * (nyc - 1), [], grid, from_a, from_b
    )
    from_y = [exchange(e, 0, i + 1) for i, e in enumerate(edges)]
    big = (layers, cols + 2 * HALO, rows + 128)
    final_warmth, slope = call(
        partial(solve_kernel, nyc),
        [(conductivity.shape, F32), ((2 * count, 2 * rows), BF16)],
        [vmem(*big), vmem(*big), vmem(2, *big)] + [vmem(*big)] * 5,
        grid, from_a, from_b, conductivity, recv_a, recv_b, layer_coupling, *from_y, *recv_y,
        scalars=(6,),
    )
    answer_y = [
        call(
            partial(gather_kernel, [(0, own * i) for i in range(3)]),
            [((6 * GROUP, WIDE), F32)],
            [],
            slope, r,
        )[0]
        for r in recv_y
    ]
    back_y = [exchange(m, 0, i + 1) for i, m in enumerate(answer_y)]
    (near_answer,) = call(
        partial(gather_kernel, [(0, 0), (1, 0)]),
        [((4 * GROUP, WIDE), F32)],
        [],
        slope, recv_a, recv_b,
    )
    answer_a, answer_b = call(
        partial(reply_kernel, nyc),
        [((2 * nyc * GROUP, WIDE), F32)] * 2,
        [],
        near_answer, *back_y,
    )
    back_a, back_b = exchange(answer_a, 1, 0), exchange(answer_b, 2, 0)
    (stay_value,) = call(
        partial(stay_gather_kernel, cols),
        [((2, cells), F32)],
        [vmem(*square), vmem(*square)],
        slope, bins, layer,
    )
    (pull,) = call(
        partial(unpack_kernel, nyc),
        [((2, cells), F32)],
        [vmem(*square), vmem(*square), vmem(2 * groups * GROUP, 2 * WIDE)],
        back_a, back_b, *back_y, stay_value, slot, power,
    )
    return final_warmth, pull


def solution(mesh):
    cell = P(("gx", "gy"))
    tile = P(None, "gx", "gy")
    return jax.shard_map(
        shards,
        mesh=mesh,
        in_specs=(cell, cell, cell, cell, cell, tile, P()),
        out_specs=(tile, P(None, ("gx", "gy"))),
        check_vma=False,
    )
```

```python
import functools

import jax
import jax.numpy as jnp
from jax import lax
from jax.experimental import pallas as pl
from jax.experimental.pallas import tpu as pltpu
from jax.sharding import PartitionSpec as P

ITERS = 4
CAP = 2048
SINK_RATE = 0.5
LOW_BOUND = 0.5
HIGH_BOUND = 33.0

WIDE = 256
GROUP = CAP // WIDE
HALO = 8
F32, BF16 = jnp.float32, jnp.bfloat16


def partner(place, kind, count):
    if kind == 0:
        return place
    if kind == 1:
        return place ^ 1
    return (place - 1 if place % 2 == 0 else place + 1) % count


def exchange(value, x_kind, y_kind):
    nx, ny = lax.axis_size("gx"), lax.axis_size("gy")
    pairs = [
        (a * ny + b, partner(a, x_kind, nx) * ny + partner(b, y_kind, ny))
        for a in range(nx)
        for b in range(ny)
    ]
    return lax.ppermute(value, ("gx", "gy"), pairs)


def pieces(value):
    high = value.astype(BF16).astype(F32)
    return high, value - high


def row_iota(count, width=128):
    return lax.broadcasted_iota(jnp.int32, (count, width), 0).astype(F32)


def onehot(row, count):
    return jnp.where(
        row_iota(count, row.shape[1]).astype(BF16) == row.astype(BF16),
        jnp.ones((), BF16),
        jnp.zeros((), BF16),
    )


def lanes(parts):
    return jnp.concatenate(parts, axis=1) if len(parts) > 1 else parts[0]


def transposed_dot(left, right):
    return lax.dot_general(left, right, (((1,), (1,)), ((), ())), preferred_element_type=F32)


def dot(left, right):
    return lax.dot_general(left, right, (((1,), (0,)), ((), ())), preferred_element_type=F32)


def kind_of(step, place):
    ahead = 1 - 2 * lax.rem(place, 2)
    return jnp.where(step == 0, 0, jnp.where(step == ahead, 1, 2))


def pack_kernel(
    nyc, cols, rows,
    bin_hbm, layer_hbm, off_hbm, power_hbm, spill_hbm, cond_hbm,
    msga_ref, msgb_ref, owny_ref, slot_ref, field_ref, power_ref,
    bin_ref, layer_ref, off_ref, spill_ref, edge_ref, sems, acc_ref,
):
    a, b = lax.axis_index("gx"), lax.axis_index("gy")
    copies = [
        pltpu.make_async_copy(src, dst, sems.at[i])
        for i, (src, dst) in enumerate(
            [
                (off_hbm, off_ref), (bin_hbm, bin_ref), (layer_hbm, layer_ref),
                (power_hbm, power_ref), (spill_hbm, spill_ref),
                (cond_hbm.at[:, :HALO, :], edge_ref.at[0]),
                (cond_hbm.at[:, cols - HALO :, :], edge_ref.at[1]),
            ]
        )
    ]
    for copy in copies:
        copy.start()
    acc_ref[...] = jnp.zeros_like(acc_ref)
    groups = 3 * nyc - 1
    table = groups * GROUP
    copies[0].wait()
    off = off_ref[...]
    col_code = (off >= 3).astype(jnp.int32) + (off >= 6).astype(jnp.int32)
    x_kind = kind_of(col_code - 1, a)
    y_kind = kind_of(off - 3 * col_code - 1, b)
    group = jnp.where(x_kind > 0, (x_kind - 1) * nyc + y_kind, 2 * nyc - 1 + y_kind)
    group = jnp.where(off == 4, -1, group)
    size = off.shape[0]
    r_i = lax.broadcasted_iota(jnp.int32, (size, size), 0)
    c_i = lax.broadcasted_iota(jnp.int32, (size, size), 1)
    upper = jnp.where(r_i < c_i, 1.0, 0.0).astype(BF16)
    lower = jnp.where(r_i > c_i, 1.0, 0.0).astype(BF16)
    ones = jnp.ones((size, size), BF16)
    slot = jnp.full(off.shape, -1.0, F32)
    for g in range(groups):
        mine = group == g
        mask = jnp.where(mine, 1.0, 0.0).astype(BF16)
        totals = dot(mask, ones).astype(BF16)
        rank = dot(mask, upper) + dot(lower, totals)
        slot = jnp.where(mine, rank + float(g * CAP), slot)
    slot_ref[...] = slot
    for copy in copies[1:]:
        copy.wait()
    code = layer_ref[...] * (cols * rows) + bin_ref[...]
    field_ref[0] = (code // rows).astype(F32)
    field_ref[1] = (code % rows).astype(F32)
    power = power_ref[...]
    spill = spill_ref[...]
    field_ref[2], field_ref[3] = pieces(power * (1.0 - spill))
    field_ref[4], field_ref[5] = pieces(power * spill)
    step = 32

    def body(j, carry):
        base = pl.multiple_of(j * step, step)
        slots = slot_ref[pl.ds(base, step), :]
        qs = jnp.floor(slots * (1.0 / WIDE))
        lams = slots - qs * WIDE
        vals = [field_ref[f, pl.ds(base, step), :] for f in range(6)]
        picks, marks = [], []
        for i in range(step):
            hit = row_iota(table) == qs[i : i + 1]
            picks.append(
                jnp.concatenate([jnp.where(hit, v[i : i + 1], 0.0) for v in vals], axis=0).astype(BF16)
            )
            marks.append(onehot(lams[i : i + 1], WIDE))
        acc_ref[...] += transposed_dot(lanes(picks), lanes(marks))
        return carry

    lax.fori_loop(0, size // step, body, 0)
    out = [acc_ref[f * table : (f + 1) * table, :] for f in range(6)]
    sent = [out[0] * float(rows) + out[1], out[2] + out[3], out[4] + out[5]]

    def put(ref, at, g):
        for f in range(3):
            ref[(at * 3 + f) * GROUP : (at * 3 + f + 1) * GROUP, :] = sent[f][
                g * GROUP : (g + 1) * GROUP
            ]

    for y in range(nyc):
        put(msga_ref, y, y)
        put(msgb_ref, y, nyc + y)
        if y:
            put(owny_ref, y - 1, 2 * nyc + y - 1)
    first, last = edge_ref[0], edge_ref[1]
    even = lax.rem(a, 2) == 0
    top = nyc * 3 * GROUP
    flat = (-1, rows)
    msga_ref[top:, :] = jnp.where(even, last, first).reshape(flat)
    msgb_ref[top:, :] = jnp.where(even, first, last).reshape(flat)


def deposit_block(lc, r, main, spill, cols, cells):
    picks, marks = [], []
    zero = jnp.zeros((), BF16)
    narrow = lambda x: x.astype(BF16)
    for lc_i, r_i, (mh, ml), (sh, sl) in zip(lc, r, main, spill):
        spot = narrow(row_iota(cells, lc_i.shape[1]))
        other = jnp.where(lc_i >= float(cells - cols), lc_i - cols, lc_i + cols)
        here, there = spot == narrow(lc_i), spot == narrow(other)
        high = jnp.where(here, narrow(mh), jnp.where(there, narrow(sh), zero))
        low = jnp.where(here, narrow(ml), jnp.where(there, narrow(sl), zero))
        picks.append(jnp.concatenate([high, low], axis=0))
        marks.append(onehot(r_i, WIDE))
    return transposed_dot(lanes(picks), lanes(marks))


def stay_deposit_kernel(cols, field_ref, slot_ref, grid_ref, val_ref):
    count = grid_ref.shape[0] // 2
    size = slot_ref.shape[0]
    stays = slot_ref[...] < 0.0
    for f in range(4):
        val_ref[f] = jnp.where(stays, field_ref[2 + f], 0.0)
    grid_ref[...] = jnp.zeros_like(grid_ref)
    step = 64

    def body(j, carry):
        base = pl.multiple_of(j * step, step)
        lcs, rs = field_ref[0, pl.ds(base, step), :], field_ref[1, pl.ds(base, step), :]
        rows_of = lambda x: [x[i : i + 1] for i in range(step)]
        parts = [rows_of(val_ref[f, pl.ds(base, step), :]) for f in range(4)]
        grid_ref[...] += deposit_block(
            rows_of(lcs), rows_of(rs), list(zip(parts[0], parts[1])),
            list(zip(parts[2], parts[3])), cols, count,
        )
        return carry

    lax.fori_loop(0, size // step, body, 0)


def deposit_groups(grid_ref, sources, cols):
    count, rows = grid_ref.shape[0] // 2, grid_ref.shape[1]
    lc, r, main, spill = [], [], [], []
    for ref, at in sources:
        for row in range(at, at + GROUP):
            code = ref[row : row + 1, :]
            lc_i = jnp.floor(code * (1.0 / rows))
            lc.append(lc_i)
            r.append(code - lc_i * rows)
            main.append(pieces(ref[row + GROUP : row + GROUP + 1, :]))
            spill.append(pieces(ref[row + 2 * GROUP : row + 2 * GROUP + 1, :]))
    grid_ref[...] += deposit_block(lc, r, main, spill, cols, count)


def near_deposit_kernel(cols, stay_ref, recva_ref, recvb_ref, grid_ref):
    grid_ref[...] = stay_ref[...]
    deposit_groups(grid_ref, [(recva_ref, 0), (recvb_ref, 0)], cols)


def far_deposit_kernel(cols, nyc, *refs):
    near_ref, recvy = refs[0], refs[1:nyc]
    grid_ref, edgea_ref, edgeb_ref, acc_ref = refs[nyc:]
    acc_ref[...] = near_ref[...]
    sources = [(ref, 3 * GROUP * i) for ref in recvy for i in range(3)]
    deposit_groups(acc_ref, sources, cols)
    count = acc_ref.shape[0] // 2
    grid = (acc_ref[:count, :] + acc_ref[count:, :]).reshape(grid_ref.shape)
    grid_ref[...] = grid
    first, last = grid[:, :HALO, :], grid[:, cols - HALO :, :]
    even = lax.rem(lax.axis_index("gx"), 2) == 0
    edgea_ref[...] = jnp.where(even, last, first)
    edgeb_ref[...] = jnp.where(even, first, last)


def with_columns(own, from_a, from_b):
    a = lax.axis_index("gx")
    even = lax.rem(a, 2) == 0
    right = jnp.where(even, from_a, from_b)
    left = jnp.where(even, from_b, from_a)
    right = jnp.where(a < lax.axis_size("gx") - 1, right, 0.0)
    left = jnp.where(a > 0, left, 0.0)
    return jnp.concatenate([left, own, right], axis=1)


def row_edge(wide, last):
    rows = wide.shape[1]
    tile = jnp.where(last, wide[:, rows - 128 :], wide[:, :128]).T
    return jnp.where(last, tile[128 - HALO :], tile[:HALO])


def put_edges(ref, at, edge):
    extra = edge.shape[1] - WIDE
    ref[at : at + HALO, :] = edge[:, :WIDE]
    ref[at + HALO : at + 2 * HALO, :] = jnp.concatenate(
        [edge[:, WIDE:], jnp.zeros((HALO, WIDE - extra), F32)], axis=1
    )


def get_edges(ref, at, count):
    return jnp.concatenate(
        [ref[at : at + HALO, :], ref[at + HALO : at + 2 * HALO, : count - WIDE]], axis=1
    )


def y_edges(refs, at, wide):
    even = lax.rem(lax.axis_index("gy"), 2) == 0
    for kind, ref in enumerate(refs):
        put_edges(ref, at, row_edge(wide, even if kind == 0 else jnp.logical_not(even)))


def halo_of(ref, cols, layers, top):
    return ref[top:, :].reshape(layers, HALO, ref.shape[1])


def forward_kernel(nyc, recva_ref, recvb_ref, owny_ref, cond_ref, after_ref, *msgy_refs):
    layers, cols, rows = cond_ref.shape
    size, top = 3 * GROUP, nyc * 3 * GROUP
    for y, ref in enumerate(msgy_refs):
        ref[:size, :] = owny_ref[y * size : (y + 1) * size, :]
        ref[size : 2 * size, :] = recva_ref[(y + 1) * size : (y + 2) * size, :]
        ref[2 * size : 3 * size, :] = recvb_ref[(y + 1) * size : (y + 2) * size, :]
    wide = with_columns(
        cond_ref[...], halo_of(recva_ref, cols, layers, top), halo_of(recvb_ref, cols, layers, top)
    )
    y_edges(msgy_refs, 3 * size, wide.reshape(-1, rows))


def power_edge_kernel(grid_ref, froma_ref, fromb_ref, *edge_refs):
    wide = with_columns(grid_ref[...], froma_ref[...], fromb_ref[...])
    y_edges(edge_refs, 0, wide.reshape(-1, grid_ref.shape[2]))


def with_rows(wide, edges):
    b, ny = lax.axis_index("gy"), lax.axis_size("gy")
    layers, span, rows = wide.shape
    count = layers * span
    even = lax.rem(b, 2) == 0
    one = edges[0]
    two = edges[1] if len(edges) > 1 else jnp.zeros_like(one)
    after = jnp.where(b < ny - 1, jnp.where(even, one, two), 0.0)
    before = jnp.where(b > 0, jnp.where(even, two, one), 0.0)
    tile = jnp.concatenate([after, jnp.zeros((128 - 2 * HALO, count), F32), before], axis=0).T
    return jnp.concatenate([wide, tile.reshape(layers, span, 128)], axis=2)


def shifts(span, wide_rows):
    return (
        lambda x: pltpu.roll(x, span - 1, 0),
        lambda x: pltpu.roll(x, 1, 0),
        lambda x: pltpu.roll(x, wide_rows - 1, 1),
        lambda x: pltpu.roll(x, 1, 1),
    )


def face_kernel(nyc, cond_ref, recva_ref, recvb_ref, coupling_ref, *refs):
    recvy_refs, (fc_ref, fr_ref, fl_ref, e_ref, k_ref) = refs[: nyc - 1], refs[nyc - 1 :]
    layers, cols, rows = cond_ref.shape
    span, wide_rows = cols + 2 * HALO, rows + 128
    count = layers * span
    top = nyc * 3 * GROUP
    a, b = lax.axis_index("gx"), lax.axis_index("gy")
    nx, ny = lax.axis_size("gx"), lax.axis_size("gy")
    k_ref[...] = with_rows(
        with_columns(
            cond_ref[...],
            halo_of(recva_ref, cols, layers, top),
            halo_of(recvb_ref, cols, layers, top),
        ),
        [get_edges(ref, 9 * GROUP, count) for ref in recvy_refs],
    )
    shape = (span, wide_rows)
    c_i = lax.broadcasted_iota(jnp.int32, shape, 0)
    r_i = lax.broadcasted_iota(jnp.int32, shape, 1)
    c_low = jnp.where(a > 0, 0, HALO)
    c_high = jnp.where(a < nx - 1, span, span - HALO)
    r_high = jnp.where(b < ny - 1, rows + HALO, rows)
    r_low = jnp.where(b > 0, wide_rows - HALO, wide_rows)
    inside = jnp.where((c_i >= c_low) & (c_i < c_high) & ((r_i < r_high) | (r_i >= r_low)), 1.0, 0.0)
    next_c, prev_c, next_r, prev_r = shifts(span, wide_rows)
    both_c, both_r = inside * next_c(inside), inside * next_r(inside)
    for l in range(layers):
        k = k_ref[l]
        face_c, face_r = 0.5 * (k + next_c(k)), 0.5 * (k + next_r(k))
        kept_c, kept_r = face_c * both_c, face_r * both_r
        fc_ref[l], fr_ref[l] = kept_c, kept_r
        lost_c, lost_r = face_c - kept_c, face_r - kept_r
        e_ref[l] = SINK_RATE + ((lost_c + prev_c(lost_c)) + (lost_r + prev_r(lost_r)))
        if l + 1 < layers:
            fl_ref[l] = coupling_ref[l] * (0.5 * (k + k_ref[l + 1])) * inside


def solve_kernel(nyc, grid_ref, froma_ref, fromb_ref, fc_ref, fr_ref, fl_ref, e_ref, *refs):
    edge_refs, (warmth_ref, slope_ref, p_ref, v_ref, u_ref) = refs[: nyc - 1], refs[nyc - 1 :]
    layers, cols, rows = grid_ref.shape
    span, wide_rows = cols + 2 * HALO, rows + 128
    p_ref[...] = with_rows(
        with_columns(grid_ref[...], froma_ref[...], fromb_ref[...]),
        [get_edges(ref, 0, layers * span) for ref in edge_refs],
    )
    next_c, prev_c, next_r, prev_r = shifts(span, wide_rows)
    middle = 0.5 * (HIGH_BOUND + LOW_BOUND)
    spread = 0.5 * (HIGH_BOUND - LOW_BOUND)
    sigma = middle / spread
    now = 1.0 / sigma
    for l in range(layers):
        start = p_ref[l] / middle
        v_ref[0, l] = start
        u_ref[l] = start
    for sweep in range(ITERS):
        later = 1.0 / (2.0 * sigma - now)
        keep, gain = later * now, 2.0 * later / spread
        old, new = sweep % 2, (sweep + 1) % 2
        below = None
        for l in range(layers):
            v = v_ref[old, l]
            flow_c = fc_ref[l] * (v - next_c(v))
            flow_r = fr_ref[l] * (v - next_r(v))
            result = e_ref[l] * v + (flow_c - prev_c(flow_c)) + (flow_r - prev_r(flow_r))
            if below is not None:
                result = result - below
            if l + 1 < layers:
                below = fl_ref[l] * (v - v_ref[old, l + 1])
                result = result + below
            advance = keep * u_ref[l] + gain * (p_ref[l] - result)
            u_ref[l] = advance
            v_ref[new, l] = v + advance
        now = later
    final = ITERS % 2
    cells = layers * cols
    for l in range(layers):
        v = v_ref[final, l]
        warmth_ref[l] = v[HALO : HALO + cols, :rows]
        for f, slope in enumerate((0.5 * (next_c(v) - prev_c(v)), 0.5 * (next_r(v) - prev_r(v)))):
            high, low = pieces(slope[HALO : HALO + cols, :rows])
            at = f * cells + l * cols
            slope_ref[at : at + cols, :rows] = high.astype(BF16)
            slope_ref[at : at + cols, rows:] = low.astype(BF16)


def gather_block(slope, lc, r):
    cells = slope.shape[0] // 2
    mark = onehot(r, slope.shape[1] // 2)
    found = dot(slope, jnp.concatenate([mark, mark], axis=0))
    here = row_iota(cells, lc.shape[1]) == lc
    return [
        jnp.sum(jnp.where(here, found[f * cells : (f + 1) * cells], 0.0), axis=0, keepdims=True)
        for f in range(2)
    ]


def gather_kernel(sources, slope_ref, *refs):
    ins, out_ref = refs[:-1], refs[-1]
    rows = slope_ref.shape[1] // 2
    for g, (which, at) in enumerate(sources):
        for t in range(GROUP):
            code = ins[which][at + t : at + t + 1, :]
            lc = jnp.floor(code * (1.0 / rows))
            for f, value in enumerate(gather_block(slope_ref[...], lc, code - lc * rows)):
                row = (g * 2 + f) * GROUP + t
                out_ref[row : row + 1, :] = value


def stay_gather_kernel(slope_ref, field_ref, out_ref):
    step = 32

    def body(j, carry):
        base = pl.multiple_of(j * step, step)
        lcs, rs = field_ref[0, pl.ds(base, step), :], field_ref[1, pl.ds(base, step), :]
        for i in range(0, step, 4):
            many = lambda x: lanes([x[i + k : i + k + 1] for k in range(4)])
            at = pl.multiple_of(base * 128 + i * 128, 512)
            for f, value in enumerate(gather_block(slope_ref[...], many(lcs), many(rs))):
                out_ref[f : f + 1, pl.ds(at, 512)] = value
        return carry

    lax.fori_loop(0, field_ref.shape[1] // step, body, 0)


def reply_kernel(nyc, near_ref, *refs):
    size = 2 * GROUP
    backs, (a_ref, b_ref) = refs[: nyc - 1], refs[nyc - 1 :]
    a_ref[:size, :] = near_ref[:size, :]
    b_ref[:size, :] = near_ref[size:, :]
    for y, ref in enumerate(backs):
        a_ref[(y + 1) * size : (y + 2) * size, :] = ref[size : 2 * size, :]
        b_ref[(y + 1) * size : (y + 2) * size, :] = ref[2 * size : 3 * size, :]


def unpack_kernel(nyc, backa_ref, backb_ref, *refs):
    backy, (stay_ref, slot_ref, power_ref, out_ref, table_ref) = refs[: nyc - 1], refs[nyc - 1 :]
    groups = [(backa_ref, y) for y in range(nyc)] + [(backb_ref, y) for y in range(nyc)]
    groups += [(ref, 0) for ref in backy]
    table = len(groups) * GROUP
    for f in range(2):
        whole = jnp.concatenate(
            [ref[(2 * at + f) * GROUP : (2 * at + f + 1) * GROUP, :] for ref, at in groups], axis=0
        )
        high, low = pieces(whole)
        table_ref[f * table : (f + 1) * table, :WIDE] = high
        table_ref[f * table : (f + 1) * table, WIDE:] = low
    source = table_ref[...].astype(BF16)
    step = 32

    def body(j, carry):
        base = pl.multiple_of(j * step, step)
        slots = slot_ref[pl.ds(base, step), :]
        qs = jnp.floor(slots * (1.0 / WIDE))
        lams = slots - qs * WIDE
        powers = power_ref[pl.ds(base, step), :]
        for i in range(0, step, 8):
            many = lambda x: lanes([x[i + k : i + k + 1] for k in range(8)])
            at = pl.multiple_of(base * 128 + i * 128, 1024)
            mark = onehot(many(lams), WIDE)
            found = dot(source, jnp.concatenate([mark, mark], axis=0))
            place = many(qs)
            here = row_iota(table, 1024) == place
            for f in range(2):
                value = jnp.sum(
                    jnp.where(here, found[f * table : (f + 1) * table], 0.0), axis=0, keepdims=True
                )
                value = jnp.where(place >= 0.0, value, stay_ref[f : f + 1, pl.ds(at, 1024)])
                out_ref[f : f + 1, pl.ds(at, 1024)] = -many(powers) * value
        return carry

    lax.fori_loop(0, slot_ref.shape[0] // step, body, 0)


def call(kernel, outs, scratch, *args, spaces={}):
    space = pl.BlockSpec(memory_space=pltpu.VMEM)
    specs = [pl.BlockSpec(memory_space=spaces.get(i, pltpu.VMEM)) for i in range(len(args))]
    shapes = [jax.ShapeDtypeStruct(shape, dtype) for shape, dtype in outs]
    return pl.pallas_call(
        kernel,
        out_shape=shapes,
        in_specs=specs,
        out_specs=[space] * len(shapes),
        scratch_shapes=scratch,
        compiler_params=pltpu.CompilerParams(vmem_limit_bytes=48 * 1024 * 1024),
    )(*args)


def shards(
    cell_bin, cell_layer, cell_offset, cell_power, spill_weight, conductivity, layer_coupling
):
    layers, cols, rows = conductivity.shape
    cells = cell_bin.shape[0]
    nyc = 2 if lax.axis_size("gy") == 2 else 3
    count = layers * cols
    groups = 3 * nyc - 1
    flat = lambda x: x.reshape(cells // 128, 128)
    bins, layer, off = flat(cell_bin), flat(cell_layer), flat(cell_offset)
    power, spill = flat(cell_power), flat(spill_weight)
    square = bins.shape
    own = 3 * GROUP
    message = (nyc * own + layers * HALO, WIDE)
    vmem = lambda *shape: pltpu.VMEM(shape, F32)
    partial = functools.partial

    tile = conductivity.shape
    msg_a, msg_b, own_y, slot, fields, power = call(
        partial(pack_kernel, nyc, cols, rows),
        [
            (message, F32), (message, F32), (((nyc - 1) * own, WIDE), F32),
            (square, F32), ((6, *square), F32), (square, F32),
        ],
        [pltpu.VMEM(square, jnp.int32)] * 3
        + [
            vmem(*square), vmem(2, layers, HALO, rows), pltpu.SemaphoreType.DMA((7,)),
            vmem(6 * groups * GROUP, WIDE),
        ],
        bins, layer, off, power, spill, conductivity,
        spaces={i: pltpu.HBM for i in range(6)},
    )
    recv_a, recv_b = exchange(msg_a, 1, 0), exchange(msg_b, 2, 0)
    (stay_grid,) = call(
        partial(stay_deposit_kernel, cols),
        [((2 * count, rows), F32)],
        [vmem(4, *square)],
        fields, slot,
    )
    msg_y = call(
        partial(forward_kernel, nyc),
        [((3 * own + 2 * HALO, WIDE), F32)] * (nyc - 1),
        [],
        recv_a, recv_b, own_y, conductivity, stay_grid,
        spaces={4: pl.ANY},
    )
    recv_y = [exchange(m, 0, i + 1) for i, m in enumerate(msg_y)]
    (near_grid,) = call(
        partial(near_deposit_kernel, cols),
        [((2 * count, rows), F32)],
        [],
        stay_grid, recv_a, recv_b,
    )
    edge = (layers, HALO, rows)
    grid, edge_a, edge_b = call(
        partial(far_deposit_kernel, cols, nyc),
        [(conductivity.shape, F32), (edge, F32), (edge, F32)],
        [vmem(2 * count, rows)],
        near_grid, *recv_y,
    )
    from_a, from_b = exchange(edge_a, 1, 0), exchange(edge_b, 2, 0)
    edges = call(
        power_edge_kernel, [((2 * HALO, WIDE), F32)] * (nyc - 1), [], grid, from_a, from_b
    )
    from_y = [exchange(e, 0, i + 1) for i, e in enumerate(edges)]
    big = (layers, cols + 2 * HALO, rows + 128)
    faces = call(
        partial(face_kernel, nyc),
        [(big, F32)] * 4,
        [vmem(*big)],
        conductivity, recv_a, recv_b, layer_coupling, *recv_y,
        spaces={3: pltpu.SMEM},
    )
    final_warmth, slope = call(
        partial(solve_kernel, nyc),
        [(tile, F32), ((2 * count, 2 * rows), BF16)],
        [vmem(*big), vmem(2, *big), vmem(*big)],
        grid, from_a, from_b, *faces, *from_y,
    )
    answer_y = [
        call(
            partial(gather_kernel, [(0, own * i) for i in range(3)]),
            [((6 * GROUP, WIDE), F32)],
            [],
            slope, r,
        )[0]
        for r in recv_y
    ]
    back_y = [exchange(m, 0, i + 1) for i, m in enumerate(answer_y)]
    (near_answer,) = call(
        partial(gather_kernel, [(0, 0), (1, 0)]),
        [((4 * GROUP, WIDE), F32)],
        [],
        slope, recv_a, recv_b,
    )
    answer_a, answer_b = call(
        partial(reply_kernel, nyc),
        [((2 * nyc * GROUP, WIDE), F32)] * 2,
        [],
        near_answer, *back_y,
    )
    back_a, back_b = exchange(answer_a, 1, 0), exchange(answer_b, 2, 0)
    (stay_value,) = call(stay_gather_kernel, [((2, cells), F32)], [], slope, fields)
    (pull,) = call(
        partial(unpack_kernel, nyc),
        [((2, cells), F32)],
        [vmem(2 * groups * GROUP, 2 * WIDE)],
        back_a, back_b, *back_y, stay_value, slot, power,
    )
    return final_warmth, pull


def solution(mesh):
    cell = P(("gx", "gy"))
    tile = P(None, "gx", "gy")
    return jax.shard_map(
        shards,
        mesh=mesh,
        in_specs=(cell, cell, cell, cell, cell, tile, P()),
        out_specs=(tile, P(None, ("gx", "gy"))),
        check_vma=False,
    )
```

```python
import functools

import jax
import jax.numpy as jnp
from jax import lax
from jax.experimental import pallas as pl
from jax.experimental.pallas import tpu as pltpu
from jax.sharding import PartitionSpec as P

ITERS = 4
CAP = 2048
SINK_RATE = 0.5
LOW_BOUND = 0.5
HIGH_BOUND = 33.0

WIDE = 256
GROUP = CAP // WIDE
HALO = 8
F32, BF16 = jnp.float32, jnp.bfloat16


def partner(place, kind, count):
    if kind == 0:
        return place
    if kind == 1:
        return place ^ 1
    return (place - 1 if place % 2 == 0 else place + 1) % count


def exchange(value, x_kind, y_kind):
    nx, ny = lax.axis_size("gx"), lax.axis_size("gy")
    pairs = [
        (a * ny + b, partner(a, x_kind, nx) * ny + partner(b, y_kind, ny))
        for a in range(nx)
        for b in range(ny)
    ]
    return lax.ppermute(value, ("gx", "gy"), pairs)


def pieces(value):
    high = value.astype(BF16).astype(F32)
    return high, value - high


def row_iota(count, width=128):
    return lax.broadcasted_iota(jnp.int32, (count, width), 0).astype(F32)


def onehot(row, count):
    return jnp.where(
        row_iota(count, row.shape[1]).astype(BF16) == row.astype(BF16),
        jnp.ones((), BF16),
        jnp.zeros((), BF16),
    )


def lanes(parts):
    return jnp.concatenate(parts, axis=1) if len(parts) > 1 else parts[0]


def transposed_dot(left, right):
    return lax.dot_general(left, right, (((1,), (1,)), ((), ())), preferred_element_type=F32)


def dot(left, right):
    return lax.dot_general(left, right, (((1,), (0,)), ((), ())), preferred_element_type=F32)


def kind_of(step, place):
    ahead = 1 - 2 * lax.rem(place, 2)
    return jnp.where(step == 0, 0, jnp.where(step == ahead, 1, 2))


def pack_kernel(
    nyc, cols, rows,
    bin_hbm, layer_hbm, off_hbm, power_hbm, spill_hbm, cond_hbm,
    msga_ref, msgb_ref, owny_ref, slot_ref, field_ref, power_ref,
    bin_ref, layer_ref, off_ref, spill_ref, edge_ref, sems, acc_ref,
):
    a, b = lax.axis_index("gx"), lax.axis_index("gy")
    copies = [
        pltpu.make_async_copy(src, dst, sems.at[i])
        for i, (src, dst) in enumerate(
            [
                (off_hbm, off_ref), (bin_hbm, bin_ref), (layer_hbm, layer_ref),
                (power_hbm, power_ref), (spill_hbm, spill_ref),
                (cond_hbm.at[:, :HALO, :], edge_ref.at[0]),
                (cond_hbm.at[:, cols - HALO :, :], edge_ref.at[1]),
            ]
        )
    ]
    for copy in copies:
        copy.start()
    acc_ref[...] = jnp.zeros_like(acc_ref)
    groups = 3 * nyc - 1
    table = groups * GROUP
    copies[0].wait()
    off = off_ref[...]
    col_code = (off >= 3).astype(jnp.int32) + (off >= 6).astype(jnp.int32)
    x_kind = kind_of(col_code - 1, a)
    y_kind = kind_of(off - 3 * col_code - 1, b)
    group = jnp.where(x_kind > 0, (x_kind - 1) * nyc + y_kind, 2 * nyc - 1 + y_kind)
    group = jnp.where(off == 4, -1, group)
    size = off.shape[0]
    r_i = lax.broadcasted_iota(jnp.int32, (size, size), 0)
    c_i = lax.broadcasted_iota(jnp.int32, (size, size), 1)
    upper = jnp.where(r_i < c_i, 1.0, 0.0).astype(BF16)
    lower = jnp.where(r_i > c_i, 1.0, 0.0).astype(BF16)
    ones = jnp.ones((size, size), BF16)
    slot = jnp.full(off.shape, -1.0, F32)
    for g in range(groups):
        mine = group == g
        mask = jnp.where(mine, 1.0, 0.0).astype(BF16)
        totals = dot(mask, ones).astype(BF16)
        rank = dot(mask, upper) + dot(lower, totals)
        slot = jnp.where(mine, rank + float(g * CAP), slot)
    slot_ref[...] = slot
    for copy in copies[1:]:
        copy.wait()
    code = layer_ref[...] * (cols * rows) + bin_ref[...]
    field_ref[0] = (code // rows).astype(F32)
    field_ref[1] = (code % rows).astype(F32)
    power = power_ref[...]
    spill = spill_ref[...]
    field_ref[2], field_ref[3] = pieces(power * (1.0 - spill))
    field_ref[4], field_ref[5] = pieces(power * spill)
    step = 32

    def body(j, carry):
        base = pl.multiple_of(j * step, step)
        slots = slot_ref[pl.ds(base, step), :]
        qs = jnp.floor(slots * (1.0 / WIDE))
        lams = slots - qs * WIDE
        vals = [field_ref[f, pl.ds(base, step), :] for f in range(6)]
        picks, marks = [], []
        for i in range(step):
            hit = row_iota(table) == qs[i : i + 1]
            picks.append(
                jnp.concatenate([jnp.where(hit, v[i : i + 1], 0.0) for v in vals], axis=0).astype(BF16)
            )
            marks.append(onehot(lams[i : i + 1], WIDE))
        acc_ref[...] += transposed_dot(lanes(picks), lanes(marks))
        return carry

    lax.fori_loop(0, size // step, body, 0)
    out = [acc_ref[f * table : (f + 1) * table, :] for f in range(6)]
    sent = [out[0] * float(rows) + out[1], out[2] + out[3], out[4] + out[5]]

    def put(ref, at, g):
        for f in range(3):
            ref[(at * 3 + f) * GROUP : (at * 3 + f + 1) * GROUP, :] = sent[f][
                g * GROUP : (g + 1) * GROUP
            ]

    for y in range(nyc):
        put(msga_ref, y, y)
        put(msgb_ref, y, nyc + y)
        if y:
            put(owny_ref, y - 1, 2 * nyc + y - 1)
    first, last = edge_ref[0], edge_ref[1]
    even = lax.rem(a, 2) == 0
    top = nyc * 3 * GROUP
    flat = (-1, rows)
    msga_ref[top:, :] = jnp.where(even, last, first).reshape(flat)
    msgb_ref[top:, :] = jnp.where(even, first, last).reshape(flat)


def deposit_block(lc, r, main, spill, cols, cells):
    picks, marks = [], []
    zero = jnp.zeros((), BF16)
    narrow = lambda x: x.astype(BF16)
    for lc_i, r_i, (mh, ml), (sh, sl) in zip(lc, r, main, spill):
        spot = narrow(row_iota(cells, lc_i.shape[1]))
        other = jnp.where(lc_i >= float(cells - cols), lc_i - cols, lc_i + cols)
        here, there = spot == narrow(lc_i), spot == narrow(other)
        high = jnp.where(here, narrow(mh), jnp.where(there, narrow(sh), zero))
        low = jnp.where(here, narrow(ml), jnp.where(there, narrow(sl), zero))
        picks.append(jnp.concatenate([high, low], axis=0))
        marks.append(onehot(r_i, WIDE))
    return transposed_dot(lanes(picks), lanes(marks))


def deposit_stays(grid_ref, field_ref, slot_ref, first, last, cols):
    count, step = grid_ref.shape[0] // 2, 32
    stays = slot_ref[first:last, :] < 0.0
    vals = [jnp.where(stays, field_ref[2 + f, first:last, :], 0.0) for f in range(4)]
    lcs, rs = field_ref[0, first:last, :], field_ref[1, first:last, :]
    for base in range(0, last - first, step):
        rows_of = lambda x: [x[base + i : base + i + 1] for i in range(step)]
        parts = [rows_of(v) for v in vals]
        grid_ref[...] += deposit_block(
            rows_of(lcs), rows_of(rs), list(zip(parts[0], parts[1])),
            list(zip(parts[2], parts[3])), cols, count,
        )


def stay_deposit_kernel(cols, split, field_ref, slot_ref, grid_ref):
    grid_ref[...] = jnp.zeros_like(grid_ref)
    deposit_stays(grid_ref, field_ref, slot_ref, 0, split, cols)


def deposit_groups(grid_ref, sources, cols):
    count, rows = grid_ref.shape[0] // 2, grid_ref.shape[1]
    lc, r, main, spill = [], [], [], []
    for ref, at in sources:
        for row in range(at, at + GROUP):
            code = ref[row : row + 1, :]
            lc_i = jnp.floor(code * (1.0 / rows))
            lc.append(lc_i)
            r.append(code - lc_i * rows)
            main.append(pieces(ref[row + GROUP : row + GROUP + 1, :]))
            spill.append(pieces(ref[row + 2 * GROUP : row + 2 * GROUP + 1, :]))
    grid_ref[...] += deposit_block(lc, r, main, spill, cols, count)


def near_deposit_kernel(cols, split, stay_ref, recva_ref, recvb_ref, field_ref, slot_ref, grid_ref):
    grid_ref[...] = stay_ref[...]
    deposit_stays(grid_ref, field_ref, slot_ref, split, slot_ref.shape[0], cols)
    deposit_groups(grid_ref, [(recva_ref, 0), (recvb_ref, 0)], cols)


def far_deposit_kernel(cols, nyc, *refs):
    near_ref, recvy = refs[0], refs[1:nyc]
    grid_ref, edgea_ref, edgeb_ref, acc_ref = refs[nyc:]
    acc_ref[...] = near_ref[...]
    sources = [(ref, 3 * GROUP * i) for ref in recvy for i in range(3)]
    deposit_groups(acc_ref, sources, cols)
    count = acc_ref.shape[0] // 2
    grid = (acc_ref[:count, :] + acc_ref[count:, :]).reshape(grid_ref.shape)
    grid_ref[...] = grid
    first, last = grid[:, :HALO, :], grid[:, cols - HALO :, :]
    even = lax.rem(lax.axis_index("gx"), 2) == 0
    edgea_ref[...] = jnp.where(even, last, first)
    edgeb_ref[...] = jnp.where(even, first, last)


def with_columns(own, from_a, from_b):
    a = lax.axis_index("gx")
    even = lax.rem(a, 2) == 0
    right = jnp.where(even, from_a, from_b)
    left = jnp.where(even, from_b, from_a)
    right = jnp.where(a < lax.axis_size("gx") - 1, right, 0.0)
    left = jnp.where(a > 0, left, 0.0)
    return jnp.concatenate([left, own, right], axis=1)


def row_edge(wide, last):
    rows = wide.shape[1]
    tile = jnp.where(last, wide[:, rows - 128 :], wide[:, :128]).T
    return jnp.where(last, tile[128 - HALO :], tile[:HALO])


def put_edges(ref, at, edge):
    extra = edge.shape[1] - WIDE
    ref[at : at + HALO, :] = edge[:, :WIDE]
    ref[at + HALO : at + 2 * HALO, :] = jnp.concatenate(
        [edge[:, WIDE:], jnp.zeros((HALO, WIDE - extra), F32)], axis=1
    )


def get_edges(ref, at, count):
    return jnp.concatenate(
        [ref[at : at + HALO, :], ref[at + HALO : at + 2 * HALO, : count - WIDE]], axis=1
    )


def y_edges(refs, at, wide):
    even = lax.rem(lax.axis_index("gy"), 2) == 0
    for kind, ref in enumerate(refs):
        put_edges(ref, at, row_edge(wide, even if kind == 0 else jnp.logical_not(even)))


def halo_of(ref, cols, layers, top):
    return ref[top:, :].reshape(layers, HALO, ref.shape[1])


def forward_kernel(nyc, recva_ref, recvb_ref, owny_ref, cond_ref, after_ref, *msgy_refs):
    layers, cols, rows = cond_ref.shape
    size, top = 3 * GROUP, nyc * 3 * GROUP
    for y, ref in enumerate(msgy_refs):
        ref[:size, :] = owny_ref[y * size : (y + 1) * size, :]
        ref[size : 2 * size, :] = recva_ref[(y + 1) * size : (y + 2) * size, :]
        ref[2 * size : 3 * size, :] = recvb_ref[(y + 1) * size : (y + 2) * size, :]
    wide = with_columns(
        cond_ref[...], halo_of(recva_ref, cols, layers, top), halo_of(recvb_ref, cols, layers, top)
    )
    y_edges(msgy_refs, 3 * size, wide.reshape(-1, rows))


def power_edge_kernel(grid_ref, froma_ref, fromb_ref, *edge_refs):
    wide = with_columns(grid_ref[...], froma_ref[...], fromb_ref[...])
    y_edges(edge_refs, 0, wide.reshape(-1, grid_ref.shape[2]))


def with_rows(wide, edges):
    b, ny = lax.axis_index("gy"), lax.axis_size("gy")
    layers, span, rows = wide.shape
    count = layers * span
    even = lax.rem(b, 2) == 0
    one = edges[0]
    two = edges[1] if len(edges) > 1 else jnp.zeros_like(one)
    after = jnp.where(b < ny - 1, jnp.where(even, one, two), 0.0)
    before = jnp.where(b > 0, jnp.where(even, two, one), 0.0)
    tile = jnp.concatenate([after, jnp.zeros((128 - 2 * HALO, count), F32), before], axis=0).T
    return jnp.concatenate([wide, tile.reshape(layers, span, 128)], axis=2)


def shifts(span, wide_rows):
    return (
        lambda x: pltpu.roll(x, span - 1, 0),
        lambda x: pltpu.roll(x, 1, 0),
        lambda x: pltpu.roll(x, wide_rows - 1, 1),
        lambda x: pltpu.roll(x, 1, 1),
    )


def face_kernel(nyc, cond_ref, recva_ref, recvb_ref, coupling_ref, *refs):
    recvy_refs, (fc_ref, fr_ref, fl_ref, e_ref, k_ref) = refs[: nyc - 1], refs[nyc - 1 :]
    layers, cols, rows = cond_ref.shape
    span, wide_rows = cols + 2 * HALO, rows + 128
    count = layers * span
    top = nyc * 3 * GROUP
    a, b = lax.axis_index("gx"), lax.axis_index("gy")
    nx, ny = lax.axis_size("gx"), lax.axis_size("gy")
    k_ref[...] = with_rows(
        with_columns(
            cond_ref[...],
            halo_of(recva_ref, cols, layers, top),
            halo_of(recvb_ref, cols, layers, top),
        ),
        [get_edges(ref, 9 * GROUP, count) for ref in recvy_refs],
    )
    shape = (span, wide_rows)
    c_i = lax.broadcasted_iota(jnp.int32, shape, 0)
    r_i = lax.broadcasted_iota(jnp.int32, shape, 1)
    c_low = jnp.where(a > 0, 0, HALO)
    c_high = jnp.where(a < nx - 1, span, span - HALO)
    r_high = jnp.where(b < ny - 1, rows + HALO, rows)
    r_low = jnp.where(b > 0, wide_rows - HALO, wide_rows)
    inside = jnp.where((c_i >= c_low) & (c_i < c_high) & ((r_i < r_high) | (r_i >= r_low)), 1.0, 0.0)
    next_c, prev_c, next_r, prev_r = shifts(span, wide_rows)
    both_c, both_r = inside * next_c(inside), inside * next_r(inside)
    for l in range(layers):
        k = k_ref[l]
        face_c, face_r = 0.5 * (k + next_c(k)), 0.5 * (k + next_r(k))
        kept_c, kept_r = face_c * both_c, face_r * both_r
        fc_ref[l], fr_ref[l] = kept_c, kept_r
        lost_c, lost_r = face_c - kept_c, face_r - kept_r
        e_ref[l] = SINK_RATE + ((lost_c + prev_c(lost_c)) + (lost_r + prev_r(lost_r)))
        if l + 1 < layers:
            fl_ref[l] = coupling_ref[l] * (0.5 * (k + k_ref[l + 1])) * inside


def solve_kernel(nyc, grid_ref, froma_ref, fromb_ref, fc_ref, fr_ref, fl_ref, e_ref, *refs):
    edge_refs, (warmth_ref, slope_ref, p_ref, v_ref, u_ref) = refs[: nyc - 1], refs[nyc - 1 :]
    layers, cols, rows = grid_ref.shape
    span, wide_rows = cols + 2 * HALO, rows + 128
    p_ref[...] = with_rows(
        with_columns(grid_ref[...], froma_ref[...], fromb_ref[...]),
        [get_edges(ref, 0, layers * span) for ref in edge_refs],
    )
    next_c, prev_c, next_r, prev_r = shifts(span, wide_rows)
    middle = 0.5 * (HIGH_BOUND + LOW_BOUND)
    spread = 0.5 * (HIGH_BOUND - LOW_BOUND)
    sigma = middle / spread
    now = 1.0 / sigma
    for l in range(layers):
        start = p_ref[l] / middle
        v_ref[0, l] = start
        u_ref[l] = start
    for sweep in range(ITERS):
        later = 1.0 / (2.0 * sigma - now)
        keep, gain = later * now, 2.0 * later / spread
        old, new = sweep % 2, (sweep + 1) % 2
        below = None
        for l in range(layers):
            v = v_ref[old, l]
            flow_c = fc_ref[l] * (v - next_c(v))
            flow_r = fr_ref[l] * (v - next_r(v))
            result = e_ref[l] * v + (flow_c - prev_c(flow_c)) + (flow_r - prev_r(flow_r))
            if below is not None:
                result = result - below
            if l + 1 < layers:
                below = fl_ref[l] * (v - v_ref[old, l + 1])
                result = result + below
            advance = keep * u_ref[l] + gain * (p_ref[l] - result)
            u_ref[l] = advance
            v_ref[new, l] = v + advance
        now = later
    final = ITERS % 2
    cells = layers * cols
    for l in range(layers):
        v = v_ref[final, l]
        warmth_ref[l] = v[HALO : HALO + cols, :rows]
        for f, slope in enumerate((0.5 * (next_c(v) - prev_c(v)), 0.5 * (next_r(v) - prev_r(v)))):
            high, low = pieces(slope[HALO : HALO + cols, :rows])
            for part, piece in enumerate((high, low)):
                at = (part * 2 + f) * cells + l * cols
                slope_ref[at : at + cols, :] = piece.astype(BF16)


def gather_block(slope, lc, r):
    cells = slope.shape[0] // 4
    found = dot(slope, onehot(r, slope.shape[1]))
    here = row_iota(cells, lc.shape[1]) == lc
    return [
        jnp.sum(
            jnp.where(
                here,
                found[f * cells : (f + 1) * cells] + found[(2 + f) * cells : (3 + f) * cells],
                0.0,
            ),
            axis=0,
            keepdims=True,
        )
        for f in range(2)
    ]


def gather_kernel(sources, slope_ref, *refs):
    ins, out_ref = refs[:-1], refs[-1]
    rows = slope_ref.shape[1]
    for g, (which, at) in enumerate(sources):
        for t in range(GROUP):
            code = ins[which][at + t : at + t + 1, :]
            lc = jnp.floor(code * (1.0 / rows))
            for f, value in enumerate(gather_block(slope_ref[...], lc, code - lc * rows)):
                row = (g * 2 + f) * GROUP + t
                out_ref[row : row + 1, :] = value


def stay_gather_kernel(slope_ref, field_ref, out_ref):
    step = 32

    def body(j, carry):
        base = pl.multiple_of(j * step, step)
        lcs, rs = field_ref[0, pl.ds(base, step), :], field_ref[1, pl.ds(base, step), :]
        for i in range(0, step, 4):
            many = lambda x: lanes([x[i + k : i + k + 1] for k in range(4)])
            at = pl.multiple_of(base * 128 + i * 128, 512)
            for f, value in enumerate(gather_block(slope_ref[...], many(lcs), many(rs))):
                out_ref[f : f + 1, pl.ds(at, 512)] = value
        return carry

    lax.fori_loop(0, field_ref.shape[1] // step, body, 0)


def reply_kernel(nyc, near_ref, *refs):
    size = 2 * GROUP
    backs, (a_ref, b_ref) = refs[: nyc - 1], refs[nyc - 1 :]
    a_ref[:size, :] = near_ref[:size, :]
    b_ref[:size, :] = near_ref[size:, :]
    for y, ref in enumerate(backs):
        a_ref[(y + 1) * size : (y + 2) * size, :] = ref[size : 2 * size, :]
        b_ref[(y + 1) * size : (y + 2) * size, :] = ref[2 * size : 3 * size, :]


def unpack_kernel(nyc, backa_ref, backb_ref, *refs):
    backy, (stay_ref, slot_ref, power_ref, out_ref, table_ref) = refs[: nyc - 1], refs[nyc - 1 :]
    groups = [(backa_ref, y) for y in range(nyc)] + [(backb_ref, y) for y in range(nyc)]
    groups += [(ref, 0) for ref in backy]
    table = len(groups) * GROUP
    for f in range(2):
        whole = jnp.concatenate(
            [ref[(2 * at + f) * GROUP : (2 * at + f + 1) * GROUP, :] for ref, at in groups], axis=0
        )
        for part, piece in enumerate(pieces(whole)):
            at = (part * 2 + f) * table
            table_ref[at : at + table, :] = piece
    source = table_ref[...].astype(BF16)
    step = 32

    def body(j, carry):
        base = pl.multiple_of(j * step, step)
        slots = slot_ref[pl.ds(base, step), :]
        qs = jnp.floor(slots * (1.0 / WIDE))
        lams = slots - qs * WIDE
        powers = power_ref[pl.ds(base, step), :]
        for i in range(0, step, 8):
            many = lambda x: lanes([x[i + k : i + k + 1] for k in range(8)])
            at = pl.multiple_of(base * 128 + i * 128, 1024)
            mark = onehot(many(lams), WIDE)
            found = dot(source, mark)
            place = many(qs)
            here = row_iota(table, 1024) == place
            for f in range(2):
                both = found[f * table : (f + 1) * table] + found[(2 + f) * table : (3 + f) * table]
                value = jnp.sum(jnp.where(here, both, 0.0), axis=0, keepdims=True)
                value = jnp.where(place >= 0.0, value, stay_ref[f : f + 1, pl.ds(at, 1024)])
                out_ref[f : f + 1, pl.ds(at, 1024)] = -many(powers) * value
        return carry

    lax.fori_loop(0, slot_ref.shape[0] // step, body, 0)


def call(kernel, outs, scratch, *args, spaces={}):
    space = pl.BlockSpec(memory_space=pltpu.VMEM)
    specs = [pl.BlockSpec(memory_space=spaces.get(i, pltpu.VMEM)) for i in range(len(args))]
    shapes = [jax.ShapeDtypeStruct(shape, dtype) for shape, dtype in outs]
    return pl.pallas_call(
        kernel,
        out_shape=shapes,
        in_specs=specs,
        out_specs=[space] * len(shapes),
        scratch_shapes=scratch,
        compiler_params=pltpu.CompilerParams(vmem_limit_bytes=48 * 1024 * 1024),
    )(*args)


def shards(
    cell_bin, cell_layer, cell_offset, cell_power, spill_weight, conductivity, layer_coupling
):
    layers, cols, rows = conductivity.shape
    cells = cell_bin.shape[0]
    nyc = 2 if lax.axis_size("gy") == 2 else 3
    count = layers * cols
    groups = 3 * nyc - 1
    flat = lambda x: x.reshape(cells // 128, 128)
    bins, layer, off = flat(cell_bin), flat(cell_layer), flat(cell_offset)
    power, spill = flat(cell_power), flat(spill_weight)
    square = bins.shape
    split = square[0] * 3 // 4
    own = 3 * GROUP
    message = (nyc * own + layers * HALO, WIDE)
    vmem = lambda *shape: pltpu.VMEM(shape, F32)
    partial = functools.partial

    tile = conductivity.shape
    msg_a, msg_b, own_y, slot, fields, power = call(
        partial(pack_kernel, nyc, cols, rows),
        [
            (message, F32), (message, F32), (((nyc - 1) * own, WIDE), F32),
            (square, F32), ((6, *square), F32), (square, F32),
        ],
        [pltpu.VMEM(square, jnp.int32)] * 3
        + [
            vmem(*square), vmem(2, layers, HALO, rows), pltpu.SemaphoreType.DMA((7,)),
            vmem(6 * groups * GROUP, WIDE),
        ],
        *[
            pltpu.with_memory_space_constraint(x, pltpu.HBM)
            for x in (bins, layer, off, power, spill, conductivity)
        ],
        spaces={i: pltpu.HBM for i in range(6)},
    )
    recv_a, recv_b = exchange(msg_a, 1, 0), exchange(msg_b, 2, 0)
    (stay_grid,) = call(
        partial(stay_deposit_kernel, cols, split),
        [((2 * count, rows), F32)],
        [],
        fields, slot,
    )
    msg_y = call(
        partial(forward_kernel, nyc),
        [((3 * own + 2 * HALO, WIDE), F32)] * (nyc - 1),
        [],
        recv_a, recv_b, own_y, conductivity, stay_grid,
        spaces={4: pl.ANY},
    )
    recv_y = [exchange(m, 0, i + 1) for i, m in enumerate(msg_y)]
    (near_grid,) = call(
        partial(near_deposit_kernel, cols, split),
        [((2 * count, rows), F32)],
        [],
        stay_grid, recv_a, recv_b, fields, slot,
    )
    edge = (layers, HALO, rows)
    grid, edge_a, edge_b = call(
        partial(far_deposit_kernel, cols, nyc),
        [(conductivity.shape, F32), (edge, F32), (edge, F32)],
        [vmem(2 * count, rows)],
        near_grid, *recv_y,
    )
    from_a, from_b = exchange(edge_a, 1, 0), exchange(edge_b, 2, 0)
    edges = call(
        power_edge_kernel, [((2 * HALO, WIDE), F32)] * (nyc - 1), [], grid, from_a, from_b
    )
    from_y = [exchange(e, 0, i + 1) for i, e in enumerate(edges)]
    big = (layers, cols + 2 * HALO, rows + 128)
    faces = call(
        partial(face_kernel, nyc),
        [(big, F32)] * 4,
        [vmem(*big)],
        conductivity, recv_a, recv_b, layer_coupling, *recv_y,
        spaces={3: pltpu.SMEM},
    )
    final_warmth, slope = call(
        partial(solve_kernel, nyc),
        [(tile, F32), ((4 * count, rows), BF16)],
        [vmem(*big), vmem(2, *big), vmem(*big)],
        grid, from_a, from_b, *faces, *from_y,
    )
    answer_y = [
        call(
            partial(gather_kernel, [(0, own * i) for i in range(3)]),
            [((6 * GROUP, WIDE), F32)],
            [],
            slope, r,
        )[0]
        for r in recv_y
    ]
    back_y = [exchange(m, 0, i + 1) for i, m in enumerate(answer_y)]
    (near_answer,) = call(
        partial(gather_kernel, [(0, 0), (1, 0)]),
        [((4 * GROUP, WIDE), F32)],
        [],
        slope, recv_a, recv_b,
    )
    answer_a, answer_b = call(
        partial(reply_kernel, nyc),
        [((2 * nyc * GROUP, WIDE), F32)] * 2,
        [],
        near_answer, *back_y,
    )
    back_a, back_b = exchange(answer_a, 1, 0), exchange(answer_b, 2, 0)
    (stay_value,) = call(stay_gather_kernel, [((2, cells), F32)], [], slope, fields)
    (pull,) = call(
        partial(unpack_kernel, nyc),
        [((2, cells), F32)],
        [vmem(4 * groups * GROUP, WIDE)],
        back_a, back_b, *back_y, stay_value, slot, power,
    )
    return final_warmth, pull


def solution(mesh):
    cell = P(("gx", "gy"))
    tile = P(None, "gx", "gy")
    return jax.shard_map(
        shards,
        mesh=mesh,
        in_specs=(cell, cell, cell, cell, cell, tile, P()),
        out_specs=(tile, P(None, ("gx", "gy"))),
        check_vma=False,
    )
```

```python
import functools

import jax
import jax.numpy as jnp
from jax import lax
from jax.experimental import pallas as pl
from jax.experimental.pallas import tpu as pltpu
from jax.sharding import PartitionSpec as P

ITERS = 4
CAP = 2048
SINK_RATE = 0.5
LOW_BOUND = 0.5
HIGH_BOUND = 33.0

WIDE = 256
GROUP = CAP // WIDE
HALO = 8
F32, BF16 = jnp.float32, jnp.bfloat16


def partner(place, kind, count):
    if kind == 0:
        return place
    if kind == 1:
        return place ^ 1
    other = place - 1 if place % 2 == 0 else place + 1
    return other if 0 <= other < count else None


def exchange(value, x_kind, y_kind):
    nx, ny = lax.axis_size("gx"), lax.axis_size("gy")
    pairs = []
    for a in range(nx):
        for b in range(ny):
            x, y = partner(a, x_kind, nx), partner(b, y_kind, ny)
            if x is None:
                x, y = a, b ^ 1
            elif y is None:
                x, y = a ^ 1, b
            pairs.append((a * ny + b, x * ny + y))
    return lax.ppermute(value, ("gx", "gy"), pairs)


def pieces(value):
    high = value.astype(BF16).astype(F32)
    return high, value - high


def row_iota(count, width=128):
    return lax.broadcasted_iota(jnp.int32, (count, width), 0).astype(F32)


def onehot(row, count):
    return jnp.where(
        row_iota(count, row.shape[1]).astype(BF16) == row.astype(BF16),
        jnp.ones((), BF16),
        jnp.zeros((), BF16),
    )


def lanes(parts):
    return jnp.concatenate(parts, axis=1) if len(parts) > 1 else parts[0]


def transposed_dot(left, right):
    return lax.dot_general(left, right, (((1,), (1,)), ((), ())), preferred_element_type=F32)


def dot(left, right):
    return lax.dot_general(left, right, (((1,), (0,)), ((), ())), preferred_element_type=F32)


def kind_of(step, place):
    ahead = 1 - 2 * lax.rem(place, 2)
    return jnp.where(step == 0, 0, jnp.where(step == ahead, 1, 2))


def pack_kernel(
    nyc, cols, rows,
    bin_hbm, layer_hbm, off_hbm, power_hbm, spill_hbm, cond_hbm,
    msga_ref, msgb_ref, owny_ref, slot_ref, field_ref, power_ref,
    bin_ref, layer_ref, off_ref, spill_ref, edge_ref, sems, acc_ref,
):
    a, b = lax.axis_index("gx"), lax.axis_index("gy")
    copies = [
        pltpu.make_async_copy(src, dst, sems.at[i])
        for i, (src, dst) in enumerate(
            [
                (off_hbm, off_ref), (bin_hbm, bin_ref), (layer_hbm, layer_ref),
                (power_hbm, power_ref), (spill_hbm, spill_ref),
                (cond_hbm.at[:, :HALO, :], edge_ref.at[0]),
                (cond_hbm.at[:, cols - HALO :, :], edge_ref.at[1]),
            ]
        )
    ]
    for copy in copies:
        copy.start()
    acc_ref[...] = jnp.zeros_like(acc_ref)
    groups = 3 * nyc - 1
    table = groups * GROUP
    copies[0].wait()
    off = off_ref[...]
    col_code = (off >= 3).astype(jnp.int32) + (off >= 6).astype(jnp.int32)
    x_kind = kind_of(col_code - 1, a)
    y_kind = kind_of(off - 3 * col_code - 1, b)
    group = jnp.where(x_kind > 0, (x_kind - 1) * nyc + y_kind, 2 * nyc - 1 + y_kind)
    group = jnp.where(off == 4, -1, group)
    size = off.shape[0]
    r_i = lax.broadcasted_iota(jnp.int32, (size, size), 0)
    c_i = lax.broadcasted_iota(jnp.int32, (size, size), 1)
    upper = jnp.where(r_i < c_i, 1.0, 0.0).astype(BF16)
    lower = jnp.where(r_i > c_i, 1.0, 0.0).astype(BF16)
    ones = jnp.ones((size, size), BF16)
    slot = jnp.full(off.shape, -1.0, F32)
    for g in range(groups):
        mine = group == g
        mask = jnp.where(mine, 1.0, 0.0).astype(BF16)
        totals = dot(mask, ones).astype(BF16)
        rank = dot(mask, upper) + dot(lower, totals)
        slot = jnp.where(mine, rank + float(g * CAP), slot)
    slot_ref[...] = slot
    for copy in copies[1:]:
        copy.wait()
    code = layer_ref[...] * (cols * rows) + bin_ref[...]
    field_ref[0] = (code // rows).astype(F32)
    field_ref[1] = (code % rows).astype(F32)
    power = power_ref[...]
    spill = spill_ref[...]
    field_ref[2], field_ref[3] = pieces(power * (1.0 - spill))
    field_ref[4], field_ref[5] = pieces(power * spill)
    step = 32

    def body(j, carry):
        base = pl.multiple_of(j * step, step)
        slots = slot_ref[pl.ds(base, step), :]
        qs = jnp.floor(slots * (1.0 / WIDE))
        lams = slots - qs * WIDE
        vals = [field_ref[f, pl.ds(base, step), :] for f in range(6)]
        picks, marks = [], []
        for i in range(step):
            hit = row_iota(table) == qs[i : i + 1]
            picks.append(
                jnp.concatenate([jnp.where(hit, v[i : i + 1], 0.0) for v in vals], axis=0).astype(BF16)
            )
            marks.append(onehot(lams[i : i + 1], WIDE))
        acc_ref[...] += transposed_dot(lanes(picks), lanes(marks))
        return carry

    lax.fori_loop(0, size // step, body, 0)
    out = [acc_ref[f * table : (f + 1) * table, :] for f in range(6)]
    sent = [out[0] * float(rows) + out[1], out[2] + out[3], out[4] + out[5]]

    def put(ref, at, g):
        for f in range(3):
            ref[(at * 3 + f) * GROUP : (at * 3 + f + 1) * GROUP, :] = sent[f][
                g * GROUP : (g + 1) * GROUP
            ]

    for y in range(nyc):
        put(msga_ref, y, y)
        put(msgb_ref, y, nyc + y)
        if y:
            put(owny_ref, y - 1, 2 * nyc + y - 1)
    first, last = edge_ref[0], edge_ref[1]
    even = lax.rem(a, 2) == 0
    top = nyc * 3 * GROUP
    flat = (-1, rows)
    msga_ref[top:, :] = jnp.where(even, last, first).reshape(flat)
    msgb_ref[top:, :] = jnp.where(even, first, last).reshape(flat)


def deposit_block(lc, r, main, spill, cols, cells):
    picks, marks = [], []
    zero = jnp.zeros((), BF16)
    narrow = lambda x: x.astype(BF16)
    for lc_i, r_i, (mh, ml), (sh, sl) in zip(lc, r, main, spill):
        spot = narrow(row_iota(cells, lc_i.shape[1]))
        other = jnp.where(lc_i >= float(cells - cols), lc_i - cols, lc_i + cols)
        here, there = spot == narrow(lc_i), spot == narrow(other)
        high = jnp.where(here, narrow(mh), jnp.where(there, narrow(sh), zero))
        low = jnp.where(here, narrow(ml), jnp.where(there, narrow(sl), zero))
        picks.append(jnp.concatenate([high, low], axis=0))
        marks.append(onehot(r_i, WIDE))
    return transposed_dot(lanes(picks), lanes(marks))


def deposit_stays(grid_ref, field_ref, slot_ref, first, last, cols):
    count, step = grid_ref.shape[0] // 2, 32
    stays = slot_ref[first:last, :] < 0.0
    vals = [jnp.where(stays, field_ref[2 + f, first:last, :], 0.0) for f in range(4)]
    lcs, rs = field_ref[0, first:last, :], field_ref[1, first:last, :]
    for base in range(0, last - first, step):
        rows_of = lambda x: [x[base + i : base + i + 1] for i in range(step)]
        parts = [rows_of(v) for v in vals]
        grid_ref[...] += deposit_block(
            rows_of(lcs), rows_of(rs), list(zip(parts[0], parts[1])),
            list(zip(parts[2], parts[3])), cols, count,
        )


def stay_deposit_kernel(cols, split, field_ref, slot_ref, grid_ref):
    grid_ref[...] = jnp.zeros_like(grid_ref)
    deposit_stays(grid_ref, field_ref, slot_ref, 0, split, cols)


def deposit_groups(grid_ref, sources, cols):
    count, rows = grid_ref.shape[0] // 2, grid_ref.shape[1]
    lc, r, main, spill = [], [], [], []
    for ref, at in sources:
        for row in range(at, at + GROUP):
            code = ref[row : row + 1, :]
            lc_i = jnp.floor(code * (1.0 / rows))
            lc.append(lc_i)
            r.append(code - lc_i * rows)
            main.append(pieces(ref[row + GROUP : row + GROUP + 1, :]))
            spill.append(pieces(ref[row + 2 * GROUP : row + 2 * GROUP + 1, :]))
    grid_ref[...] += deposit_block(lc, r, main, spill, cols, count)


def near_deposit_kernel(cols, split, stay_ref, recva_ref, recvb_ref, field_ref, slot_ref, grid_ref):
    grid_ref[...] = stay_ref[...]
    deposit_stays(grid_ref, field_ref, slot_ref, split, slot_ref.shape[0], cols)
    deposit_groups(grid_ref, [(recva_ref, 0), (recvb_ref, 0)], cols)


def far_deposit_kernel(cols, nyc, *refs):
    near_ref, recvy = refs[0], refs[1:nyc]
    grid_ref, edgea_ref, edgeb_ref, acc_ref = refs[nyc:]
    acc_ref[...] = near_ref[...]
    sources = [(ref, 3 * GROUP * i) for ref in recvy for i in range(3)]
    deposit_groups(acc_ref, sources, cols)
    count = acc_ref.shape[0] // 2
    grid = (acc_ref[:count, :] + acc_ref[count:, :]).reshape(grid_ref.shape)
    grid_ref[...] = grid
    first, last = grid[:, :HALO, :], grid[:, cols - HALO :, :]
    even = lax.rem(lax.axis_index("gx"), 2) == 0
    edgea_ref[...] = jnp.where(even, last, first)
    edgeb_ref[...] = jnp.where(even, first, last)


def with_columns(own, from_a, from_b):
    a = lax.axis_index("gx")
    even = lax.rem(a, 2) == 0
    right = jnp.where(even, from_a, from_b)
    left = jnp.where(even, from_b, from_a)
    right = jnp.where(a < lax.axis_size("gx") - 1, right, 0.0)
    left = jnp.where(a > 0, left, 0.0)
    return jnp.concatenate([left, own, right], axis=1)


def row_edge(wide, last):
    rows = wide.shape[1]
    tile = jnp.where(last, wide[:, rows - 128 :], wide[:, :128]).T
    return jnp.where(last, tile[128 - HALO :], tile[:HALO])


def put_edges(ref, at, edge):
    extra = edge.shape[1] - WIDE
    ref[at : at + HALO, :] = edge[:, :WIDE]
    ref[at + HALO : at + 2 * HALO, :] = jnp.concatenate(
        [edge[:, WIDE:], jnp.zeros((HALO, WIDE - extra), F32)], axis=1
    )


def get_edges(ref, at, count):
    return jnp.concatenate(
        [ref[at : at + HALO, :], ref[at + HALO : at + 2 * HALO, : count - WIDE]], axis=1
    )


def y_edges(refs, at, wide):
    even = lax.rem(lax.axis_index("gy"), 2) == 0
    for kind, ref in enumerate(refs):
        put_edges(ref, at, row_edge(wide, even if kind == 0 else jnp.logical_not(even)))


def halo_of(ref, cols, layers, top):
    return ref[top:, :].reshape(layers, HALO, ref.shape[1])


def forward_kernel(nyc, recva_ref, recvb_ref, owny_ref, cond_ref, after_ref, *msgy_refs):
    layers, cols, rows = cond_ref.shape
    size, top = 3 * GROUP, nyc * 3 * GROUP
    for y, ref in enumerate(msgy_refs):
        ref[:size, :] = owny_ref[y * size : (y + 1) * size, :]
        ref[size : 2 * size, :] = recva_ref[(y + 1) * size : (y + 2) * size, :]
        ref[2 * size : 3 * size, :] = recvb_ref[(y + 1) * size : (y + 2) * size, :]
    wide = with_columns(
        cond_ref[...], halo_of(recva_ref, cols, layers, top), halo_of(recvb_ref, cols, layers, top)
    )
    y_edges(msgy_refs, 3 * size, wide.reshape(-1, rows))


def power_edge_kernel(grid_ref, froma_ref, fromb_ref, *edge_refs):
    wide = with_columns(grid_ref[...], froma_ref[...], fromb_ref[...])
    y_edges(edge_refs, 0, wide.reshape(-1, grid_ref.shape[2]))


def with_rows(wide, edges):
    b, ny = lax.axis_index("gy"), lax.axis_size("gy")
    layers, span, rows = wide.shape
    count = layers * span
    even = lax.rem(b, 2) == 0
    one = edges[0]
    two = edges[1] if len(edges) > 1 else jnp.zeros_like(one)
    after = jnp.where(b < ny - 1, jnp.where(even, one, two), 0.0)
    before = jnp.where(b > 0, jnp.where(even, two, one), 0.0)
    tile = jnp.concatenate([after, jnp.zeros((128 - 2 * HALO, count), F32), before], axis=0).T
    return jnp.concatenate([wide, tile.reshape(layers, span, 128)], axis=2)


def shifts(span, wide_rows):
    return (
        lambda x: pltpu.roll(x, span - 1, 0),
        lambda x: pltpu.roll(x, 1, 0),
        lambda x: pltpu.roll(x, wide_rows - 1, 1),
        lambda x: pltpu.roll(x, 1, 1),
    )


def face_kernel(nyc, cond_ref, recva_ref, recvb_ref, coupling_ref, *refs):
    recvy_refs, (fc_ref, fr_ref, fl_ref, e_ref, k_ref) = refs[: nyc - 1], refs[nyc - 1 :]
    layers, cols, rows = cond_ref.shape
    span, wide_rows = cols + 2 * HALO, rows + 128
    count = layers * span
    top = nyc * 3 * GROUP
    a, b = lax.axis_index("gx"), lax.axis_index("gy")
    nx, ny = lax.axis_size("gx"), lax.axis_size("gy")
    k_ref[...] = with_rows(
        with_columns(
            cond_ref[...],
            halo_of(recva_ref, cols, layers, top),
            halo_of(recvb_ref, cols, layers, top),
        ),
        [get_edges(ref, 9 * GROUP, count) for ref in recvy_refs],
    )
    shape = (span, wide_rows)
    c_i = lax.broadcasted_iota(jnp.int32, shape, 0)
    r_i = lax.broadcasted_iota(jnp.int32, shape, 1)
    c_low = jnp.where(a > 0, 0, HALO)
    c_high = jnp.where(a < nx - 1, span, span - HALO)
    r_high = jnp.where(b < ny - 1, rows + HALO, rows)
    r_low = jnp.where(b > 0, wide_rows - HALO, wide_rows)
    inside = jnp.where((c_i >= c_low) & (c_i < c_high) & ((r_i < r_high) | (r_i >= r_low)), 1.0, 0.0)
    next_c, prev_c, next_r, prev_r = shifts(span, wide_rows)
    both_c, both_r = inside * next_c(inside), inside * next_r(inside)
    for l in range(layers):
        k = k_ref[l]
        face_c, face_r = 0.5 * (k + next_c(k)), 0.5 * (k + next_r(k))
        kept_c, kept_r = face_c * both_c, face_r * both_r
        fc_ref[l], fr_ref[l] = kept_c, kept_r
        lost_c, lost_r = face_c - kept_c, face_r - kept_r
        e_ref[l] = SINK_RATE + ((lost_c + prev_c(lost_c)) + (lost_r + prev_r(lost_r)))
        if l + 1 < layers:
            fl_ref[l] = coupling_ref[l] * (0.5 * (k + k_ref[l + 1])) * inside


def solve_kernel(nyc, grid_ref, froma_ref, fromb_ref, fc_ref, fr_ref, fl_ref, e_ref, *refs):
    edge_refs, (warmth_ref, slope_ref, p_ref, v_ref, u_ref) = refs[: nyc - 1], refs[nyc - 1 :]
    layers, cols, rows = grid_ref.shape
    span, wide_rows = cols + 2 * HALO, rows + 128
    p_ref[...] = with_rows(
        with_columns(grid_ref[...], froma_ref[...], fromb_ref[...]),
        [get_edges(ref, 0, layers * span) for ref in edge_refs],
    )
    next_c, prev_c, next_r, prev_r = shifts(span, wide_rows)
    middle = 0.5 * (HIGH_BOUND + LOW_BOUND)
    spread = 0.5 * (HIGH_BOUND - LOW_BOUND)
    sigma = middle / spread
    now = 1.0 / sigma
    for l in range(layers):
        start = p_ref[l] / middle
        v_ref[0, l] = start
        u_ref[l] = start
    for sweep in range(ITERS):
        later = 1.0 / (2.0 * sigma - now)
        keep, gain = later * now, 2.0 * later / spread
        old, new = sweep % 2, (sweep + 1) % 2
        below = None
        for l in range(layers):
            v = v_ref[old, l]
            flow_c = fc_ref[l] * (v - next_c(v))
            flow_r = fr_ref[l] * (v - next_r(v))
            result = e_ref[l] * v + (flow_c - prev_c(flow_c)) + (flow_r - prev_r(flow_r))
            if below is not None:
                result = result - below
            if l + 1 < layers:
                below = fl_ref[l] * (v - v_ref[old, l + 1])
                result = result + below
            advance = keep * u_ref[l] + gain * (p_ref[l] - result)
            u_ref[l] = advance
            v_ref[new, l] = v + advance
        now = later
    final = ITERS % 2
    cells = layers * cols
    for l in range(layers):
        v = v_ref[final, l]
        warmth_ref[l] = v[HALO : HALO + cols, :rows]
        for f, slope in enumerate((0.5 * (next_c(v) - prev_c(v)), 0.5 * (next_r(v) - prev_r(v)))):
            high, low = pieces(slope[HALO : HALO + cols, :rows])
            for part, piece in enumerate((high, low)):
                at = (part * 2 + f) * cells + l * cols
                slope_ref[at : at + cols, :] = piece.astype(BF16)


def gather_block(slope, lc, r):
    cells = slope.shape[0] // 4
    found = dot(slope, onehot(r, slope.shape[1]))
    here = row_iota(cells, lc.shape[1]) == lc
    return [
        jnp.sum(
            jnp.where(
                here,
                found[f * cells : (f + 1) * cells] + found[(2 + f) * cells : (3 + f) * cells],
                0.0,
            ),
            axis=0,
            keepdims=True,
        )
        for f in range(2)
    ]


def gather_kernel(sources, slope_ref, *refs):
    ins, out_ref = refs[:-1], refs[-1]
    rows = slope_ref.shape[1]
    for g, (which, at) in enumerate(sources):
        for t in range(GROUP):
            code = ins[which][at + t : at + t + 1, :]
            lc = jnp.floor(code * (1.0 / rows))
            for f, value in enumerate(gather_block(slope_ref[...], lc, code - lc * rows)):
                row = (g * 2 + f) * GROUP + t
                out_ref[row : row + 1, :] = value


def stay_gather_kernel(slope_ref, field_ref, out_ref):
    step = 32

    def body(j, carry):
        base = pl.multiple_of(j * step, step)
        lcs, rs = field_ref[0, pl.ds(base, step), :], field_ref[1, pl.ds(base, step), :]
        for i in range(0, step, 4):
            many = lambda x: lanes([x[i + k : i + k + 1] for k in range(4)])
            at = pl.multiple_of(base * 128 + i * 128, 512)
            for f, value in enumerate(gather_block(slope_ref[...], many(lcs), many(rs))):
                out_ref[f : f + 1, pl.ds(at, 512)] = value
        return carry

    lax.fori_loop(0, field_ref.shape[1] // step, body, 0)


def reply_kernel(nyc, near_ref, *refs):
    size = 2 * GROUP
    backs, (a_ref, b_ref) = refs[: nyc - 1], refs[nyc - 1 :]
    a_ref[:size, :] = near_ref[:size, :]
    b_ref[:size, :] = near_ref[size:, :]
    for y, ref in enumerate(backs):
        a_ref[(y + 1) * size : (y + 2) * size, :] = ref[size : 2 * size, :]
        b_ref[(y + 1) * size : (y + 2) * size, :] = ref[2 * size : 3 * size, :]


def unpack_kernel(nyc, backa_ref, backb_ref, *refs):
    backy, (stay_ref, slot_ref, power_ref, out_ref, table_ref) = refs[: nyc - 1], refs[nyc - 1 :]
    groups = [(backa_ref, y) for y in range(nyc)] + [(backb_ref, y) for y in range(nyc)]
    groups += [(ref, 0) for ref in backy]
    table = len(groups) * GROUP
    for f in range(2):
        whole = jnp.concatenate(
            [ref[(2 * at + f) * GROUP : (2 * at + f + 1) * GROUP, :] for ref, at in groups], axis=0
        )
        for part, piece in enumerate(pieces(whole)):
            at = (part * 2 + f) * table
            table_ref[at : at + table, :] = piece
    source = table_ref[...].astype(BF16)
    step = 32

    def body(j, carry):
        base = pl.multiple_of(j * step, step)
        slots = slot_ref[pl.ds(base, step), :]
        qs = jnp.floor(slots * (1.0 / WIDE))
        lams = slots - qs * WIDE
        powers = power_ref[pl.ds(base, step), :]
        for i in range(0, step, 8):
            many = lambda x: lanes([x[i + k : i + k + 1] for k in range(8)])
            at = pl.multiple_of(base * 128 + i * 128, 1024)
            mark = onehot(many(lams), WIDE)
            found = dot(source, mark)
            place = many(qs)
            here = row_iota(table, 1024) == place
            for f in range(2):
                both = found[f * table : (f + 1) * table] + found[(2 + f) * table : (3 + f) * table]
                value = jnp.sum(jnp.where(here, both, 0.0), axis=0, keepdims=True)
                value = jnp.where(place >= 0.0, value, stay_ref[f : f + 1, pl.ds(at, 1024)])
                out_ref[f : f + 1, pl.ds(at, 1024)] = -many(powers) * value
        return carry

    lax.fori_loop(0, slot_ref.shape[0] // step, body, 0)


def call(kernel, outs, scratch, *args, spaces={}):
    space = pl.BlockSpec(memory_space=pltpu.VMEM)
    specs = [pl.BlockSpec(memory_space=spaces.get(i, pltpu.VMEM)) for i in range(len(args))]
    shapes = [jax.ShapeDtypeStruct(shape, dtype) for shape, dtype in outs]
    return pl.pallas_call(
        kernel,
        out_shape=shapes,
        in_specs=specs,
        out_specs=[space] * len(shapes),
        scratch_shapes=scratch,
        compiler_params=pltpu.CompilerParams(vmem_limit_bytes=48 * 1024 * 1024),
    )(*args)


def shards(
    cell_bin, cell_layer, cell_offset, cell_power, spill_weight, conductivity, layer_coupling
):
    layers, cols, rows = conductivity.shape
    cells = cell_bin.shape[0]
    nyc = 2 if lax.axis_size("gy") == 2 else 3
    count = layers * cols
    groups = 3 * nyc - 1
    flat = lambda x: x.reshape(cells // 128, 128)
    bins, layer, off = flat(cell_bin), flat(cell_layer), flat(cell_offset)
    power, spill = flat(cell_power), flat(spill_weight)
    square = bins.shape
    split = square[0] * 3 // 4
    own = 3 * GROUP
    message = (nyc * own + layers * HALO, WIDE)
    vmem = lambda *shape: pltpu.VMEM(shape, F32)
    partial = functools.partial

    tile = conductivity.shape
    msg_a, msg_b, own_y, slot, fields, power = call(
        partial(pack_kernel, nyc, cols, rows),
        [
            (message, F32), (message, F32), (((nyc - 1) * own, WIDE), F32),
            (square, F32), ((6, *square), F32), (square, F32),
        ],
        [pltpu.VMEM(square, jnp.int32)] * 3
        + [
            vmem(*square), vmem(2, layers, HALO, rows), pltpu.SemaphoreType.DMA((7,)),
            vmem(6 * groups * GROUP, WIDE),
        ],
        *[
            pltpu.with_memory_space_constraint(x, pltpu.HBM)
            for x in (bins, layer, off, power, spill, conductivity)
        ],
        spaces={i: pltpu.HBM for i in range(6)},
    )
    recv_a, recv_b = exchange(msg_a, 1, 0), exchange(msg_b, 2, 0)
    (stay_grid,) = call(
        partial(stay_deposit_kernel, cols, split),
        [((2 * count, rows), F32)],
        [],
        fields, slot,
    )
    msg_y = call(
        partial(forward_kernel, nyc),
        [((3 * own + 2 * HALO, WIDE), F32)] * (nyc - 1),
        [],
        recv_a, recv_b, own_y, conductivity, stay_grid,
        spaces={4: pl.ANY},
    )
    recv_y = [exchange(m, 0, i + 1) for i, m in enumerate(msg_y)]
    (near_grid,) = call(
        partial(near_deposit_kernel, cols, split),
        [((2 * count, rows), F32)],
        [],
        stay_grid, recv_a, recv_b, fields, slot,
    )
    edge = (layers, HALO, rows)
    grid, edge_a, edge_b = call(
        partial(far_deposit_kernel, cols, nyc),
        [(conductivity.shape, F32), (edge, F32), (edge, F32)],
        [vmem(2 * count, rows)],
        near_grid, *recv_y,
    )
    from_a, from_b = exchange(edge_a, 1, 0), exchange(edge_b, 2, 0)
    edges = call(
        power_edge_kernel, [((2 * HALO, WIDE), F32)] * (nyc - 1), [], grid, from_a, from_b
    )
    from_y = [exchange(e, 0, i + 1) for i, e in enumerate(edges)]
    big = (layers, cols + 2 * HALO, rows + 128)
    faces = call(
        partial(face_kernel, nyc),
        [(big, F32)] * 4,
        [vmem(*big)],
        conductivity, recv_a, recv_b, layer_coupling, *recv_y,
        spaces={3: pltpu.SMEM},
    )
    final_warmth, slope = call(
        partial(solve_kernel, nyc),
        [(tile, F32), ((4 * count, rows), BF16)],
        [vmem(*big), vmem(2, *big), vmem(*big)],
        grid, from_a, from_b, *faces, *from_y,
    )
    answer_y = [
        call(
            partial(gather_kernel, [(0, own * i) for i in range(3)]),
            [((6 * GROUP, WIDE), F32)],
            [],
            slope, r,
        )[0]
        for r in recv_y
    ]
    back_y = [exchange(m, 0, i + 1) for i, m in enumerate(answer_y)]
    (near_answer,) = call(
        partial(gather_kernel, [(0, 0), (1, 0)]),
        [((4 * GROUP, WIDE), F32)],
        [],
        slope, recv_a, recv_b,
    )
    answer_a, answer_b = call(
        partial(reply_kernel, nyc),
        [((2 * nyc * GROUP, WIDE), F32)] * 2,
        [],
        near_answer, *back_y,
    )
    back_a, back_b = exchange(answer_a, 1, 0), exchange(answer_b, 2, 0)
    (stay_value,) = call(stay_gather_kernel, [((2, cells), F32)], [], slope, fields)
    (pull,) = call(
        partial(unpack_kernel, nyc),
        [((2, cells), F32)],
        [vmem(4 * groups * GROUP, WIDE)],
        back_a, back_b, *back_y, stay_value, slot, power,
    )
    return final_warmth, pull


def solution(mesh):
    cell = P(("gx", "gy"))
    tile = P(None, "gx", "gy")
    return jax.shard_map(
        shards,
        mesh=mesh,
        in_specs=(cell, cell, cell, cell, cell, tile, P()),
        out_specs=(tile, P(None, ("gx", "gy"))),
        check_vma=False,
    )
```

```python
import functools

import jax
import jax.numpy as jnp
from jax import lax
from jax.experimental import pallas as pl
from jax.experimental.pallas import tpu as pltpu
from jax.sharding import PartitionSpec as P

ITERS = 4
CAP = 2048
SINK_RATE = 0.5
LOW_BOUND = 0.5
HIGH_BOUND = 33.0

WIDE = 256
GROUP = CAP // WIDE
BLOCK = 32
HALO = 8
F32, BF16 = jnp.float32, jnp.bfloat16


def partner(place, kind, count):
    if kind == 0:
        return place
    if kind == 1:
        return place ^ 1
    other = place - 1 if place % 2 == 0 else place + 1
    return other if 0 <= other < count else None


def exchange(value, x_kind, y_kind):
    nx, ny = lax.axis_size("gx"), lax.axis_size("gy")
    pairs = []
    for a in range(nx):
        for b in range(ny):
            x, y = partner(a, x_kind, nx), partner(b, y_kind, ny)
            if x is None:
                x, y = a, b ^ 1
            elif y is None:
                x, y = a ^ 1, b
            pairs.append((a * ny + b, x * ny + y))
    return lax.ppermute(value, ("gx", "gy"), pairs)


def pieces(value):
    high = value.astype(BF16).astype(F32)
    return high, value - high


def row_iota(count, width=128):
    return lax.broadcasted_iota(jnp.int32, (count, width), 0).astype(F32)


def onehot(row, count):
    return jnp.where(
        row_iota(count, row.shape[1]).astype(BF16) == row.astype(BF16),
        jnp.ones((), BF16),
        jnp.zeros((), BF16),
    )


def lanes(parts):
    return jnp.concatenate(parts, axis=1) if len(parts) > 1 else parts[0]


def transposed_dot(left, right):
    return lax.dot_general(left, right, (((1,), (1,)), ((), ())), preferred_element_type=F32)


def dot(left, right):
    return lax.dot_general(left, right, (((1,), (0,)), ((), ())), preferred_element_type=F32)


def kind_of(step, place):
    ahead = 1 - 2 * lax.rem(place, 2)
    return jnp.where(step == 0, 0, jnp.where(step == ahead, 1, 2))


def pack_kernel(
    nyc, cols, rows,
    bin_hbm, layer_hbm, off_hbm, power_hbm, spill_hbm, cond_hbm,
    msga_ref, msgb_ref, owny_ref, slot_ref, field_ref, power_ref,
    bin_ref, layer_ref, off_ref, spill_ref, edge_ref, sems, acc_ref,
):
    a, b = lax.axis_index("gx"), lax.axis_index("gy")
    copies = [
        pltpu.make_async_copy(src, dst, sems.at[i])
        for i, (src, dst) in enumerate(
            [
                (off_hbm, off_ref), (bin_hbm, bin_ref), (layer_hbm, layer_ref),
                (power_hbm, power_ref), (spill_hbm, spill_ref),
                (cond_hbm.at[:, :HALO, :], edge_ref.at[0]),
                (cond_hbm.at[:, cols - HALO :, :], edge_ref.at[1]),
            ]
        )
    ]
    for copy in copies:
        copy.start()
    acc_ref[...] = jnp.zeros_like(acc_ref)
    groups = 3 * nyc - 1
    table = groups * GROUP
    copies[0].wait()
    off = off_ref[...]
    col_code = (off >= 3).astype(jnp.int32) + (off >= 6).astype(jnp.int32)
    x_kind = kind_of(col_code - 1, a)
    y_kind = kind_of(off - 3 * col_code - 1, b)
    group = jnp.where(x_kind > 0, (x_kind - 1) * nyc + y_kind, 2 * nyc - 1 + y_kind)
    group = jnp.where(off == 4, -1, group)
    size = off.shape[0]
    r_i = lax.broadcasted_iota(jnp.int32, (size, size), 0)
    c_i = lax.broadcasted_iota(jnp.int32, (size, size), 1)
    upper = jnp.where(r_i < c_i, 1.0, 0.0).astype(BF16)
    lower = jnp.where(r_i > c_i, 1.0, 0.0).astype(BF16)
    ones = jnp.ones((size, size), BF16)
    slot = jnp.full(off.shape, -1.0, F32)
    for g in range(groups):
        mine = group == g
        mask = jnp.where(mine, 1.0, 0.0).astype(BF16)
        totals = dot(mask, ones).astype(BF16)
        rank = dot(mask, upper) + dot(lower, totals)
        slot = jnp.where(mine, rank + float(g * CAP), slot)
    slot_ref[...] = slot
    for copy in copies[1:]:
        copy.wait()
    code = layer_ref[...] * (cols * rows) + bin_ref[...]
    field_ref[0] = (code // rows).astype(F32)
    field_ref[1] = (code % rows).astype(F32)
    power = power_ref[...]
    spill = spill_ref[...]
    field_ref[2], field_ref[3] = pieces(power * (1.0 - spill))
    field_ref[4], field_ref[5] = pieces(power * spill)
    step = 32

    def body(j, carry):
        base = pl.multiple_of(j * step, step)
        slots = slot_ref[pl.ds(base, step), :]
        qs = jnp.floor(slots * (1.0 / WIDE))
        lams = slots - qs * WIDE
        vals = [field_ref[f, pl.ds(base, step), :] for f in range(6)]
        picks, marks = [], []
        for i in range(step):
            hit = row_iota(table) == qs[i : i + 1]
            picks.append(
                jnp.concatenate([jnp.where(hit, v[i : i + 1], 0.0) for v in vals], axis=0).astype(BF16)
            )
            marks.append(onehot(lams[i : i + 1], WIDE))
        acc_ref[...] += transposed_dot(lanes(picks), lanes(marks))
        return carry

    lax.fori_loop(0, size // step, body, 0)
    out = [acc_ref[f * table : (f + 1) * table, :] for f in range(6)]
    sent = [out[0] * float(rows) + out[1], out[2] + out[3], out[4] + out[5]]

    def put(ref, at, g):
        for f in range(3):
            ref[(at * 3 + f) * GROUP : (at * 3 + f + 1) * GROUP, :] = sent[f][
                g * GROUP : (g + 1) * GROUP
            ]

    for y in range(nyc):
        put(msga_ref, y, y)
        put(msgb_ref, y, nyc + y)
        if y:
            put(owny_ref, y - 1, 2 * nyc + y - 1)
    first, last = edge_ref[0], edge_ref[1]
    even = lax.rem(a, 2) == 0
    top = nyc * 3 * GROUP
    flat = (-1, rows)
    msga_ref[top:, :] = jnp.where(even, last, first).reshape(flat)
    msgb_ref[top:, :] = jnp.where(even, first, last).reshape(flat)


def deposit_block(lc, r, main, spill, cols, cells):
    picks, marks = [], []
    zero = jnp.zeros((), BF16)
    narrow = lambda x: x.astype(BF16)
    for lc_i, r_i, (mh, ml), (sh, sl) in zip(lc, r, main, spill):
        spot = narrow(row_iota(cells, lc_i.shape[1]))
        other = jnp.where(lc_i >= float(cells - cols), lc_i - cols, lc_i + cols)
        here, there = spot == narrow(lc_i), spot == narrow(other)
        high = jnp.where(here, narrow(mh), jnp.where(there, narrow(sh), zero))
        low = jnp.where(here, narrow(ml), jnp.where(there, narrow(sl), zero))
        picks.append(jnp.concatenate([high, low], axis=0))
        marks.append(onehot(r_i, WIDE))
    return transposed_dot(lanes(picks), lanes(marks))


def deposit_stays(grid_ref, field_ref, slot_ref, first, last, cols):
    count, step = grid_ref.shape[0] // 2, 32
    stays = slot_ref[first:last, :] < 0.0
    vals = [jnp.where(stays, field_ref[2 + f, first:last, :], 0.0) for f in range(4)]
    lcs, rs = field_ref[0, first:last, :], field_ref[1, first:last, :]
    for base in range(0, last - first, step):
        rows_of = lambda x: [x[base + i : base + i + 1] for i in range(step)]
        parts = [rows_of(v) for v in vals]
        grid_ref[...] += deposit_block(
            rows_of(lcs), rows_of(rs), list(zip(parts[0], parts[1])),
            list(zip(parts[2], parts[3])), cols, count,
        )


def stay_deposit_kernel(cols, split, field_ref, slot_ref, grid_ref):
    grid_ref[...] = jnp.zeros_like(grid_ref)
    deposit_stays(grid_ref, field_ref, slot_ref, 0, split, cols)


def deposit_groups(grid_ref, sources, cols):
    count, rows = grid_ref.shape[0] // 2, grid_ref.shape[1]
    lc, r, main, spill = [], [], [], []
    for ref, at in sources:
        for row in range(at, at + GROUP):
            code = ref[row : row + 1, :]
            lc_i = jnp.floor(code * (1.0 / rows))
            lc.append(lc_i)
            r.append(code - lc_i * rows)
            main.append(pieces(ref[row + GROUP : row + GROUP + 1, :]))
            spill.append(pieces(ref[row + 2 * GROUP : row + 2 * GROUP + 1, :]))
    grid_ref[...] += deposit_block(lc, r, main, spill, cols, count)


def near_deposit_kernel(cols, split, stay_ref, recva_ref, recvb_ref, field_ref, slot_ref, grid_ref):
    grid_ref[...] = stay_ref[...]
    deposit_stays(grid_ref, field_ref, slot_ref, split, slot_ref.shape[0], cols)
    deposit_groups(grid_ref, [(recva_ref, 0), (recvb_ref, 0)], cols)


def far_deposit_kernel(cols, nyc, *refs):
    near_ref, recvy = refs[0], refs[1:nyc]
    grid_ref, edgea_ref, edgeb_ref, acc_ref = refs[nyc:]
    acc_ref[...] = near_ref[...]
    sources = [(ref, 3 * GROUP * i) for ref in recvy for i in range(3)]
    deposit_groups(acc_ref, sources, cols)
    count = acc_ref.shape[0] // 2
    grid = (acc_ref[:count, :] + acc_ref[count:, :]).reshape(grid_ref.shape)
    grid_ref[...] = grid
    first, last = grid[:, :HALO, :], grid[:, cols - HALO :, :]
    even = lax.rem(lax.axis_index("gx"), 2) == 0
    edgea_ref[...] = jnp.where(even, last, first)
    edgeb_ref[...] = jnp.where(even, first, last)


def with_columns(own, from_a, from_b):
    a = lax.axis_index("gx")
    even = lax.rem(a, 2) == 0
    right = jnp.where(even, from_a, from_b)
    left = jnp.where(even, from_b, from_a)
    right = jnp.where(a < lax.axis_size("gx") - 1, right, 0.0)
    left = jnp.where(a > 0, left, 0.0)
    return jnp.concatenate([left, own, right], axis=1)


def row_edge(wide, last):
    rows = wide.shape[1]
    tile = jnp.where(last, wide[:, rows - 128 :], wide[:, :128]).T
    return jnp.where(last, tile[128 - HALO :], tile[:HALO])


def put_edges(ref, at, edge):
    extra = edge.shape[1] - WIDE
    ref[at : at + HALO, :] = edge[:, :WIDE]
    ref[at + HALO : at + 2 * HALO, :] = jnp.concatenate(
        [edge[:, WIDE:], jnp.zeros((HALO, WIDE - extra), F32)], axis=1
    )


def get_edges(ref, at, count):
    return jnp.concatenate(
        [ref[at : at + HALO, :], ref[at + HALO : at + 2 * HALO, : count - WIDE]], axis=1
    )


def y_edges(refs, at, wide):
    even = lax.rem(lax.axis_index("gy"), 2) == 0
    for kind, ref in enumerate(refs):
        put_edges(ref, at, row_edge(wide, even if kind == 0 else jnp.logical_not(even)))


def halo_of(ref, cols, layers, top):
    return ref[top:, :].reshape(layers, HALO, ref.shape[1])


def forward_kernel(nyc, recva_ref, recvb_ref, owny_ref, cond_ref, after_ref, *msgy_refs):
    layers, cols, rows = cond_ref.shape
    size, top = 3 * GROUP, nyc * 3 * GROUP
    for y, ref in enumerate(msgy_refs):
        ref[:size, :] = owny_ref[y * size : (y + 1) * size, :]
        ref[size : 2 * size, :] = recva_ref[(y + 1) * size : (y + 2) * size, :]
        ref[2 * size : 3 * size, :] = recvb_ref[(y + 1) * size : (y + 2) * size, :]
    wide = with_columns(
        cond_ref[...], halo_of(recva_ref, cols, layers, top), halo_of(recvb_ref, cols, layers, top)
    )
    y_edges(msgy_refs, 3 * size, wide.reshape(-1, rows))


def power_edge_kernel(grid_ref, froma_ref, fromb_ref, after_ref, *edge_refs):
    wide = with_columns(grid_ref[...], froma_ref[...], fromb_ref[...])
    y_edges(edge_refs, 0, wide.reshape(-1, grid_ref.shape[2]))


def with_rows(wide, edges):
    b, ny = lax.axis_index("gy"), lax.axis_size("gy")
    layers, span, rows = wide.shape
    count = layers * span
    even = lax.rem(b, 2) == 0
    one = edges[0]
    two = edges[1] if len(edges) > 1 else jnp.zeros_like(one)
    after = jnp.where(b < ny - 1, jnp.where(even, one, two), 0.0)
    before = jnp.where(b > 0, jnp.where(even, two, one), 0.0)
    tile = jnp.concatenate([after, jnp.zeros((128 - 2 * HALO, count), F32), before], axis=0).T
    return jnp.concatenate([wide, tile.reshape(layers, span, 128)], axis=2)


def shifts(span, wide_rows):
    return (
        lambda x: pltpu.roll(x, span - 1, 0),
        lambda x: pltpu.roll(x, 1, 0),
        lambda x: pltpu.roll(x, wide_rows - 1, 1),
        lambda x: pltpu.roll(x, 1, 1),
    )


def face_kernel(nyc, cond_ref, recva_ref, recvb_ref, coupling_ref, *refs):
    recvy_refs, (fc_ref, fr_ref, fl_ref, e_ref, k_ref) = refs[: nyc - 1], refs[nyc - 1 :]
    layers, cols, rows = cond_ref.shape
    span, wide_rows = cols + 2 * HALO, rows + 128
    count = layers * span
    top = nyc * 3 * GROUP
    a, b = lax.axis_index("gx"), lax.axis_index("gy")
    nx, ny = lax.axis_size("gx"), lax.axis_size("gy")
    k_ref[...] = with_rows(
        with_columns(
            cond_ref[...],
            halo_of(recva_ref, cols, layers, top),
            halo_of(recvb_ref, cols, layers, top),
        ),
        [get_edges(ref, 9 * GROUP, count) for ref in recvy_refs],
    )
    shape = (span, wide_rows)
    c_i = lax.broadcasted_iota(jnp.int32, shape, 0)
    r_i = lax.broadcasted_iota(jnp.int32, shape, 1)
    c_low = jnp.where(a > 0, 0, HALO)
    c_high = jnp.where(a < nx - 1, span, span - HALO)
    r_high = jnp.where(b < ny - 1, rows + HALO, rows)
    r_low = jnp.where(b > 0, wide_rows - HALO, wide_rows)
    inside = jnp.where((c_i >= c_low) & (c_i < c_high) & ((r_i < r_high) | (r_i >= r_low)), 1.0, 0.0)
    next_c, prev_c, next_r, prev_r = shifts(span, wide_rows)
    both_c, both_r = inside * next_c(inside), inside * next_r(inside)
    for l in range(layers):
        k = k_ref[l]
        face_c, face_r = 0.5 * (k + next_c(k)), 0.5 * (k + next_r(k))
        kept_c, kept_r = face_c * both_c, face_r * both_r
        fc_ref[l], fr_ref[l] = kept_c, kept_r
        lost_c, lost_r = face_c - kept_c, face_r - kept_r
        e_ref[l] = SINK_RATE + ((lost_c + prev_c(lost_c)) + (lost_r + prev_r(lost_r)))
        if l + 1 < layers:
            fl_ref[l] = coupling_ref[l] * (0.5 * (k + k_ref[l + 1])) * inside


def solve_kernel(nyc, grid_ref, froma_ref, fromb_ref, fc_ref, fr_ref, fl_ref, e_ref, *refs):
    edge_refs, (warmth_ref, slope_ref, p_ref, v_ref, u_ref) = refs[: nyc - 1], refs[nyc - 1 :]
    layers, cols, rows = grid_ref.shape
    span, wide_rows = cols + 2 * HALO, rows + 128
    p_ref[...] = with_rows(
        with_columns(grid_ref[...], froma_ref[...], fromb_ref[...]),
        [get_edges(ref, 0, layers * span) for ref in edge_refs],
    )
    next_c, prev_c, next_r, prev_r = shifts(span, wide_rows)
    middle = 0.5 * (HIGH_BOUND + LOW_BOUND)
    spread = 0.5 * (HIGH_BOUND - LOW_BOUND)
    sigma = middle / spread
    now = 1.0 / sigma
    for l in range(layers):
        start = p_ref[l] * (1.0 / middle)
        v_ref[0, l] = start
        u_ref[l] = start
    for sweep in range(ITERS):
        later = 1.0 / (2.0 * sigma - now)
        keep, gain = later * now, 2.0 * later / spread
        old, new = sweep % 2, (sweep + 1) % 2
        below = None
        for l in range(layers):
            v = v_ref[old, l]
            flow_c = fc_ref[l] * (v - next_c(v))
            flow_r = fr_ref[l] * (v - next_r(v))
            result = e_ref[l] * v + (flow_c - prev_c(flow_c)) + (flow_r - prev_r(flow_r))
            if below is not None:
                result = result - below
            if l + 1 < layers:
                below = fl_ref[l] * (v - v_ref[old, l + 1])
                result = result + below
            advance = keep * u_ref[l] + gain * (p_ref[l] - result)
            u_ref[l] = advance
            v_ref[new, l] = v + advance
        now = later
    final = ITERS % 2
    for l in range(layers):
        v = v_ref[final, l]
        warmth_ref[l] = v[HALO : HALO + cols, :rows]
        for f, slope in enumerate((0.5 * (next_c(v) - prev_c(v)), 0.5 * (next_r(v) - prev_r(v)))):
            high, low = pieces(slope[HALO : HALO + cols, :rows])
            for part, piece in enumerate((high, low)):
                at = ((l * 2 + part) * 2 + f) * cols
                slope_ref[at : at + cols, :] = piece.astype(BF16)


def pick(found, lc, first):
    cols = found.shape[0] // 4
    here = row_iota(cols, lc.shape[1]) == lc - first
    return [
        jnp.where(here, found[f * cols : (f + 1) * cols] + found[(2 + f) * cols : (3 + f) * cols], 0.0)
        for f in range(2)
    ]


def gather_block(slope, lc, r, layers):
    size = slope.shape[0] // layers
    found = dot(slope, onehot(r, slope.shape[1]))
    parts = [pick(found[l * size : (l + 1) * size], lc, l * (size // 4)) for l in range(layers)]
    return [jnp.sum(sum(p[f] for p in parts), axis=0, keepdims=True) for f in range(2)]


def gather_kernel(layers, sources, slope_ref, *refs):
    ins, out_ref = refs[:-1], refs[-1]
    rows = slope_ref.shape[1]
    for g, (which, at) in enumerate(sources):
        for t in range(GROUP):
            code = ins[which][at + t : at + t + 1, :]
            lc = jnp.floor(code * (1.0 / rows))
            for f, value in enumerate(gather_block(slope_ref[...], lc, code - lc * rows, layers)):
                row = (g * 2 + f) * GROUP + t
                out_ref[row : row + 1, :] = value


def sort_kernel(layers, cols, table, field_ref, slot_ref, after_ref, order_ref, place_ref, unit_ref):
    size = slot_ref.shape[0]
    span = BLOCK * size // WIDE
    r_i = lax.broadcasted_iota(jnp.int32, (size, size), 0)
    c_i = lax.broadcasted_iota(jnp.int32, (size, size), 1)
    flag = lambda x: jnp.where(x, 1.0, 0.0).astype(BF16)
    upper, ones = flag(r_i < c_i), jnp.ones((size, size), BF16)
    same = (r_i // BLOCK) == (c_i // BLOCK)
    both = jnp.concatenate([flag(same & (r_i > c_i)), flag(same)], axis=1)
    layer = jnp.floor(field_ref[0] * (1.0 / cols))
    ahead = jnp.zeros((size, size), F32)
    rank = jnp.zeros((size, size), F32)
    lane = lax.broadcasted_iota(jnp.int32, (size, size), 1).astype(F32)
    passed = jnp.zeros((size, size), F32)
    for l in range(layers):
        mine = layer == float(l)
        mask = flag(mine)
        totals = dot(mask, ones)
        stack = jnp.concatenate([totals.astype(BF16), ahead.astype(BF16)], axis=0)
        rank = jnp.where(mine, dot(mask, upper) + dot(both, stack), rank)
        ahead = ahead + totals
        if l + 1 < layers:
            end = jnp.floor(dot(both[:, size:], ahead.astype(BF16)) * (1.0 / WIDE))
            passed = passed + jnp.where(jnp.minimum(end, span - 1.0) + l < lane, 1.0, 0.0)
    unit_ref[...] = ((lane - passed) * layers + passed).astype(jnp.int32)
    row = jnp.floor(rank * (1.0 / WIDE))
    lam = rank - row * WIDE
    slot = slot_ref[...]
    place_ref[...] = jnp.where(slot >= 0.0, slot, (row + layer + table) * WIDE + lam)
    for k in range(size // BLOCK):
        picks, marks = [], []
        for i in range(k * BLOCK, (k + 1) * BLOCK):
            hit = row_iota(span) == row[i : i + 1]
            picks.append(
                jnp.concatenate(
                    [jnp.where(hit, field_ref[f, i : i + 1, :], 0.0) for f in range(2)], axis=0
                ).astype(BF16)
            )
            marks.append(onehot(lam[i : i + 1], WIDE))
        sorted_rows = transposed_dot(lanes(picks), lanes(marks))
        for f in range(2):
            order_ref[f, k * span : (k + 1) * span, :] = sorted_rows[f * span : (f + 1) * span]


def units_of(layers, size):
    return BLOCK * size // WIDE + layers


def stay_gather_kernel(layers, slope_ref, order_ref, unit_ref, out_ref):
    blocks = unit_ref.shape[0] // BLOCK
    span = order_ref.shape[1] // blocks
    size = slope_ref.shape[0] // layers
    units = units_of(layers, unit_ref.shape[0])

    def body(k, carry):
        for u in range(units - 1):
            code = unit_ref[k * BLOCK, u]
            layer, at = lax.rem(code, layers), k * span + code // layers
            lc, r = order_ref[0, pl.ds(at, 1), :], order_ref[1, pl.ds(at, 1), :]
            rows = slope_ref[pl.ds(pl.multiple_of(layer * size, size), size), :]
            first = (layer * (size // 4)).astype(F32)
            for f, part in enumerate(pick(dot(rows, onehot(r, slope_ref.shape[1])), lc, first)):
                out_ref[k, f * units + u : f * units + u + 1, :] = jnp.sum(part, axis=0, keepdims=True)
        for f in range(2):
            out_ref[k, (f + 1) * units - 1 : (f + 1) * units, :] = jnp.zeros((1, WIDE), F32)
        return carry

    lax.fori_loop(0, blocks, body, 0)


def reply_kernel(nyc, near_ref, *refs):
    size = 2 * GROUP
    backs, (a_ref, b_ref) = refs[: nyc - 1], refs[nyc - 1 :]
    a_ref[:size, :] = near_ref[:size, :]
    b_ref[:size, :] = near_ref[size:, :]
    for y, ref in enumerate(backs):
        a_ref[(y + 1) * size : (y + 2) * size, :] = ref[size : 2 * size, :]
        b_ref[(y + 1) * size : (y + 2) * size, :] = ref[2 * size : 3 * size, :]


def unpack_kernel(nyc, backa_ref, backb_ref, *refs):
    backy, (stay_ref, place_ref, power_ref, out_ref, table_ref) = refs[: nyc - 1], refs[nyc - 1 :]
    groups = [(backa_ref, y) for y in range(nyc)] + [(backb_ref, y) for y in range(nyc)]
    groups += [(ref, 0) for ref in backy]
    sent, units = len(groups) * GROUP, stay_ref.shape[1] // 2
    table = sent + units
    for f in range(2):
        whole = jnp.concatenate(
            [ref[(2 * at + f) * GROUP : (2 * at + f + 1) * GROUP, :] for ref, at in groups], axis=0
        )
        for part, piece in enumerate(pieces(whole)):
            at = (part * 2 + f) * table
            table_ref[at : at + sent, :] = piece

    def body(k, carry):
        base = pl.multiple_of(k * BLOCK, BLOCK)
        for f in range(2):
            for part, piece in enumerate(pieces(stay_ref[k, f * units : (f + 1) * units, :])):
                at = (part * 2 + f) * table + sent
                table_ref[at : at + units, :] = piece
        source = table_ref[...].astype(BF16)
        places = place_ref[pl.ds(base, BLOCK), :]
        qs = jnp.floor(places * (1.0 / WIDE))
        lams = places - qs * WIDE
        powers = power_ref[pl.ds(base, BLOCK), :]
        for i in range(0, BLOCK, 8):
            many = lambda x: lanes([x[i + j : i + j + 1] for j in range(8)])
            at = pl.multiple_of(base * 128 + i * 128, 1024)
            found = dot(source, onehot(many(lams), WIDE))
            here = row_iota(table, 1024) == many(qs)
            for f in range(2):
                both = found[f * table : (f + 1) * table] + found[(2 + f) * table : (3 + f) * table]
                value = jnp.sum(jnp.where(here, both, 0.0), axis=0, keepdims=True)
                out_ref[f : f + 1, pl.ds(at, 1024)] = -many(powers) * value
        return carry

    lax.fori_loop(0, place_ref.shape[0] // BLOCK, body, 0)


def call(kernel, outs, scratch, *args, spaces={}):
    space = pl.BlockSpec(memory_space=pltpu.VMEM)
    specs = [pl.BlockSpec(memory_space=spaces.get(i, pltpu.VMEM)) for i in range(len(args))]
    shapes = [jax.ShapeDtypeStruct(shape, dtype) for shape, dtype in outs]
    return pl.pallas_call(
        kernel,
        out_shape=shapes,
        in_specs=specs,
        out_specs=[space] * len(shapes),
        scratch_shapes=scratch,
        compiler_params=pltpu.CompilerParams(vmem_limit_bytes=48 * 1024 * 1024),
    )(*args)


def shards(
    cell_bin, cell_layer, cell_offset, cell_power, spill_weight, conductivity, layer_coupling
):
    layers, cols, rows = conductivity.shape
    cells = cell_bin.shape[0]
    nyc = 2 if lax.axis_size("gy") == 2 else 3
    count = layers * cols
    groups = 3 * nyc - 1
    flat = lambda x: x.reshape(cells // 128, 128)
    bins, layer, off = flat(cell_bin), flat(cell_layer), flat(cell_offset)
    power, spill = flat(cell_power), flat(spill_weight)
    square = bins.shape
    split = square[0] * 3 // 4
    own = 3 * GROUP
    message = (nyc * own + layers * HALO, WIDE)
    vmem = lambda *shape: pltpu.VMEM(shape, F32)
    partial = functools.partial

    tile = conductivity.shape
    msg_a, msg_b, own_y, slot, fields, power = call(
        partial(pack_kernel, nyc, cols, rows),
        [
            (message, F32), (message, F32), (((nyc - 1) * own, WIDE), F32),
            (square, F32), ((6, *square), F32), (square, F32),
        ],
        [pltpu.VMEM(square, jnp.int32)] * 3
        + [
            vmem(*square), vmem(2, layers, HALO, rows), pltpu.SemaphoreType.DMA((7,)),
            vmem(6 * groups * GROUP, WIDE),
        ],
        *[
            pltpu.with_memory_space_constraint(x, pltpu.HBM)
            for x in (bins, layer, off, power, spill, conductivity)
        ],
        spaces={i: pltpu.HBM for i in range(6)},
    )
    recv_a, recv_b = exchange(msg_a, 1, 0), exchange(msg_b, 2, 0)
    (stay_grid,) = call(
        partial(stay_deposit_kernel, cols, split),
        [((2 * count, rows), F32)],
        [],
        fields, slot,
    )
    msg_y = call(
        partial(forward_kernel, nyc),
        [((3 * own + 2 * HALO, WIDE), F32)] * (nyc - 1),
        [],
        recv_a, recv_b, own_y, conductivity, stay_grid,
        spaces={4: pl.ANY},
    )
    recv_y = [exchange(m, 0, i + 1) for i, m in enumerate(msg_y)]
    (near_grid,) = call(
        partial(near_deposit_kernel, cols, split),
        [((2 * count, rows), F32)],
        [],
        stay_grid, recv_a, recv_b, fields, slot,
    )
    edge = (layers, HALO, rows)
    grid, edge_a, edge_b = call(
        partial(far_deposit_kernel, cols, nyc),
        [(conductivity.shape, F32), (edge, F32), (edge, F32)],
        [vmem(2 * count, rows)],
        near_grid, *recv_y,
    )
    from_a, from_b = exchange(edge_a, 1, 0), exchange(edge_b, 2, 0)
    table = groups * GROUP
    order, place, unit = call(
        partial(sort_kernel, layers, cols, table),
        [((2, cells // WIDE, WIDE), F32), (square, F32), (square, jnp.int32)],
        [],
        fields, slot, grid,
        spaces={2: pl.ANY},
    )
    edges = call(
        power_edge_kernel,
        [((2 * HALO, WIDE), F32)] * (nyc - 1),
        [],
        grid, from_a, from_b, order,
        spaces={3: pl.ANY},
    )
    from_y = [exchange(e, 0, i + 1) for i, e in enumerate(edges)]
    big = (layers, cols + 2 * HALO, rows + 128)
    faces = call(
        partial(face_kernel, nyc),
        [(big, F32)] * 4,
        [vmem(*big)],
        conductivity, recv_a, recv_b, layer_coupling, *recv_y,
        spaces={3: pltpu.SMEM},
    )
    final_warmth, slope = call(
        partial(solve_kernel, nyc),
        [(tile, F32), ((4 * count, rows), BF16)],
        [vmem(*big), vmem(2, *big), vmem(*big)],
        grid, from_a, from_b, *faces, *from_y,
    )
    answer_y = [
        call(
            partial(gather_kernel, layers, [(0, own * i) for i in range(3)]),
            [((6 * GROUP, WIDE), F32)],
            [],
            slope, r,
        )[0]
        for r in recv_y
    ]
    back_y = [exchange(m, 0, i + 1) for i, m in enumerate(answer_y)]
    (near_answer,) = call(
        partial(gather_kernel, layers, [(0, 0), (1, 0)]),
        [((4 * GROUP, WIDE), F32)],
        [],
        slope, recv_a, recv_b,
    )
    answer_a, answer_b = call(
        partial(reply_kernel, nyc),
        [((2 * nyc * GROUP, WIDE), F32)] * 2,
        [],
        near_answer, *back_y,
    )
    back_a, back_b = exchange(answer_a, 1, 0), exchange(answer_b, 2, 0)
    units = units_of(layers, square[0])
    (stay_value,) = call(
        partial(stay_gather_kernel, layers),
        [((square[0] // BLOCK, 2 * units, WIDE), F32)],
        [],
        slope, order, unit,
        spaces={2: pltpu.SMEM},
    )
    (pull,) = call(
        partial(unpack_kernel, nyc),
        [((2, cells), F32)],
        [vmem(4 * (table + units), WIDE)],
        back_a, back_b, *back_y, stay_value, place, power,
    )
    return final_warmth, pull


def solution(mesh):
    cell = P(("gx", "gy"))
    tile = P(None, "gx", "gy")
    return jax.shard_map(
        shards,
        mesh=mesh,
        in_specs=(cell, cell, cell, cell, cell, tile, P()),
        out_specs=(tile, P(None, ("gx", "gy"))),
        check_vma=False,
    )
```

```python
import functools

import jax
import jax.numpy as jnp
from jax import lax
from jax.experimental import pallas as pl
from jax.experimental.pallas import tpu as pltpu
from jax.sharding import PartitionSpec as P

ITERS = 4
CAP = 2048
SINK_RATE = 0.5
LOW_BOUND = 0.5
HIGH_BOUND = 33.0

WIDE = 256
GROUP = CAP // WIDE
BLOCK = 32
HALO = 8
F32, BF16 = jnp.float32, jnp.bfloat16


def partner(place, kind, count):
    if kind == 0:
        return place
    if kind == 1:
        return place ^ 1
    other = place - 1 if place % 2 == 0 else place + 1
    return other if 0 <= other < count else None


def exchange(value, x_kind, y_kind):
    nx, ny = lax.axis_size("gx"), lax.axis_size("gy")
    pairs = []
    for a in range(nx):
        for b in range(ny):
            x, y = partner(a, x_kind, nx), partner(b, y_kind, ny)
            if x is None:
                x, y = a, b ^ 1
            elif y is None:
                x, y = a ^ 1, b
            pairs.append((a * ny + b, x * ny + y))
    return lax.ppermute(value, ("gx", "gy"), pairs)


def pieces(value):
    high = value.astype(BF16).astype(F32)
    return high, value - high


def row_iota(count, width=128):
    return lax.broadcasted_iota(jnp.int32, (count, width), 0).astype(F32)


def onehot(row, count):
    return jnp.where(
        row_iota(count, row.shape[1]).astype(BF16) == row.astype(BF16),
        jnp.ones((), BF16),
        jnp.zeros((), BF16),
    )


def lanes(parts):
    return jnp.concatenate(parts, axis=1) if len(parts) > 1 else parts[0]


def transposed_dot(left, right):
    return lax.dot_general(left, right, (((1,), (1,)), ((), ())), preferred_element_type=F32)


def dot(left, right):
    return lax.dot_general(left, right, (((1,), (0,)), ((), ())), preferred_element_type=F32)


def kind_of(step, place):
    ahead = 1 - 2 * lax.rem(place, 2)
    return jnp.where(step == 0, 0, jnp.where(step == ahead, 1, 2))


def pack_kernel(
    nyc, cols, rows,
    bin_hbm, layer_hbm, off_hbm, power_hbm, spill_hbm, cond_hbm,
    msga_ref, msgb_ref, owny_ref, slot_ref, field_ref, power_ref,
    bin_ref, layer_ref, off_ref, spill_ref, edge_ref, sems, acc_ref,
):
    a, b = lax.axis_index("gx"), lax.axis_index("gy")
    copies = [
        pltpu.make_async_copy(src, dst, sems.at[i])
        for i, (src, dst) in enumerate(
            [
                (off_hbm, off_ref), (bin_hbm, bin_ref), (layer_hbm, layer_ref),
                (power_hbm, power_ref), (spill_hbm, spill_ref),
                (cond_hbm.at[:, :HALO, :], edge_ref.at[0]),
                (cond_hbm.at[:, cols - HALO :, :], edge_ref.at[1]),
            ]
        )
    ]
    for copy in copies:
        copy.start()
    acc_ref[...] = jnp.zeros_like(acc_ref)
    groups = 3 * nyc - 1
    table = groups * GROUP
    copies[0].wait()
    off = off_ref[...]
    col_code = (off >= 3).astype(jnp.int32) + (off >= 6).astype(jnp.int32)
    x_kind = kind_of(col_code - 1, a)
    y_kind = kind_of(off - 3 * col_code - 1, b)
    group = jnp.where(x_kind > 0, (x_kind - 1) * nyc + y_kind, 2 * nyc - 1 + y_kind)
    group = jnp.where(off == 4, -1, group)
    size = off.shape[0]
    r_i = lax.broadcasted_iota(jnp.int32, (size, size), 0)
    c_i = lax.broadcasted_iota(jnp.int32, (size, size), 1)
    upper = jnp.where(r_i < c_i, 1.0, 0.0).astype(BF16)
    lower = jnp.where(r_i > c_i, 1.0, 0.0).astype(BF16)
    ones = jnp.ones((size, size), BF16)
    slot = jnp.full(off.shape, -1.0, F32)
    for g in range(groups):
        mine = group == g
        mask = jnp.where(mine, 1.0, 0.0).astype(BF16)
        totals = dot(mask, ones).astype(BF16)
        rank = dot(mask, upper) + dot(lower, totals)
        slot = jnp.where(mine, rank + float(g * CAP), slot)
    slot_ref[...] = slot
    for copy in copies[1:]:
        copy.wait()
    code = layer_ref[...] * (cols * rows) + bin_ref[...]
    field_ref[0] = (code // rows).astype(F32)
    field_ref[1] = (code % rows).astype(F32)
    power = power_ref[...]
    spill = spill_ref[...]
    field_ref[2], field_ref[3] = pieces(power * (1.0 - spill))
    field_ref[4], field_ref[5] = pieces(power * spill)
    step = 32

    def body(j, carry):
        base = pl.multiple_of(j * step, step)
        slots = slot_ref[pl.ds(base, step), :]
        qs = jnp.floor(slots * (1.0 / WIDE))
        lams = slots - qs * WIDE
        vals = [field_ref[f, pl.ds(base, step), :] for f in range(6)]
        picks, marks = [], []
        for i in range(step):
            hit = row_iota(table) == qs[i : i + 1]
            picks.append(
                jnp.concatenate([jnp.where(hit, v[i : i + 1], 0.0) for v in vals], axis=0).astype(BF16)
            )
            marks.append(onehot(lams[i : i + 1], WIDE))
        acc_ref[...] += transposed_dot(lanes(picks), lanes(marks))
        return carry

    lax.fori_loop(0, size // step, body, 0)
    out = [acc_ref[f * table : (f + 1) * table, :] for f in range(6)]
    sent = [out[0] * float(rows) + out[1], out[2] + out[3], out[4] + out[5]]

    def put(ref, at, g):
        for f in range(3):
            ref[(at * 3 + f) * GROUP : (at * 3 + f + 1) * GROUP, :] = sent[f][
                g * GROUP : (g + 1) * GROUP
            ]

    for y in range(nyc):
        put(msga_ref, y, y)
        put(msgb_ref, y, nyc + y)
        if y:
            put(owny_ref, y - 1, 2 * nyc + y - 1)
    first, last = edge_ref[0], edge_ref[1]
    even = lax.rem(a, 2) == 0
    top = nyc * 3 * GROUP
    flat = (-1, rows)
    msga_ref[top:, :] = jnp.where(even, last, first).reshape(flat)
    msgb_ref[top:, :] = jnp.where(even, first, last).reshape(flat)


def deposit_block(lc, r, main, spill, cols, cells):
    picks, marks = [], []
    zero = jnp.zeros((), BF16)
    narrow = lambda x: x.astype(BF16)
    for lc_i, r_i, (mh, ml), (sh, sl) in zip(lc, r, main, spill):
        spot = narrow(row_iota(cells, lc_i.shape[1]))
        other = jnp.where(lc_i >= float(cells - cols), lc_i - cols, lc_i + cols)
        here, there = spot == narrow(lc_i), spot == narrow(other)
        high = jnp.where(here, narrow(mh), jnp.where(there, narrow(sh), zero))
        low = jnp.where(here, narrow(ml), jnp.where(there, narrow(sl), zero))
        picks.append(jnp.concatenate([high, low], axis=0))
        marks.append(onehot(r_i, WIDE))
    return transposed_dot(lanes(picks), lanes(marks))


def deposit_stays(grid_ref, field_ref, slot_ref, first, last, cols):
    count, step = grid_ref.shape[0] // 2, 32
    stays = slot_ref[first:last, :] < 0.0
    vals = [jnp.where(stays, field_ref[2 + f, first:last, :], 0.0) for f in range(4)]
    lcs, rs = field_ref[0, first:last, :], field_ref[1, first:last, :]
    for base in range(0, last - first, step):
        rows_of = lambda x: [x[base + i : base + i + 1] for i in range(step)]
        parts = [rows_of(v) for v in vals]
        grid_ref[...] += deposit_block(
            rows_of(lcs), rows_of(rs), list(zip(parts[0], parts[1])),
            list(zip(parts[2], parts[3])), cols, count,
        )


def stay_deposit_kernel(cols, split, field_ref, slot_ref, grid_ref):
    grid_ref[...] = jnp.zeros_like(grid_ref)
    deposit_stays(grid_ref, field_ref, slot_ref, 0, split, cols)


def deposit_groups(grid_ref, sources, cols):
    count, rows = grid_ref.shape[0] // 2, grid_ref.shape[1]
    lc, r, main, spill = [], [], [], []
    for ref, at in sources:
        for row in range(at, at + GROUP):
            code = ref[row : row + 1, :]
            lc_i = jnp.floor(code * (1.0 / rows))
            lc.append(lc_i)
            r.append(code - lc_i * rows)
            main.append(pieces(ref[row + GROUP : row + GROUP + 1, :]))
            spill.append(pieces(ref[row + 2 * GROUP : row + 2 * GROUP + 1, :]))
    grid_ref[...] += deposit_block(lc, r, main, spill, cols, count)


def near_deposit_kernel(cols, split, stay_ref, recva_ref, recvb_ref, field_ref, slot_ref, grid_ref):
    grid_ref[...] = stay_ref[...]
    deposit_stays(grid_ref, field_ref, slot_ref, split, slot_ref.shape[0], cols)
    deposit_groups(grid_ref, [(recva_ref, 0), (recvb_ref, 0)], cols)


def far_deposit_kernel(cols, nyc, *refs):
    near_ref, recvy = refs[0], refs[1:nyc]
    grid_ref, edgea_ref, edgeb_ref, acc_ref = refs[nyc:]
    acc_ref[...] = near_ref[...]
    sources = [(ref, 3 * GROUP * i) for ref in recvy for i in range(3)]
    deposit_groups(acc_ref, sources, cols)
    count = acc_ref.shape[0] // 2
    grid = (acc_ref[:count, :] + acc_ref[count:, :]).reshape(grid_ref.shape)
    grid_ref[...] = grid
    first, last = grid[:, :HALO, :], grid[:, cols - HALO :, :]
    even = lax.rem(lax.axis_index("gx"), 2) == 0
    edgea_ref[...] = jnp.where(even, last, first)
    edgeb_ref[...] = jnp.where(even, first, last)


def with_columns(own, from_a, from_b):
    a = lax.axis_index("gx")
    even = lax.rem(a, 2) == 0
    right = jnp.where(even, from_a, from_b)
    left = jnp.where(even, from_b, from_a)
    right = jnp.where(a < lax.axis_size("gx") - 1, right, 0.0)
    left = jnp.where(a > 0, left, 0.0)
    return jnp.concatenate([left, own, right], axis=1)


def row_edge(wide, last):
    rows = wide.shape[1]
    tile = jnp.where(last, wide[:, rows - 128 :], wide[:, :128]).T
    return jnp.where(last, tile[128 - HALO :], tile[:HALO])


def put_edges(ref, at, edge):
    extra = edge.shape[1] - WIDE
    ref[at : at + HALO, :] = edge[:, :WIDE]
    ref[at + HALO : at + 2 * HALO, :] = jnp.concatenate(
        [edge[:, WIDE:], jnp.zeros((HALO, WIDE - extra), F32)], axis=1
    )


def get_edges(ref, at, count):
    return jnp.concatenate(
        [ref[at : at + HALO, :], ref[at + HALO : at + 2 * HALO, : count - WIDE]], axis=1
    )


def y_edges(refs, at, wide):
    even = lax.rem(lax.axis_index("gy"), 2) == 0
    for kind, ref in enumerate(refs):
        put_edges(ref, at, row_edge(wide, even if kind == 0 else jnp.logical_not(even)))


def halo_of(ref, cols, layers, top):
    return ref[top:, :].reshape(layers, HALO, ref.shape[1])


def forward_kernel(nyc, recva_ref, recvb_ref, owny_ref, cond_ref, after_ref, *msgy_refs):
    layers, cols, rows = cond_ref.shape
    size, top = 3 * GROUP, nyc * 3 * GROUP
    for y, ref in enumerate(msgy_refs):
        ref[:size, :] = owny_ref[y * size : (y + 1) * size, :]
        ref[size : 2 * size, :] = recva_ref[(y + 1) * size : (y + 2) * size, :]
        ref[2 * size : 3 * size, :] = recvb_ref[(y + 1) * size : (y + 2) * size, :]
    wide = with_columns(
        cond_ref[...], halo_of(recva_ref, cols, layers, top), halo_of(recvb_ref, cols, layers, top)
    )
    y_edges(msgy_refs, 3 * size, wide.reshape(-1, rows))


def power_edge_kernel(grid_ref, froma_ref, fromb_ref, after_ref, *edge_refs):
    wide = with_columns(grid_ref[...], froma_ref[...], fromb_ref[...])
    y_edges(edge_refs, 0, wide.reshape(-1, grid_ref.shape[2]))


def with_rows(wide, edges):
    b, ny = lax.axis_index("gy"), lax.axis_size("gy")
    layers, span, rows = wide.shape
    count = layers * span
    even = lax.rem(b, 2) == 0
    one = edges[0]
    two = edges[1] if len(edges) > 1 else jnp.zeros_like(one)
    after = jnp.where(b < ny - 1, jnp.where(even, one, two), 0.0)
    before = jnp.where(b > 0, jnp.where(even, two, one), 0.0)
    tile = jnp.concatenate([after, jnp.zeros((128 - 2 * HALO, count), F32), before], axis=0).T
    return jnp.concatenate([wide, tile.reshape(layers, span, 128)], axis=2)


def face_kernel(nyc, cond_ref, recva_ref, recvb_ref, coupling_ref, *refs):
    recvy_refs, (cn_ref, cp_ref, rn_ref, rp_ref, fl_ref, d_ref, k_ref) = refs[: nyc - 1], refs[nyc - 1 :]
    layers, cols, rows = cond_ref.shape
    span, wide_rows = cols + 2 * HALO, rows + 128
    count = layers * span
    top = nyc * 3 * GROUP
    a, b = lax.axis_index("gx"), lax.axis_index("gy")
    nx, ny = lax.axis_size("gx"), lax.axis_size("gy")
    k_ref[...] = with_rows(
        with_columns(
            cond_ref[...],
            halo_of(recva_ref, cols, layers, top),
            halo_of(recvb_ref, cols, layers, top),
        ),
        [get_edges(ref, 9 * GROUP, count) for ref in recvy_refs],
    )
    shape = (span, wide_rows)
    c_i = lax.broadcasted_iota(jnp.int32, shape, 0)
    r_i = lax.broadcasted_iota(jnp.int32, shape, 1)
    c_low = jnp.where(a > 0, 0, HALO)
    c_high = jnp.where(a < nx - 1, span, span - HALO)
    r_high = jnp.where(b < ny - 1, rows + HALO, rows)
    r_low = jnp.where(b > 0, wide_rows - HALO, wide_rows)
    inside = jnp.where((c_i >= c_low) & (c_i < c_high) & ((r_i < r_high) | (r_i >= r_low)), 1.0, 0.0)
    next_c = lambda x: pltpu.roll(x, span - 1, 0)
    prev_c = lambda x: pltpu.roll(x, 1, 0)
    next_r = lambda x: pltpu.roll(x, wide_rows - 1, 1)
    prev_r = lambda x: pltpu.roll(x, 1, 1)
    both_c, both_r = inside * next_c(inside), inside * next_r(inside)
    below = None
    for l in range(layers):
        k = k_ref[l]
        face_c, face_r = 0.5 * (k + next_c(k)), 0.5 * (k + next_r(k))
        kept_c, kept_r = face_c * both_c, face_r * both_r
        cn_ref[l], cp_ref[l] = kept_c, prev_c(kept_c)
        rn_ref[l], rp_ref[l] = kept_r, prev_r(kept_r)
        total = SINK_RATE + ((face_c + prev_c(face_c)) + (face_r + prev_r(face_r)))
        if below is not None:
            total = total + below
        if l + 1 < layers:
            below = coupling_ref[l] * (0.5 * (k + k_ref[l + 1]))
            fl_ref[l] = below * inside
            total = total + below
        d_ref[l] = total


def solve_kernel(
    nyc, grid_ref, froma_ref, fromb_ref, cn_ref, cp_ref, rn_ref, rp_ref, fl_ref, d_ref, *refs
):
    edge_refs, (warmth_ref, slope_ref, p_ref, v_ref, u_ref) = refs[: nyc - 1], refs[nyc - 1 :]
    layers, cols, rows = grid_ref.shape
    span, wide_rows = cols + 2 * HALO, rows + 128
    p_ref[...] = with_rows(
        with_columns(grid_ref[...], froma_ref[...], fromb_ref[...]),
        [get_edges(ref, 0, layers * span) for ref in edge_refs],
    )
    next_r = lambda x: pltpu.roll(x, wide_rows - 1, 1)
    prev_r = lambda x: pltpu.roll(x, 1, 1)
    middle = 0.5 * (HIGH_BOUND + LOW_BOUND)
    spread = 0.5 * (HIGH_BOUND - LOW_BOUND)
    sigma = middle / spread
    now = 1.0 / sigma
    blank = jnp.zeros((8, wide_rows), F32)
    for l in range(layers):
        for side in range(2):
            v_ref[side, l, :8, :] = blank
            v_ref[side, l, 8 + span :, :] = blank
        v_ref[0, l, 8 : 8 + span, :] = p_ref[l] * (1.0 / middle)
    for sweep in range(ITERS):
        later = 1.0 / (2.0 * sigma - now)
        keep, gain = later * now, 2.0 * later / spread
        old, new = sweep % 2, (sweep + 1) % 2
        for c in range(0, span, 8):
            at, here = slice(c, c + 8), slice(c + 8, c + 16)
            vs = [v_ref[old, l, here, :] for l in range(layers)]
            for l in range(layers):
                v = vs[l]
                rest = p_ref[l, at, :] - d_ref[l, at, :] * v
                rest = rest + cn_ref[l, at, :] * v_ref[old, l, c + 9 : c + 17, :]
                rest = rest + cp_ref[l, at, :] * v_ref[old, l, c + 7 : c + 15, :]
                rest = rest + rn_ref[l, at, :] * next_r(v) + rp_ref[l, at, :] * prev_r(v)
                if l + 1 < layers:
                    rest = rest + fl_ref[l, at, :] * vs[l + 1]
                if l:
                    rest = rest + fl_ref[l - 1, at, :] * vs[l - 1]
                advance = keep * (u_ref[l, at, :] if sweep else v) + gain * rest
                if sweep + 1 < ITERS:
                    u_ref[l, at, :] = advance
                v_ref[new, l, here, :] = v + advance
        now = later
    final = ITERS % 2
    for l in range(layers):
        warmth_ref[l] = v_ref[final, l, 8 + HALO : 8 + HALO + cols, :rows]
        for c in range(0, cols, 16):
            at = 8 + HALO + c
            v = v_ref[final, l, at : at + 16, :]
            slopes = (
                0.5 * (v_ref[final, l, at + 1 : at + 17, :rows] - v_ref[final, l, at - 1 : at + 15, :rows]),
                0.5 * (next_r(v) - prev_r(v))[:, :rows],
            )
            for f, slope in enumerate(slopes):
                for part, piece in enumerate(pieces(slope)):
                    put = ((l * 2 + part) * 2 + f) * cols + c
                    slope_ref[put : put + 16, :] = piece.astype(BF16)


def pick(found, lc, first):
    cols = found.shape[0] // 4
    here = row_iota(cols, lc.shape[1]) == lc - first
    return [
        jnp.where(here, found[f * cols : (f + 1) * cols] + found[(2 + f) * cols : (3 + f) * cols], 0.0)
        for f in range(2)
    ]


def gather_block(slope, lc, r, layers):
    size = slope.shape[0] // layers
    found = dot(slope, onehot(r, slope.shape[1]))
    parts = [pick(found[l * size : (l + 1) * size], lc, l * (size // 4)) for l in range(layers)]
    return [jnp.sum(sum(p[f] for p in parts), axis=0, keepdims=True) for f in range(2)]


def gather_kernel(layers, sources, slope_ref, *refs):
    ins, out_ref = refs[:-1], refs[-1]
    rows = slope_ref.shape[1]
    for g, (which, at) in enumerate(sources):
        for t in range(GROUP):
            code = ins[which][at + t : at + t + 1, :]
            lc = jnp.floor(code * (1.0 / rows))
            for f, value in enumerate(gather_block(slope_ref[...], lc, code - lc * rows, layers)):
                row = (g * 2 + f) * GROUP + t
                out_ref[row : row + 1, :] = value


def sort_kernel(layers, cols, table, field_ref, slot_ref, after_ref, order_ref, place_ref, unit_ref):
    size = slot_ref.shape[0]
    span = BLOCK * size // WIDE
    r_i = lax.broadcasted_iota(jnp.int32, (size, size), 0)
    c_i = lax.broadcasted_iota(jnp.int32, (size, size), 1)
    flag = lambda x: jnp.where(x, 1.0, 0.0).astype(BF16)
    upper, ones = flag(r_i < c_i), jnp.ones((size, size), BF16)
    same = (r_i // BLOCK) == (c_i // BLOCK)
    both = jnp.concatenate([flag(same & (r_i > c_i)), flag(same)], axis=1)
    layer = jnp.floor(field_ref[0] * (1.0 / cols))
    ahead = jnp.zeros((size, size), F32)
    rank = jnp.zeros((size, size), F32)
    lane = lax.broadcasted_iota(jnp.int32, (size, size), 1).astype(F32)
    passed = jnp.zeros((size, size), F32)
    for l in range(layers):
        mine = layer == float(l)
        mask = flag(mine)
        totals = dot(mask, ones)
        stack = jnp.concatenate([totals.astype(BF16), ahead.astype(BF16)], axis=0)
        rank = jnp.where(mine, dot(mask, upper) + dot(both, stack), rank)
        ahead = ahead + totals
        if l + 1 < layers:
            end = jnp.floor(dot(both[:, size:], ahead.astype(BF16)) * (1.0 / WIDE))
            passed = passed + jnp.where(jnp.minimum(end, span - 1.0) + l < lane, 1.0, 0.0)
    unit_ref[...] = ((lane - passed) * layers + passed).astype(jnp.int32)
    row = jnp.floor(rank * (1.0 / WIDE))
    lam = rank - row * WIDE
    slot = slot_ref[...]
    place_ref[...] = jnp.where(slot >= 0.0, slot, (row + layer + table) * WIDE + lam)
    for k in range(size // BLOCK):
        picks, marks = [], []
        for i in range(k * BLOCK, (k + 1) * BLOCK):
            hit = row_iota(span) == row[i : i + 1]
            picks.append(
                jnp.concatenate(
                    [jnp.where(hit, field_ref[f, i : i + 1, :], 0.0) for f in range(2)], axis=0
                ).astype(BF16)
            )
            marks.append(onehot(lam[i : i + 1], WIDE))
        sorted_rows = transposed_dot(lanes(picks), lanes(marks))
        for f in range(2):
            order_ref[f, k * span : (k + 1) * span, :] = sorted_rows[f * span : (f + 1) * span]


def units_of(layers, size):
    return BLOCK * size // WIDE + layers


def stay_gather_kernel(layers, slope_ref, order_ref, unit_ref, out_ref):
    blocks = unit_ref.shape[0] // BLOCK
    span = order_ref.shape[1] // blocks
    size = slope_ref.shape[0] // layers
    units = units_of(layers, unit_ref.shape[0])

    def body(k, carry):
        for u in range(units - 1):
            code = unit_ref[k * BLOCK, u]
            layer, at = lax.rem(code, layers), k * span + code // layers
            lc, r = order_ref[0, pl.ds(at, 1), :], order_ref[1, pl.ds(at, 1), :]
            rows = slope_ref[pl.ds(pl.multiple_of(layer * size, size), size), :]
            first = (layer * (size // 4)).astype(F32)
            for f, part in enumerate(pick(dot(rows, onehot(r, slope_ref.shape[1])), lc, first)):
                out_ref[k, f * units + u : f * units + u + 1, :] = jnp.sum(part, axis=0, keepdims=True)
        for f in range(2):
            out_ref[k, (f + 1) * units - 1 : (f + 1) * units, :] = jnp.zeros((1, WIDE), F32)
        return carry

    lax.fori_loop(0, blocks, body, 0)


def reply_kernel(nyc, near_ref, *refs):
    size = 2 * GROUP
    backs, (a_ref, b_ref) = refs[: nyc - 1], refs[nyc - 1 :]
    a_ref[:size, :] = near_ref[:size, :]
    b_ref[:size, :] = near_ref[size:, :]
    for y, ref in enumerate(backs):
        a_ref[(y + 1) * size : (y + 2) * size, :] = ref[size : 2 * size, :]
        b_ref[(y + 1) * size : (y + 2) * size, :] = ref[2 * size : 3 * size, :]


def unpack_kernel(nyc, backa_ref, backb_ref, *refs):
    backy, (stay_ref, place_ref, power_ref, out_ref, table_ref) = refs[: nyc - 1], refs[nyc - 1 :]
    groups = [(backa_ref, y) for y in range(nyc)] + [(backb_ref, y) for y in range(nyc)]
    groups += [(ref, 0) for ref in backy]
    sent, units = len(groups) * GROUP, stay_ref.shape[1] // 2
    table = sent + units
    for f in range(2):
        whole = jnp.concatenate(
            [ref[(2 * at + f) * GROUP : (2 * at + f + 1) * GROUP, :] for ref, at in groups], axis=0
        )
        for part, piece in enumerate(pieces(whole)):
            at = (part * 2 + f) * table
            table_ref[at : at + sent, :] = piece

    def body(k, carry):
        base = pl.multiple_of(k * BLOCK, BLOCK)
        for f in range(2):
            for part, piece in enumerate(pieces(stay_ref[k, f * units : (f + 1) * units, :])):
                at = (part * 2 + f) * table + sent
                table_ref[at : at + units, :] = piece
        source = table_ref[...].astype(BF16)
        places = place_ref[pl.ds(base, BLOCK), :]
        qs = jnp.floor(places * (1.0 / WIDE))
        lams = places - qs * WIDE
        powers = power_ref[pl.ds(base, BLOCK), :]
        for i in range(0, BLOCK, 8):
            many = lambda x: lanes([x[i + j : i + j + 1] for j in range(8)])
            at = pl.multiple_of(base * 128 + i * 128, 1024)
            found = dot(source, onehot(many(lams), WIDE))
            here = row_iota(table, 1024) == many(qs)
            for f in range(2):
                both = found[f * table : (f + 1) * table] + found[(2 + f) * table : (3 + f) * table]
                value = jnp.sum(jnp.where(here, both, 0.0), axis=0, keepdims=True)
                out_ref[f : f + 1, pl.ds(at, 1024)] = -many(powers) * value
        return carry

    lax.fori_loop(0, place_ref.shape[0] // BLOCK, body, 0)


def call(kernel, outs, scratch, *args, spaces={}):
    space = pl.BlockSpec(memory_space=pltpu.VMEM)
    specs = [pl.BlockSpec(memory_space=spaces.get(i, pltpu.VMEM)) for i in range(len(args))]
    shapes = [jax.ShapeDtypeStruct(shape, dtype) for shape, dtype in outs]
    return pl.pallas_call(
        kernel,
        out_shape=shapes,
        in_specs=specs,
        out_specs=[space] * len(shapes),
        scratch_shapes=scratch,
        compiler_params=pltpu.CompilerParams(vmem_limit_bytes=48 * 1024 * 1024),
    )(*args)


def shards(
    cell_bin, cell_layer, cell_offset, cell_power, spill_weight, conductivity, layer_coupling
):
    layers, cols, rows = conductivity.shape
    cells = cell_bin.shape[0]
    nyc = 2 if lax.axis_size("gy") == 2 else 3
    count = layers * cols
    groups = 3 * nyc - 1
    flat = lambda x: x.reshape(cells // 128, 128)
    bins, layer, off = flat(cell_bin), flat(cell_layer), flat(cell_offset)
    power, spill = flat(cell_power), flat(spill_weight)
    square = bins.shape
    split = square[0] * 3 // 4
    own = 3 * GROUP
    message = (nyc * own + layers * HALO, WIDE)
    vmem = lambda *shape: pltpu.VMEM(shape, F32)
    partial = functools.partial

    tile = conductivity.shape
    msg_a, msg_b, own_y, slot, fields, power = call(
        partial(pack_kernel, nyc, cols, rows),
        [
            (message, F32), (message, F32), (((nyc - 1) * own, WIDE), F32),
            (square, F32), ((6, *square), F32), (square, F32),
        ],
        [pltpu.VMEM(square, jnp.int32)] * 3
        + [
            vmem(*square), vmem(2, layers, HALO, rows), pltpu.SemaphoreType.DMA((7,)),
            vmem(6 * groups * GROUP, WIDE),
        ],
        *[
            pltpu.with_memory_space_constraint(x, pltpu.HBM)
            for x in (bins, layer, off, power, spill, conductivity)
        ],
        spaces={i: pltpu.HBM for i in range(6)},
    )
    recv_a, recv_b = exchange(msg_a, 1, 0), exchange(msg_b, 2, 0)
    (stay_grid,) = call(
        partial(stay_deposit_kernel, cols, split),
        [((2 * count, rows), F32)],
        [],
        fields, slot,
    )
    msg_y = call(
        partial(forward_kernel, nyc),
        [((3 * own + 2 * HALO, WIDE), F32)] * (nyc - 1),
        [],
        recv_a, recv_b, own_y, conductivity, stay_grid,
        spaces={4: pl.ANY},
    )
    recv_y = [exchange(m, 0, i + 1) for i, m in enumerate(msg_y)]
    (near_grid,) = call(
        partial(near_deposit_kernel, cols, split),
        [((2 * count, rows), F32)],
        [],
        stay_grid, recv_a, recv_b, fields, slot,
    )
    edge = (layers, HALO, rows)
    grid, edge_a, edge_b = call(
        partial(far_deposit_kernel, cols, nyc),
        [(conductivity.shape, F32), (edge, F32), (edge, F32)],
        [vmem(2 * count, rows)],
        near_grid, *recv_y,
    )
    from_a, from_b = exchange(edge_a, 1, 0), exchange(edge_b, 2, 0)
    table = groups * GROUP
    order, place, unit = call(
        partial(sort_kernel, layers, cols, table),
        [((2, cells // WIDE, WIDE), F32), (square, F32), (square, jnp.int32)],
        [],
        fields, slot, grid,
        spaces={2: pl.ANY},
    )
    edges = call(
        power_edge_kernel,
        [((2 * HALO, WIDE), F32)] * (nyc - 1),
        [],
        grid, from_a, from_b, order,
        spaces={3: pl.ANY},
    )
    from_y = [exchange(e, 0, i + 1) for i, e in enumerate(edges)]
    big = (layers, cols + 2 * HALO, rows + 128)
    faces = call(
        partial(face_kernel, nyc),
        [(big, F32)] * 6,
        [vmem(*big)],
        conductivity, recv_a, recv_b, layer_coupling, *recv_y,
        spaces={3: pltpu.SMEM},
    )
    final_warmth, slope = call(
        partial(solve_kernel, nyc),
        [(tile, F32), ((4 * count, rows), BF16)],
        [vmem(*big), vmem(2, layers, big[1] + 16, big[2]), vmem(*big)],
        grid, from_a, from_b, *faces, *from_y,
    )
    answer_y = [
        call(
            partial(gather_kernel, layers, [(0, own * i) for i in range(3)]),
            [((6 * GROUP, WIDE), F32)],
            [],
            slope, r,
        )[0]
        for r in recv_y
    ]
    back_y = [exchange(m, 0, i + 1) for i, m in enumerate(answer_y)]
    (near_answer,) = call(
        partial(gather_kernel, layers, [(0, 0), (1, 0)]),
        [((4 * GROUP, WIDE), F32)],
        [],
        slope, recv_a, recv_b,
    )
    answer_a, answer_b = call(
        partial(reply_kernel, nyc),
        [((2 * nyc * GROUP, WIDE), F32)] * 2,
        [],
        near_answer, *back_y,
    )
    back_a, back_b = exchange(answer_a, 1, 0), exchange(answer_b, 2, 0)
    units = units_of(layers, square[0])
    (stay_value,) = call(
        partial(stay_gather_kernel, layers),
        [((square[0] // BLOCK, 2 * units, WIDE), F32)],
        [],
        slope, order, unit,
        spaces={2: pltpu.SMEM},
    )
    (pull,) = call(
        partial(unpack_kernel, nyc),
        [((2, cells), F32)],
        [vmem(4 * (table + units), WIDE)],
        back_a, back_b, *back_y, stay_value, place, power,
    )
    return final_warmth, pull


def solution(mesh):
    cell = P(("gx", "gy"))
    tile = P(None, "gx", "gy")
    return jax.shard_map(
        shards,
        mesh=mesh,
        in_specs=(cell, cell, cell, cell, cell, tile, P()),
        out_specs=(tile, P(None, ("gx", "gy"))),
        check_vma=False,
    )
```

```python
import functools

import jax
import jax.numpy as jnp
from jax import lax
from jax.experimental import pallas as pl
from jax.experimental.pallas import tpu as pltpu
from jax.sharding import PartitionSpec as P

ITERS = 4
CAP = 2048
SINK_RATE = 0.5
LOW_BOUND = 0.5
HIGH_BOUND = 33.0

WIDE = 256
GROUP = CAP // WIDE
BLOCK = 32
HALO = 8
F32, BF16 = jnp.float32, jnp.bfloat16


def partner(place, kind, count):
    if kind == 0:
        return place
    if kind == 1:
        return place ^ 1
    other = place - 1 if place % 2 == 0 else place + 1
    return other if 0 <= other < count else None


def exchange(value, x_kind, y_kind):
    nx, ny = lax.axis_size("gx"), lax.axis_size("gy")
    pairs = []
    for a in range(nx):
        for b in range(ny):
            x, y = partner(a, x_kind, nx), partner(b, y_kind, ny)
            if x is None:
                x, y = a, b ^ 1
            elif y is None:
                x, y = a ^ 1, b
            pairs.append((a * ny + b, x * ny + y))
    return lax.ppermute(value, ("gx", "gy"), pairs)


def pieces(value):
    high = value.astype(BF16).astype(F32)
    return high, value - high


def row_iota(count, width=128):
    return lax.broadcasted_iota(jnp.int32, (count, width), 0).astype(F32)


def onehot(row, count):
    return jnp.where(
        row_iota(count, row.shape[1]).astype(BF16) == row.astype(BF16),
        jnp.ones((), BF16),
        jnp.zeros((), BF16),
    )


def lanes(parts):
    return jnp.concatenate(parts, axis=1) if len(parts) > 1 else parts[0]


def transposed_dot(left, right):
    return lax.dot_general(left, right, (((1,), (1,)), ((), ())), preferred_element_type=F32)


def dot(left, right):
    return lax.dot_general(left, right, (((1,), (0,)), ((), ())), preferred_element_type=F32)


def kind_of(step, place):
    ahead = 1 - 2 * lax.rem(place, 2)
    return jnp.where(step == 0, 0, jnp.where(step == ahead, 1, 2))


def pack_kernel(
    nyc, layers, cols, rows,
    bin_hbm, layer_hbm, off_hbm, power_hbm, spill_hbm, cond_hbm,
    msga_ref, msgb_ref, owny_ref, slot_ref, field_ref, power_ref,
    bin_ref, layer_ref, off_ref, spill_ref, edge_ref, sems, acc_ref,
):
    a, b = lax.axis_index("gx"), lax.axis_index("gy")
    copies = [
        pltpu.make_async_copy(src, dst, sems.at[i])
        for i, (src, dst) in enumerate(
            [
                (off_hbm, off_ref), (layer_hbm, layer_ref), (bin_hbm, bin_ref),
                (power_hbm, power_ref), (spill_hbm, spill_ref),
                (cond_hbm.at[:, :HALO, :], edge_ref.at[0]),
                (cond_hbm.at[:, cols - HALO :, :], edge_ref.at[1]),
            ]
        )
    ]
    for copy in copies:
        copy.start()
    acc_ref[...] = jnp.zeros_like(acc_ref)
    groups = 3 * nyc - 1
    table = groups * GROUP
    copies[0].wait()
    copies[1].wait()
    off = off_ref[...]
    col_code = (off >= 3).astype(jnp.int32) + (off >= 6).astype(jnp.int32)
    x_kind = kind_of(col_code - 1, a)
    y_kind = kind_of(off - 3 * col_code - 1, b)
    group = jnp.where(x_kind > 0, (x_kind - 1) * nyc + y_kind, 2 * nyc - 1 + y_kind)
    key = jnp.where(off == 4, -1, group * layers + layer_ref[...])
    size = off.shape[0]
    r_i = lax.broadcasted_iota(jnp.int32, (size, size), 0)
    c_i = lax.broadcasted_iota(jnp.int32, (size, size), 1)
    flag = lambda x: jnp.where(x, 1.0, 0.0).astype(BF16)
    ones = jnp.ones((size, size), BF16)
    before = jnp.concatenate([flag(r_i < c_i), ones], axis=1)
    rank = jnp.zeros((size, size), F32)
    counts = jnp.zeros((size, size), F32)
    for g in range(groups):
        keys = range(g * layers, (g + 1) * layers)
        counted = dot(jnp.concatenate([flag(key == k) for k in keys], axis=0), before)
        for i, k in enumerate(keys):
            block = counted[i * size : (i + 1) * size]
            rank = jnp.where(key == k, block[:, :size], rank)
            counts = jnp.where(c_i == k, block[:, size:], counts)
    narrow = counts.astype(BF16)
    ahead = dot(narrow, flag((r_i // layers == c_i // layers) & (r_i < c_i))).astype(BF16)
    base = dot(
        jnp.concatenate([flag(r_i > c_i), ones], axis=1), jnp.concatenate([narrow, ahead], axis=0)
    )
    base = jnp.take_along_axis(base, jnp.maximum(key, 0), axis=1, mode="promise_in_bounds")
    slot = jnp.where(key >= 0, rank + base + (group * CAP).astype(F32), -1.0)
    slot_ref[...] = slot
    for copy in copies[2:]:
        copy.wait()
    code = layer_ref[...] * (cols * rows) + bin_ref[...]
    field_ref[0] = (code // rows).astype(F32)
    field_ref[1] = (code % rows).astype(F32)
    power = power_ref[...]
    spill = spill_ref[...]
    field_ref[2], field_ref[3] = pieces(power * (1.0 - spill))
    field_ref[4], field_ref[5] = pieces(power * spill)
    step = 32

    def body(j, carry):
        base = pl.multiple_of(j * step, step)
        slots = slot_ref[pl.ds(base, step), :]
        qs = jnp.floor(slots * (1.0 / WIDE))
        lams = slots - qs * WIDE
        vals = [field_ref[f, pl.ds(base, step), :] for f in range(6)]
        picks, marks = [], []
        for i in range(step):
            hit = row_iota(table) == qs[i : i + 1]
            picks.append(
                jnp.concatenate([jnp.where(hit, v[i : i + 1], 0.0) for v in vals], axis=0).astype(BF16)
            )
            marks.append(onehot(lams[i : i + 1], WIDE))
        acc_ref[...] += transposed_dot(lanes(picks), lanes(marks))
        return carry

    lax.fori_loop(0, size // step, body, 0)
    out = [acc_ref[f * table : (f + 1) * table, :] for f in range(6)]
    sent = [out[0] * float(rows) + out[1], out[2] + out[3], out[4] + out[5]]

    def put(ref, at, g):
        for f in range(3):
            ref[(at * 3 + f) * GROUP : (at * 3 + f + 1) * GROUP, :] = sent[f][
                g * GROUP : (g + 1) * GROUP
            ]

    for y in range(nyc):
        put(msga_ref, y, y)
        put(msgb_ref, y, nyc + y)
        if y:
            put(owny_ref, y - 1, 2 * nyc + y - 1)
    first, last = edge_ref[0], edge_ref[1]
    even = lax.rem(a, 2) == 0
    top = nyc * 3 * GROUP
    flat = (-1, rows)
    msga_ref[top:, :] = jnp.where(even, last, first).reshape(flat)
    msgb_ref[top:, :] = jnp.where(even, first, last).reshape(flat)


def deposit_block(lc, r, main, spill, cols, cells):
    picks, marks = [], []
    zero = jnp.zeros((), BF16)
    narrow = lambda x: x.astype(BF16)
    for lc_i, r_i, (mh, ml), (sh, sl) in zip(lc, r, main, spill):
        spot = narrow(row_iota(cells, lc_i.shape[1]))
        other = jnp.where(lc_i >= float(cells - cols), lc_i - cols, lc_i + cols)
        here, there = spot == narrow(lc_i), spot == narrow(other)
        high = jnp.where(here, narrow(mh), jnp.where(there, narrow(sh), zero))
        low = jnp.where(here, narrow(ml), jnp.where(there, narrow(sl), zero))
        picks.append(jnp.concatenate([high, low], axis=0))
        marks.append(onehot(r_i, WIDE))
    return transposed_dot(lanes(picks), lanes(marks))


def deposit_stays(grid_ref, field_ref, slot_ref, first, last, cols):
    count, step = grid_ref.shape[0] // 2, 32
    stays = slot_ref[first:last, :] < 0.0
    vals = [jnp.where(stays, field_ref[2 + f, first:last, :], 0.0) for f in range(4)]
    lcs, rs = field_ref[0, first:last, :], field_ref[1, first:last, :]
    for base in range(0, last - first, step):
        rows_of = lambda x: [x[base + i : base + i + 1] for i in range(step)]
        parts = [rows_of(v) for v in vals]
        grid_ref[...] += deposit_block(
            rows_of(lcs), rows_of(rs), list(zip(parts[0], parts[1])),
            list(zip(parts[2], parts[3])), cols, count,
        )


def stay_deposit_kernel(cols, split, field_ref, slot_ref, grid_ref):
    grid_ref[...] = jnp.zeros_like(grid_ref)
    deposit_stays(grid_ref, field_ref, slot_ref, 0, split, cols)


def deposit_groups(grid_ref, sources, cols):
    count, rows = grid_ref.shape[0] // 2, grid_ref.shape[1]
    lc, r, main, spill = [], [], [], []
    for ref, at in sources:
        for row in range(at, at + GROUP):
            code = ref[row : row + 1, :]
            lc_i = jnp.floor(code * (1.0 / rows))
            lc.append(lc_i)
            r.append(code - lc_i * rows)
            main.append(pieces(ref[row + GROUP : row + GROUP + 1, :]))
            spill.append(pieces(ref[row + 2 * GROUP : row + 2 * GROUP + 1, :]))
    grid_ref[...] += deposit_block(lc, r, main, spill, cols, count)


def count_units(unit_ref, sources, layers, cells):
    unit_ref[...] = jnp.zeros_like(unit_ref)
    lane = lax.broadcasted_iota(jnp.int32, (1, 128), 1).astype(F32)
    for g, (ref, at) in enumerate(sources):
        layer = jnp.floor(ref[at : at + GROUP, :] * (1.0 / cells))
        layer = jnp.where(ref[at + GROUP : at + 2 * GROUP, :] > 0.0, layer, float(layers))
        passed = jnp.zeros((1, 128), F32)
        for l in range(layers - 1):
            end = jnp.sum(jnp.where(layer <= l, 1.0, 0.0), axis=0, keepdims=True)
            end = jnp.floor(jnp.sum(end, axis=1, keepdims=True) * (1.0 / WIDE))
            passed = passed + jnp.where(jnp.minimum(end, GROUP - 1.0) + l < lane, 1.0, 0.0)
        unit_ref[g : g + 1, :] = ((lane - passed) * layers + passed).astype(jnp.int32)


def near_deposit_kernel(
    cols, split, stay_ref, recva_ref, recvb_ref, field_ref, slot_ref, grid_ref, unit_ref
):
    count, rows = grid_ref.shape[0] // 2, grid_ref.shape[1]
    count_units(unit_ref, [(recva_ref, 0), (recvb_ref, 0)], count // cols, cols * rows)
    grid_ref[...] = stay_ref[...]
    deposit_stays(grid_ref, field_ref, slot_ref, split, slot_ref.shape[0], cols)
    deposit_groups(grid_ref, [(recva_ref, 0), (recvb_ref, 0)], cols)


def far_deposit_kernel(cols, nyc, *refs):
    near_ref, recvy = refs[0], refs[1:nyc]
    grid_ref, edgea_ref, edgeb_ref, acc_ref = refs[nyc:]
    acc_ref[...] = near_ref[...]
    sources = [(ref, 3 * GROUP * i) for ref in recvy for i in range(3)]
    deposit_groups(acc_ref, sources, cols)
    count = acc_ref.shape[0] // 2
    grid = (acc_ref[:count, :] + acc_ref[count:, :]).reshape(grid_ref.shape)
    grid_ref[...] = grid
    first, last = grid[:, :HALO, :], grid[:, cols - HALO :, :]
    even = lax.rem(lax.axis_index("gx"), 2) == 0
    edgea_ref[...] = jnp.where(even, last, first)
    edgeb_ref[...] = jnp.where(even, first, last)


def with_columns(own, from_a, from_b):
    a = lax.axis_index("gx")
    even = lax.rem(a, 2) == 0
    right = jnp.where(even, from_a, from_b)
    left = jnp.where(even, from_b, from_a)
    right = jnp.where(a < lax.axis_size("gx") - 1, right, 0.0)
    left = jnp.where(a > 0, left, 0.0)
    return jnp.concatenate([left, own, right], axis=1)


def row_edge(wide, last):
    rows = wide.shape[1]
    tile = jnp.where(last, wide[:, rows - 128 :], wide[:, :128]).T
    return jnp.where(last, tile[128 - HALO :], tile[:HALO])


def put_edges(ref, at, edge):
    extra = edge.shape[1] - WIDE
    ref[at : at + HALO, :] = edge[:, :WIDE]
    ref[at + HALO : at + 2 * HALO, :] = jnp.concatenate(
        [edge[:, WIDE:], jnp.zeros((HALO, WIDE - extra), F32)], axis=1
    )


def get_edges(ref, at, count):
    return jnp.concatenate(
        [ref[at : at + HALO, :], ref[at + HALO : at + 2 * HALO, : count - WIDE]], axis=1
    )


def y_edges(refs, at, wide):
    even = lax.rem(lax.axis_index("gy"), 2) == 0
    for kind, ref in enumerate(refs):
        put_edges(ref, at, row_edge(wide, even if kind == 0 else jnp.logical_not(even)))


def halo_of(ref, cols, layers, top):
    return ref[top:, :].reshape(layers, HALO, ref.shape[1])


def forward_kernel(nyc, recva_ref, recvb_ref, owny_ref, cond_ref, after_ref, *msgy_refs):
    layers, cols, rows = cond_ref.shape
    size, top = 3 * GROUP, nyc * 3 * GROUP
    for y, ref in enumerate(msgy_refs):
        ref[:size, :] = owny_ref[y * size : (y + 1) * size, :]
        ref[size : 2 * size, :] = recva_ref[(y + 1) * size : (y + 2) * size, :]
        ref[2 * size : 3 * size, :] = recvb_ref[(y + 1) * size : (y + 2) * size, :]
    wide = with_columns(
        cond_ref[...], halo_of(recva_ref, cols, layers, top), halo_of(recvb_ref, cols, layers, top)
    )
    y_edges(msgy_refs, 3 * size, wide.reshape(-1, rows))


def power_edge_kernel(grid_ref, froma_ref, fromb_ref, after_ref, *edge_refs):
    wide = with_columns(grid_ref[...], froma_ref[...], fromb_ref[...])
    y_edges(edge_refs, 0, wide.reshape(-1, grid_ref.shape[2]))


def with_rows(wide, edges):
    b, ny = lax.axis_index("gy"), lax.axis_size("gy")
    layers, span, rows = wide.shape
    count = layers * span
    even = lax.rem(b, 2) == 0
    one = edges[0]
    two = edges[1] if len(edges) > 1 else jnp.zeros_like(one)
    after = jnp.where(b < ny - 1, jnp.where(even, one, two), 0.0)
    before = jnp.where(b > 0, jnp.where(even, two, one), 0.0)
    tile = jnp.concatenate([after, jnp.zeros((128 - 2 * HALO, count), F32), before], axis=0).T
    return jnp.concatenate([wide, tile.reshape(layers, span, 128)], axis=2)


def face_kernel(nyc, cond_ref, recva_ref, recvb_ref, coupling_ref, *refs):
    recvy_refs = refs[: nyc - 1]
    cn_ref, cp_ref, rn_ref, rp_ref, fl_ref, d_ref, unit_ref, k_ref = refs[nyc - 1 :]
    layers, cols, rows = cond_ref.shape
    span, wide_rows = cols + 2 * HALO, rows + 128
    count = layers * span
    top = nyc * 3 * GROUP
    sources = [(ref, 3 * GROUP * i) for ref in recvy_refs for i in range(3)]
    count_units(unit_ref, sources, layers, cols * rows)
    a, b = lax.axis_index("gx"), lax.axis_index("gy")
    nx, ny = lax.axis_size("gx"), lax.axis_size("gy")
    k_ref[...] = with_rows(
        with_columns(
            cond_ref[...],
            halo_of(recva_ref, cols, layers, top),
            halo_of(recvb_ref, cols, layers, top),
        ),
        [get_edges(ref, 9 * GROUP, count) for ref in recvy_refs],
    )
    shape = (span, wide_rows)
    c_i = lax.broadcasted_iota(jnp.int32, shape, 0)
    r_i = lax.broadcasted_iota(jnp.int32, shape, 1)
    c_low = jnp.where(a > 0, 0, HALO)
    c_high = jnp.where(a < nx - 1, span, span - HALO)
    r_high = jnp.where(b < ny - 1, rows + HALO, rows)
    r_low = jnp.where(b > 0, wide_rows - HALO, wide_rows)
    inside = jnp.where((c_i >= c_low) & (c_i < c_high) & ((r_i < r_high) | (r_i >= r_low)), 1.0, 0.0)
    next_c = lambda x: pltpu.roll(x, span - 1, 0)
    prev_c = lambda x: pltpu.roll(x, 1, 0)
    next_r = lambda x: pltpu.roll(x, wide_rows - 1, 1)
    prev_r = lambda x: pltpu.roll(x, 1, 1)
    both_c, both_r = inside * next_c(inside), inside * next_r(inside)
    below = None
    for l in range(layers):
        k = k_ref[l]
        face_c, face_r = 0.5 * (k + next_c(k)), 0.5 * (k + next_r(k))
        kept_c, kept_r = face_c * both_c, face_r * both_r
        cn_ref[l], cp_ref[l] = kept_c, prev_c(kept_c)
        rn_ref[l], rp_ref[l] = kept_r, prev_r(kept_r)
        total = SINK_RATE + ((face_c + prev_c(face_c)) + (face_r + prev_r(face_r)))
        if below is not None:
            total = total + below
        if l + 1 < layers:
            below = coupling_ref[l] * (0.5 * (k + k_ref[l + 1]))
            fl_ref[l] = below * inside
            total = total + below
        d_ref[l] = total


def solve_kernel(
    nyc, grid_ref, froma_ref, fromb_ref, cn_ref, cp_ref, rn_ref, rp_ref, fl_ref, d_ref, *refs
):
    edge_refs, (warmth_ref, slope_ref, p_ref, v_ref, u_ref) = refs[: nyc - 1], refs[nyc - 1 :]
    layers, cols, rows = grid_ref.shape
    span, wide_rows = cols + 2 * HALO, rows + 128
    p_ref[...] = with_rows(
        with_columns(grid_ref[...], froma_ref[...], fromb_ref[...]),
        [get_edges(ref, 0, layers * span) for ref in edge_refs],
    )
    next_r = lambda x: pltpu.roll(x, wide_rows - 1, 1)
    prev_r = lambda x: pltpu.roll(x, 1, 1)
    middle = 0.5 * (HIGH_BOUND + LOW_BOUND)
    spread = 0.5 * (HIGH_BOUND - LOW_BOUND)
    sigma = middle / spread
    now = 1.0 / sigma
    blank = jnp.zeros((8, wide_rows), F32)
    for l in range(layers):
        for side in range(2):
            v_ref[side, l, :8, :] = blank
            v_ref[side, l, 8 + span :, :] = blank
        v_ref[0, l, 8 : 8 + span, :] = p_ref[l] * (1.0 / middle)
    for sweep in range(ITERS):
        later = 1.0 / (2.0 * sigma - now)
        keep, gain = later * now, 2.0 * later / spread
        old, new = sweep % 2, (sweep + 1) % 2
        for c in range(0, span, 8):
            at, here = slice(c, c + 8), slice(c + 8, c + 16)
            vs = [v_ref[old, l, here, :] for l in range(layers)]
            for l in range(layers):
                v = vs[l]
                rest = p_ref[l, at, :] - d_ref[l, at, :] * v
                rest = rest + cn_ref[l, at, :] * v_ref[old, l, c + 9 : c + 17, :]
                rest = rest + cp_ref[l, at, :] * v_ref[old, l, c + 7 : c + 15, :]
                rest = rest + rn_ref[l, at, :] * next_r(v) + rp_ref[l, at, :] * prev_r(v)
                if l + 1 < layers:
                    rest = rest + fl_ref[l, at, :] * vs[l + 1]
                if l:
                    rest = rest + fl_ref[l - 1, at, :] * vs[l - 1]
                advance = keep * (u_ref[l, at, :] if sweep else v) + gain * rest
                if sweep + 1 < ITERS:
                    u_ref[l, at, :] = advance
                v_ref[new, l, here, :] = v + advance
        now = later
    final = ITERS % 2
    for l in range(layers):
        warmth_ref[l] = v_ref[final, l, 8 + HALO : 8 + HALO + cols, :rows]
        for c in range(0, cols, 16):
            at = 8 + HALO + c
            v = v_ref[final, l, at : at + 16, :]
            slopes = (
                0.5 * (v_ref[final, l, at + 1 : at + 17, :rows] - v_ref[final, l, at - 1 : at + 15, :rows]),
                0.5 * (next_r(v) - prev_r(v))[:, :rows],
            )
            for f, slope in enumerate(slopes):
                for part, piece in enumerate(pieces(slope)):
                    put = ((l * 2 + part) * 2 + f) * cols + c
                    slope_ref[put : put + 16, :] = piece.astype(BF16)


def pick(found, lc, first):
    cols = found.shape[0] // 4
    here = row_iota(cols, lc.shape[1]) == lc - first
    return [
        jnp.where(here, found[f * cols : (f + 1) * cols] + found[(2 + f) * cols : (3 + f) * cols], 0.0)
        for f in range(2)
    ]


def gather_unit(layers, slope_ref, code, lc, r):
    size = slope_ref.shape[0] // layers
    layer = lax.rem(code, layers)
    rows = slope_ref[pl.ds(pl.multiple_of(layer * size, size), size), :]
    found = dot(rows, onehot(r, slope_ref.shape[1]))
    first = (layer * (size // 4)).astype(F32)
    return [jnp.sum(part, axis=0, keepdims=True) for part in pick(found, lc, first)]


def gather_kernel(layers, sources, slope_ref, unit_ref, *refs):
    ins, out_ref = refs[:-1], refs[-1]
    rows = slope_ref.shape[1]
    for g, (which, at, line) in enumerate(sources):
        totals = [jnp.zeros((GROUP, WIDE), F32)] * 2
        for u in range(GROUP + layers - 1):
            code = unit_ref[line, u]
            row = lax.div(code, layers)
            slots = ins[which][pl.ds(at + row, 1), :]
            lc = jnp.floor(slots * (1.0 / rows))
            hit = row_iota(GROUP, WIDE) == row.astype(F32)
            for f, value in enumerate(gather_unit(layers, slope_ref, code, lc, slots - lc * rows)):
                totals[f] = totals[f] + jnp.where(hit, value, 0.0)
        for f in range(2):
            out_ref[(g * 2 + f) * GROUP : (g * 2 + f + 1) * GROUP, :] = totals[f]


def sort_kernel(layers, cols, table, field_ref, slot_ref, after_ref, order_ref, place_ref, unit_ref):
    size = slot_ref.shape[0]
    span = BLOCK * size // WIDE
    r_i = lax.broadcasted_iota(jnp.int32, (size, size), 0)
    c_i = lax.broadcasted_iota(jnp.int32, (size, size), 1)
    flag = lambda x: jnp.where(x, 1.0, 0.0).astype(BF16)
    upper, ones = flag(r_i < c_i), jnp.ones((size, size), BF16)
    same = (r_i // BLOCK) == (c_i // BLOCK)
    both = jnp.concatenate([flag(same & (r_i > c_i)), flag(same)], axis=1)
    layer = jnp.floor(field_ref[0] * (1.0 / cols))
    ahead = jnp.zeros((size, size), F32)
    rank = jnp.zeros((size, size), F32)
    lane = lax.broadcasted_iota(jnp.int32, (size, size), 1).astype(F32)
    passed = jnp.zeros((size, size), F32)
    for l in range(layers):
        mine = layer == float(l)
        mask = flag(mine)
        totals = dot(mask, ones)
        stack = jnp.concatenate([totals.astype(BF16), ahead.astype(BF16)], axis=0)
        rank = jnp.where(mine, dot(mask, upper) + dot(both, stack), rank)
        ahead = ahead + totals
        if l + 1 < layers:
            end = jnp.floor(dot(both[:, size:], ahead.astype(BF16)) * (1.0 / WIDE))
            passed = passed + jnp.where(jnp.minimum(end, span - 1.0) + l < lane, 1.0, 0.0)
    unit = ((lane - passed) * layers + passed).astype(jnp.int32)
    for k in range(size // BLOCK):
        unit_ref[k : k + 1, :] = unit[k * BLOCK : k * BLOCK + 1]
    row = jnp.floor(rank * (1.0 / WIDE))
    lam = rank - row * WIDE
    slot = slot_ref[...]
    place_ref[...] = jnp.where(slot >= 0.0, slot, (row + layer + table) * WIDE + lam)
    for k in range(size // BLOCK):
        picks, marks = [], []
        for i in range(k * BLOCK, (k + 1) * BLOCK):
            hit = row_iota(span) == row[i : i + 1]
            picks.append(
                jnp.concatenate(
                    [jnp.where(hit, field_ref[f, i : i + 1, :], 0.0) for f in range(2)], axis=0
                ).astype(BF16)
            )
            marks.append(onehot(lam[i : i + 1], WIDE))
        sorted_rows = transposed_dot(lanes(picks), lanes(marks))
        for f in range(2):
            order_ref[f, k * span : (k + 1) * span, :] = sorted_rows[f * span : (f + 1) * span]


def stay_gather_kernel(layers, start, slope_ref, order_ref, unit_ref, out_ref):
    span = order_ref.shape[1] // unit_ref.shape[0]
    units = span + layers

    def body(j, carry):
        k = j + start
        for u in range(units - 1):
            code = unit_ref[k, u]
            at = k * span + lax.div(code, layers)
            lc, r = order_ref[0, pl.ds(at, 1), :], order_ref[1, pl.ds(at, 1), :]
            for f, value in enumerate(gather_unit(layers, slope_ref, code, lc, r)):
                out_ref[j, f * units + u : f * units + u + 1, :] = value
        for f in range(2):
            out_ref[j, (f + 1) * units - 1 : (f + 1) * units, :] = jnp.zeros((1, WIDE), F32)
        return carry

    lax.fori_loop(0, out_ref.shape[0], body, 0)


def reply_kernel(nyc, near_ref, after_ref, *refs):
    size = 2 * GROUP
    backs, (a_ref, b_ref) = refs[: nyc - 1], refs[nyc - 1 :]
    a_ref[:size, :] = near_ref[:size, :]
    b_ref[:size, :] = near_ref[size:, :]
    for y, ref in enumerate(backs):
        a_ref[(y + 1) * size : (y + 2) * size, :] = ref[size : 2 * size, :]
        b_ref[(y + 1) * size : (y + 2) * size, :] = ref[2 * size : 3 * size, :]


def unpack_kernel(nyc, backa_ref, backb_ref, *refs):
    backy = refs[: nyc - 1]
    early_ref, late_ref, place_ref, power_ref, out_ref, table_ref = refs[nyc - 1 :]
    groups = [(backa_ref, y) for y in range(nyc)] + [(backb_ref, y) for y in range(nyc)]
    groups += [(ref, 0) for ref in backy]
    sent, units = len(groups) * GROUP, early_ref.shape[1] // 2
    table = sent + units
    for f in range(2):
        whole = jnp.concatenate(
            [ref[(2 * at + f) * GROUP : (2 * at + f + 1) * GROUP, :] for ref, at in groups], axis=0
        )
        for part, piece in enumerate(pieces(whole)):
            at = (part * 2 + f) * table
            table_ref[at : at + sent, :] = piece

    def body(stay_ref, start, k, carry):
        base = pl.multiple_of((k + start) * BLOCK, BLOCK)
        for f in range(2):
            for part, piece in enumerate(pieces(stay_ref[k, f * units : (f + 1) * units, :])):
                at = (part * 2 + f) * table + sent
                table_ref[at : at + units, :] = piece
        source = table_ref[...].astype(BF16)
        places = place_ref[pl.ds(base, BLOCK), :]
        qs = jnp.floor(places * (1.0 / WIDE))
        lams = places - qs * WIDE
        powers = power_ref[pl.ds(base, BLOCK), :]
        for i in range(0, BLOCK, 8):
            many = lambda x: lanes([x[i + j : i + j + 1] for j in range(8)])
            at = pl.multiple_of(base * 128 + i * 128, 1024)
            found = dot(source, onehot(many(lams), WIDE))
            here = row_iota(table, 1024) == many(qs)
            for f in range(2):
                both = found[f * table : (f + 1) * table] + found[(2 + f) * table : (3 + f) * table]
                value = jnp.sum(jnp.where(here, both, 0.0), axis=0, keepdims=True)
                out_ref[f : f + 1, pl.ds(at, 1024)] = -many(powers) * value
        return carry

    early = early_ref.shape[0]
    lax.fori_loop(0, early, functools.partial(body, early_ref, 0), 0)
    lax.fori_loop(0, late_ref.shape[0], functools.partial(body, late_ref, early), 0)


def call(kernel, outs, scratch, *args, spaces={}):
    space = pl.BlockSpec(memory_space=pltpu.VMEM)
    specs = [pl.BlockSpec(memory_space=spaces.get(i, pltpu.VMEM)) for i in range(len(args))]
    shapes = [jax.ShapeDtypeStruct(shape, dtype) for shape, dtype in outs]
    return pl.pallas_call(
        kernel,
        out_shape=shapes,
        in_specs=specs,
        out_specs=[space] * len(shapes),
        scratch_shapes=scratch,
        compiler_params=pltpu.CompilerParams(vmem_limit_bytes=48 * 1024 * 1024),
    )(*args)


def shards(
    cell_bin, cell_layer, cell_offset, cell_power, spill_weight, conductivity, layer_coupling
):
    layers, cols, rows = conductivity.shape
    cells = cell_bin.shape[0]
    nyc = 2 if lax.axis_size("gy") == 2 else 3
    count = layers * cols
    groups = 3 * nyc - 1
    flat = lambda x: x.reshape(cells // 128, 128)
    bins, layer, off = flat(cell_bin), flat(cell_layer), flat(cell_offset)
    power, spill = flat(cell_power), flat(spill_weight)
    square = bins.shape
    split = square[0] * 3 // 4
    own = 3 * GROUP
    message = (nyc * own + layers * HALO, WIDE)
    vmem = lambda *shape: pltpu.VMEM(shape, F32)
    partial = functools.partial

    tile = conductivity.shape
    msg_a, msg_b, own_y, slot, fields, power = call(
        partial(pack_kernel, nyc, layers, cols, rows),
        [
            (message, F32), (message, F32), (((nyc - 1) * own, WIDE), F32),
            (square, F32), ((6, *square), F32), (square, F32),
        ],
        [pltpu.VMEM(square, jnp.int32)] * 3
        + [
            vmem(*square), vmem(2, layers, HALO, rows), pltpu.SemaphoreType.DMA((7,)),
            vmem(6 * groups * GROUP, WIDE),
        ],
        *[
            pltpu.with_memory_space_constraint(x, pltpu.HBM)
            for x in (bins, layer, off, power, spill, conductivity)
        ],
        spaces={i: pltpu.HBM for i in range(6)},
    )
    recv_a, recv_b = exchange(msg_a, 1, 0), exchange(msg_b, 2, 0)
    (stay_grid,) = call(
        partial(stay_deposit_kernel, cols, split),
        [((2 * count, rows), F32)],
        [],
        fields, slot,
    )
    msg_y = call(
        partial(forward_kernel, nyc),
        [((3 * own + 2 * HALO, WIDE), F32)] * (nyc - 1),
        [],
        recv_a, recv_b, own_y, conductivity, stay_grid,
        spaces={4: pl.ANY},
    )
    recv_y = [exchange(m, 0, i + 1) for i, m in enumerate(msg_y)]
    near_grid, near_unit = call(
        partial(near_deposit_kernel, cols, split),
        [((2 * count, rows), F32), ((8, 128), jnp.int32)],
        [],
        stay_grid, recv_a, recv_b, fields, slot,
    )
    edge = (layers, HALO, rows)
    grid, edge_a, edge_b = call(
        partial(far_deposit_kernel, cols, nyc),
        [(conductivity.shape, F32), (edge, F32), (edge, F32)],
        [vmem(2 * count, rows)],
        near_grid, *recv_y,
    )
    from_a, from_b = exchange(edge_a, 1, 0), exchange(edge_b, 2, 0)
    table = groups * GROUP
    order, place, unit = call(
        partial(sort_kernel, layers, cols, table),
        [((2, cells // WIDE, WIDE), F32), (square, F32), ((square[0] // BLOCK, 128), jnp.int32)],
        [],
        fields, slot, grid,
        spaces={2: pl.ANY},
    )
    edges = call(
        power_edge_kernel,
        [((2 * HALO, WIDE), F32)] * (nyc - 1),
        [],
        grid, from_a, from_b, order,
        spaces={3: pl.ANY},
    )
    from_y = [exchange(e, 0, i + 1) for i, e in enumerate(edges)]
    big = (layers, cols + 2 * HALO, rows + 128)
    *faces, far_unit = call(
        partial(face_kernel, nyc),
        [(big, F32)] * 6 + [((8, 128), jnp.int32)],
        [vmem(*big)],
        conductivity, recv_a, recv_b, layer_coupling, *recv_y,
        spaces={3: pltpu.SMEM},
    )
    final_warmth, slope = call(
        partial(solve_kernel, nyc),
        [(tile, F32), ((4 * count, rows), BF16)],
        [vmem(*big), vmem(2, layers, big[1] + 16, big[2]), vmem(*big)],
        grid, from_a, from_b, *faces, *from_y,
    )
    answer_y = [
        call(
            partial(gather_kernel, layers, [(0, own * i, 3 * y + i) for i in range(3)]),
            [((6 * GROUP, WIDE), F32)],
            [],
            slope, far_unit, r,
            spaces={1: pltpu.SMEM},
        )[0]
        for y, r in enumerate(recv_y)
    ]
    back_y = [exchange(m, 0, i + 1) for i, m in enumerate(answer_y)]
    (near_answer,) = call(
        partial(gather_kernel, layers, [(0, 0, 0), (1, 0, 1)]),
        [((4 * GROUP, WIDE), F32)],
        [],
        slope, near_unit, recv_a, recv_b,
        spaces={1: pltpu.SMEM},
    )
    blocks, early = square[0] // BLOCK, 1
    units = order.shape[1] // blocks + layers
    stay_values = [
        functools.partial(
            call,
            partial(stay_gather_kernel, layers, start),
            [((size, 2 * units, WIDE), F32)],
            [],
            slope, order, unit,
            spaces={2: pltpu.SMEM},
        )
        for start, size in ((0, early), (early, blocks - early))
    ]
    (early_value,) = stay_values[0]()
    answer_a, answer_b = call(
        partial(reply_kernel, nyc),
        [((2 * nyc * GROUP, WIDE), F32)] * 2,
        [],
        near_answer, early_value, *back_y,
        spaces={1: pl.ANY},
    )
    back_a, back_b = exchange(answer_a, 1, 0), exchange(answer_b, 2, 0)
    (late_value,) = stay_values[1]()
    (pull,) = call(
        partial(unpack_kernel, nyc),
        [((2, cells), F32)],
        [vmem(4 * (table + units), WIDE)],
        back_a, back_b, *back_y, early_value, late_value, place, power,
    )
    return final_warmth, pull


def solution(mesh):
    cell = P(("gx", "gy"))
    tile = P(None, "gx", "gy")
    return jax.shard_map(
        shards,
        mesh=mesh,
        in_specs=(cell, cell, cell, cell, cell, tile, P()),
        out_specs=(tile, P(None, ("gx", "gy"))),
        check_vma=False,
    )
```

```python
import functools

import jax
import jax.numpy as jnp
from jax import lax
from jax.experimental import pallas as pl
from jax.experimental.pallas import tpu as pltpu
from jax.sharding import PartitionSpec as P

ITERS = 4
CAP = 2048
SINK_RATE = 0.5
LOW_BOUND = 0.5
HIGH_BOUND = 33.0

WIDE = 256
GROUP = CAP // WIDE
BLOCK = 32
HALO = 8
F32, BF16 = jnp.float32, jnp.bfloat16


def partner(place, kind, count):
    if kind == 0:
        return place
    if kind == 1:
        return place ^ 1
    other = place - 1 if place % 2 == 0 else place + 1
    return other if 0 <= other < count else None


def exchange(value, x_kind, y_kind):
    nx, ny = lax.axis_size("gx"), lax.axis_size("gy")
    pairs = []
    for a in range(nx):
        for b in range(ny):
            x, y = partner(a, x_kind, nx), partner(b, y_kind, ny)
            if x is None:
                x, y = a, b ^ 1
            elif y is None:
                x, y = a ^ 1, b
            pairs.append((a * ny + b, x * ny + y))
    return lax.ppermute(value, ("gx", "gy"), pairs)


def pieces(value):
    high = value.astype(BF16).astype(F32)
    return high, value - high


def row_iota(count, width=128):
    return lax.broadcasted_iota(jnp.int32, (count, width), 0).astype(F32)


def onehot(row, count):
    return jnp.where(
        row_iota(count, row.shape[1]).astype(BF16) == row.astype(BF16),
        jnp.ones((), BF16),
        jnp.zeros((), BF16),
    )


def lanes(parts):
    return jnp.concatenate(parts, axis=1) if len(parts) > 1 else parts[0]


def transposed_dot(left, right):
    return lax.dot_general(left, right, (((1,), (1,)), ((), ())), preferred_element_type=F32)


def dot(left, right):
    return lax.dot_general(left, right, (((1,), (0,)), ((), ())), preferred_element_type=F32)


def kind_of(step, place):
    ahead = 1 - 2 * lax.rem(place, 2)
    return jnp.where(step == 0, 0, jnp.where(step == ahead, 1, 2))


def pack_kernel(
    nyc, layers, cols, rows,
    bin_hbm, layer_hbm, off_hbm, power_hbm, spill_hbm, cond_hbm,
    msga_ref, msgb_ref, owny_ref, slot_ref, field_ref, power_ref,
    bin_ref, layer_ref, off_ref, spill_ref, edge_ref, sems, acc_ref,
):
    a, b = lax.axis_index("gx"), lax.axis_index("gy")
    copies = [
        pltpu.make_async_copy(src, dst, sems.at[i])
        for i, (src, dst) in enumerate(
            [
                (off_hbm, off_ref), (layer_hbm, layer_ref), (bin_hbm, bin_ref),
                (power_hbm, power_ref), (spill_hbm, spill_ref),
                (cond_hbm.at[:, :HALO, :], edge_ref.at[0]),
                (cond_hbm.at[:, cols - HALO :, :], edge_ref.at[1]),
            ]
        )
    ]
    for copy in copies:
        copy.start()
    acc_ref[...] = jnp.zeros_like(acc_ref)
    groups = 3 * nyc - 1
    table = groups * GROUP
    copies[0].wait()
    copies[1].wait()
    off = off_ref[...]
    col_code = (off >= 3).astype(jnp.int32) + (off >= 6).astype(jnp.int32)
    x_kind = kind_of(col_code - 1, a)
    y_kind = kind_of(off - 3 * col_code - 1, b)
    group = jnp.where(x_kind > 0, (x_kind - 1) * nyc + y_kind, 2 * nyc - 1 + y_kind)
    key = jnp.where(off == 4, -1, group * layers + layer_ref[...])
    size = off.shape[0]
    r_i = lax.broadcasted_iota(jnp.int32, (size, size), 0)
    c_i = lax.broadcasted_iota(jnp.int32, (size, size), 1)
    flag = lambda x: jnp.where(x, 1.0, 0.0).astype(BF16)
    ones = jnp.ones((size, size), BF16)
    before = jnp.concatenate([flag(r_i < c_i), ones], axis=1)
    rank = jnp.zeros((size, size), F32)
    counts = jnp.zeros((size, size), F32)
    for g in range(groups):
        keys = range(g * layers, (g + 1) * layers)
        counted = dot(jnp.concatenate([flag(key == k) for k in keys], axis=0), before)
        for i, k in enumerate(keys):
            block = counted[i * size : (i + 1) * size]
            rank = jnp.where(key == k, block[:, :size], rank)
            counts = jnp.where(c_i == k, block[:, size:], counts)
    narrow = counts.astype(BF16)
    ahead = dot(narrow, flag((r_i // layers == c_i // layers) & (r_i < c_i))).astype(BF16)
    base = dot(
        jnp.concatenate([flag(r_i > c_i), ones], axis=1), jnp.concatenate([narrow, ahead], axis=0)
    )
    base = jnp.take_along_axis(base, jnp.maximum(key, 0), axis=1, mode="promise_in_bounds")
    slot = jnp.where(key >= 0, rank + base + (group * CAP).astype(F32), -1.0)
    slot_ref[...] = slot
    for copy in copies[2:]:
        copy.wait()
    code = layer_ref[...] * (cols * rows) + bin_ref[...]
    field_ref[0] = (code // rows).astype(F32)
    field_ref[1] = (code % rows).astype(F32)
    power = power_ref[...]
    spill = spill_ref[...]
    field_ref[2], field_ref[3] = pieces(power * (1.0 - spill))
    field_ref[4], field_ref[5] = pieces(power * spill)
    step = 64

    def body(j, carry):
        base = pl.multiple_of(j * step, step)
        slots = slot_ref[pl.ds(base, step), :]
        qs = jnp.floor(slots * (1.0 / WIDE))
        lams = slots - qs * WIDE
        vals = [field_ref[f, pl.ds(base, step), :] for f in range(6)]
        picks, marks = [], []
        for i in range(step):
            hit = row_iota(table) == qs[i : i + 1]
            picks.append(
                jnp.concatenate([jnp.where(hit, v[i : i + 1], 0.0) for v in vals], axis=0).astype(BF16)
            )
            marks.append(onehot(lams[i : i + 1], WIDE))
        acc_ref[...] += transposed_dot(lanes(picks), lanes(marks))
        return carry

    lax.fori_loop(0, size // step, body, 0)
    out = [acc_ref[f * table : (f + 1) * table, :] for f in range(6)]
    sent = [out[0] * float(rows) + out[1], out[2] + out[3], out[4] + out[5]]

    def put(ref, at, g):
        for f in range(3):
            ref[(at * 3 + f) * GROUP : (at * 3 + f + 1) * GROUP, :] = sent[f][
                g * GROUP : (g + 1) * GROUP
            ]

    for y in range(nyc):
        put(msga_ref, y, y)
        put(msgb_ref, y, nyc + y)
        if y:
            put(owny_ref, y - 1, 2 * nyc + y - 1)
    first, last = edge_ref[0], edge_ref[1]
    even = lax.rem(a, 2) == 0
    top = nyc * 3 * GROUP
    flat = (-1, rows)
    msga_ref[top:, :] = jnp.where(even, last, first).reshape(flat)
    msgb_ref[top:, :] = jnp.where(even, first, last).reshape(flat)


def deposit_block(lc, r, main, spill, cols, cells, part=None):
    picks, marks = [], []
    zero = jnp.zeros((), BF16)
    narrow = lambda x: x.astype(BF16)
    quarter = cols // 4
    count = cells if part is None else cells // 2
    for lc_i, r_i, (mh, ml), (sh, sl) in zip(lc, r, main, spill):
        spot = narrow(row_iota(count, lc_i.shape[1]))
        step = cols
        other = lambda at: jnp.where(lc_i >= float(cells - cols), at - step, at + step)
        if part is None:
            there_i = other(lc_i)
        else:
            step = cols // 2
            layer = jnp.floor(lc_i * (1.0 / cols))
            column = lc_i - layer * cols
            inner = (column >= quarter) & (column < 3 * quarter)
            if part == "inner":
                mine, at = inner, layer * step + (column - quarter)
            else:
                mine = jnp.logical_not(inner)
                at = layer * step + jnp.where(column < quarter, column, column - step)
            there_i = jnp.where(mine, other(at), -1.0)
            lc_i = jnp.where(mine, at, -1.0)
        here, there = spot == narrow(lc_i), spot == narrow(there_i)
        high = jnp.where(here, narrow(mh), jnp.where(there, narrow(sh), zero))
        low = jnp.where(here, narrow(ml), jnp.where(there, narrow(sl), zero))
        picks.append(jnp.concatenate([high, low], axis=0))
        marks.append(onehot(r_i, WIDE))
    return transposed_dot(lanes(picks), lanes(marks))


def deposit_stays(grid_ref, field_ref, slot_ref, first, last, cols):
    count, step = grid_ref.shape[0] // 2, 32
    stays = slot_ref[first:last, :] < 0.0
    vals = [jnp.where(stays, field_ref[2 + f, first:last, :], 0.0) for f in range(4)]
    lcs, rs = field_ref[0, first:last, :], field_ref[1, first:last, :]
    for base in range(0, last - first, step):
        rows_of = lambda x: [x[base + i : base + i + 1] for i in range(step)]
        parts = [rows_of(v) for v in vals]
        grid_ref[...] += deposit_block(
            rows_of(lcs), rows_of(rs), list(zip(parts[0], parts[1])),
            list(zip(parts[2], parts[3])), cols, count,
        )


def stay_deposit_kernel(cols, split, field_ref, slot_ref, grid_ref):
    grid_ref[...] = jnp.zeros_like(grid_ref)
    deposit_stays(grid_ref, field_ref, slot_ref, 0, split, cols)


def group_deposit(sources, cols, count, part=None):
    lc, r, main, spill = [], [], [], []
    for ref, at in sources:
        rows = ref.shape[1]
        for row in range(at, at + GROUP):
            code = ref[row : row + 1, :]
            lc_i = jnp.floor(code * (1.0 / rows))
            lc.append(lc_i)
            r.append(code - lc_i * rows)
            main.append(pieces(ref[row + GROUP : row + GROUP + 1, :]))
            spill.append(pieces(ref[row + 2 * GROUP : row + 2 * GROUP + 1, :]))
    return deposit_block(lc, r, main, spill, cols, count, part)


def count_units(unit_ref, sources, layers, cells):
    unit_ref[...] = jnp.zeros_like(unit_ref)
    lane = lax.broadcasted_iota(jnp.int32, (1, 128), 1).astype(F32)
    for g, (ref, at) in enumerate(sources):
        layer = jnp.floor(ref[at : at + GROUP, :] * (1.0 / cells))
        layer = jnp.where(ref[at + GROUP : at + 2 * GROUP, :] > 0.0, layer, float(layers))
        passed = jnp.zeros((1, 128), F32)
        for l in range(layers - 1):
            end = jnp.sum(jnp.where(layer <= l, 1.0, 0.0), axis=0, keepdims=True)
            end = jnp.floor(jnp.sum(end, axis=1, keepdims=True) * (1.0 / WIDE))
            passed = passed + jnp.where(jnp.minimum(end, GROUP - 1.0) + l < lane, 1.0, 0.0)
        unit_ref[g : g + 1, :] = ((lane - passed) * layers + passed).astype(jnp.int32)


def near_deposit_kernel(
    cols, split, stay_ref, recva_ref, recvb_ref, field_ref, slot_ref, grid_ref, unit_ref
):
    count, rows = grid_ref.shape[0] // 2, grid_ref.shape[1]
    count_units(unit_ref, [(recva_ref, 0), (recvb_ref, 0)], count // cols, cols * rows)
    grid_ref[...] = stay_ref[...]
    deposit_stays(grid_ref, field_ref, slot_ref, split, slot_ref.shape[0], cols)
    grid_ref[...] += group_deposit([(recva_ref, 0), (recvb_ref, 0)], cols, count)


def half_deposit(near_ref, recvy, cols, part):
    count, rows = near_ref.shape[0] // 2, near_ref.shape[1]
    layers = count // cols
    far = group_deposit([(ref, 3 * GROUP * i) for ref in recvy for i in range(3)], cols, count, part)
    far = far[: count // 2] + far[count // 2 :]
    near = (near_ref[:count, :] + near_ref[count:, :]).reshape(layers, cols, rows)
    quarter = cols // 4
    if part == "inner":
        near = near[:, quarter : 3 * quarter]
    else:
        near = jnp.concatenate([near[:, :quarter], near[:, 3 * quarter :]], axis=1)
    return near + far.reshape(layers, cols // 2, rows)


def edge_deposit_kernel(cols, near_ref, after_ref, *refs):
    recvy, (outer_ref, edgea_ref, edgeb_ref) = refs[:-3], refs[-3:]
    outer = half_deposit(near_ref, recvy, cols, "edge")
    outer_ref[...] = outer
    first, last = outer[:, :HALO], outer[:, cols // 2 - HALO :]
    even = lax.rem(lax.axis_index("gx"), 2) == 0
    edgea_ref[...] = jnp.where(even, last, first)
    edgeb_ref[...] = jnp.where(even, first, last)


def inner_deposit_kernel(cols, near_ref, outer_ref, *refs):
    recvy, grid_ref = refs[:-1], refs[-1]
    quarter = cols // 4
    grid_ref[:, :quarter, :] = outer_ref[:, :quarter, :]
    grid_ref[:, 3 * quarter :, :] = outer_ref[:, quarter:, :]
    grid_ref[:, quarter : 3 * quarter, :] = half_deposit(near_ref, recvy, cols, "inner")


def with_columns(own, from_a, from_b):
    a = lax.axis_index("gx")
    even = lax.rem(a, 2) == 0
    right = jnp.where(even, from_a, from_b)
    left = jnp.where(even, from_b, from_a)
    right = jnp.where(a < lax.axis_size("gx") - 1, right, 0.0)
    left = jnp.where(a > 0, left, 0.0)
    return jnp.concatenate([left, own, right], axis=1)


def row_edge(wide, last):
    rows = wide.shape[1]
    tile = jnp.where(last, wide[:, rows - 128 :], wide[:, :128]).T
    return jnp.where(last, tile[128 - HALO :], tile[:HALO])


def put_edges(ref, at, edge):
    extra = edge.shape[1] - WIDE
    ref[at : at + HALO, :] = edge[:, :WIDE]
    ref[at + HALO : at + 2 * HALO, :] = jnp.concatenate(
        [edge[:, WIDE:], jnp.zeros((HALO, WIDE - extra), F32)], axis=1
    )


def get_edges(ref, at, count):
    return jnp.concatenate(
        [ref[at : at + HALO, :], ref[at + HALO : at + 2 * HALO, : count - WIDE]], axis=1
    )


def y_edges(refs, at, wide):
    even = lax.rem(lax.axis_index("gy"), 2) == 0
    for kind, ref in enumerate(refs):
        put_edges(ref, at, row_edge(wide, even if kind == 0 else jnp.logical_not(even)))


def halo_of(ref, cols, layers, top):
    return ref[top:, :].reshape(layers, HALO, ref.shape[1])


def forward_kernel(nyc, recva_ref, recvb_ref, owny_ref, cond_ref, after_ref, *msgy_refs):
    layers, cols, rows = cond_ref.shape
    size, top = 3 * GROUP, nyc * 3 * GROUP
    for y, ref in enumerate(msgy_refs):
        ref[:size, :] = owny_ref[y * size : (y + 1) * size, :]
        ref[size : 2 * size, :] = recva_ref[(y + 1) * size : (y + 2) * size, :]
        ref[2 * size : 3 * size, :] = recvb_ref[(y + 1) * size : (y + 2) * size, :]
    wide = with_columns(
        cond_ref[...], halo_of(recva_ref, cols, layers, top), halo_of(recvb_ref, cols, layers, top)
    )
    y_edges(msgy_refs, 3 * size, wide.reshape(-1, rows))


def power_edge_kernel(grid_ref, froma_ref, fromb_ref, after_ref, *edge_refs):
    wide = with_columns(grid_ref[...], froma_ref[...], fromb_ref[...])
    y_edges(edge_refs, 0, wide.reshape(-1, grid_ref.shape[2]))


def with_rows(wide, edges):
    b, ny = lax.axis_index("gy"), lax.axis_size("gy")
    layers, span, rows = wide.shape
    count = layers * span
    even = lax.rem(b, 2) == 0
    one = edges[0]
    two = edges[1] if len(edges) > 1 else jnp.zeros_like(one)
    after = jnp.where(b < ny - 1, jnp.where(even, one, two), 0.0)
    before = jnp.where(b > 0, jnp.where(even, two, one), 0.0)
    tile = jnp.concatenate([after, jnp.zeros((128 - 2 * HALO, count), F32), before], axis=0).T
    return jnp.concatenate([wide, tile.reshape(layers, span, 128)], axis=2)


def face_kernel(nyc, cond_ref, recva_ref, recvb_ref, coupling_ref, *refs):
    recvy_refs = refs[: nyc - 1]
    cn_ref, cp_ref, rn_ref, fl_ref, d_ref, unit_ref, k_ref = refs[nyc - 1 :]
    layers, cols, rows = cond_ref.shape
    span, wide_rows = cols + 2 * HALO, rows + 128
    count = layers * span
    top = nyc * 3 * GROUP
    sources = [(ref, 3 * GROUP * i) for ref in recvy_refs for i in range(3)]
    count_units(unit_ref, sources, layers, cols * rows)
    a, b = lax.axis_index("gx"), lax.axis_index("gy")
    nx, ny = lax.axis_size("gx"), lax.axis_size("gy")
    k_ref[...] = with_rows(
        with_columns(
            cond_ref[...],
            halo_of(recva_ref, cols, layers, top),
            halo_of(recvb_ref, cols, layers, top),
        ),
        [get_edges(ref, 9 * GROUP, count) for ref in recvy_refs],
    )
    shape = (span, wide_rows)
    c_i = lax.broadcasted_iota(jnp.int32, shape, 0)
    r_i = lax.broadcasted_iota(jnp.int32, shape, 1)
    c_low = jnp.where(a > 0, 0, HALO)
    c_high = jnp.where(a < nx - 1, span, span - HALO)
    r_high = jnp.where(b < ny - 1, rows + HALO, rows)
    r_low = jnp.where(b > 0, wide_rows - HALO, wide_rows)
    inside = jnp.where((c_i >= c_low) & (c_i < c_high) & ((r_i < r_high) | (r_i >= r_low)), 1.0, 0.0)
    next_c = lambda x: pltpu.roll(x, span - 1, 0)
    prev_c = lambda x: pltpu.roll(x, 1, 0)
    next_r = lambda x: pltpu.roll(x, wide_rows - 1, 1)
    prev_r = lambda x: pltpu.roll(x, 1, 1)
    both_c, both_r = inside * next_c(inside), inside * next_r(inside)
    below = None
    for l in range(layers):
        k = k_ref[l]
        face_c, face_r = 0.5 * (k + next_c(k)), 0.5 * (k + next_r(k))
        kept_c, kept_r = face_c * both_c, face_r * both_r
        cn_ref[l], cp_ref[l] = kept_c, prev_c(kept_c)
        rn_ref[l] = kept_r
        total = SINK_RATE + ((face_c + prev_c(face_c)) + (face_r + prev_r(face_r)))
        if below is not None:
            total = total + below
        if l + 1 < layers:
            below = coupling_ref[l] * (0.5 * (k + k_ref[l + 1]))
            fl_ref[l] = below * inside
            total = total + below
        d_ref[l] = total


def solve_kernel(
    nyc, grid_ref, froma_ref, fromb_ref, cn_ref, cp_ref, rn_ref, fl_ref, d_ref, *refs
):
    edge_refs, (warmth_ref, slope_ref, p_ref, v_ref, u_ref) = refs[: nyc - 1], refs[nyc - 1 :]
    layers, cols, rows = grid_ref.shape
    span, wide_rows = cols + 2 * HALO, rows + 128
    p_ref[...] = with_rows(
        with_columns(grid_ref[...], froma_ref[...], fromb_ref[...]),
        [get_edges(ref, 0, layers * span) for ref in edge_refs],
    )
    next_r = lambda x: pltpu.roll(x, wide_rows - 1, 1)
    prev_r = lambda x: pltpu.roll(x, 1, 1)
    middle = 0.5 * (HIGH_BOUND + LOW_BOUND)
    spread = 0.5 * (HIGH_BOUND - LOW_BOUND)
    sigma = middle / spread
    now = 1.0 / sigma
    blank = jnp.zeros((8, wide_rows), F32)
    for l in range(layers):
        for side in range(2):
            v_ref[side, l, :8, :] = blank
            v_ref[side, l, 8 + span :, :] = blank
        v_ref[0, l, 8 : 8 + span, :] = p_ref[l] * (1.0 / middle)
    for sweep in range(ITERS):
        later = 1.0 / (2.0 * sigma - now)
        keep, gain = later * now, 2.0 * later / spread
        old, new = sweep % 2, (sweep + 1) % 2
        for c in range(0, span, 8):
            at, here = slice(c, c + 8), slice(c + 8, c + 16)
            vs = [v_ref[old, l, here, :] for l in range(layers)]
            for l in range(layers):
                v = vs[l]
                rest = p_ref[l, at, :] - d_ref[l, at, :] * v
                rest = rest + cn_ref[l, at, :] * v_ref[old, l, c + 9 : c + 17, :]
                rest = rest + cp_ref[l, at, :] * v_ref[old, l, c + 7 : c + 15, :]
                after = rn_ref[l, at, :]
                rest = rest + (after * next_r(v) + prev_r(after * v))
                if l + 1 < layers:
                    rest = rest + fl_ref[l, at, :] * vs[l + 1]
                if l:
                    rest = rest + fl_ref[l - 1, at, :] * vs[l - 1]
                advance = keep * (u_ref[l, at, :] if sweep else v) + gain * rest
                if sweep + 1 < ITERS:
                    u_ref[l, at, :] = advance
                v_ref[new, l, here, :] = v + advance
        now = later
    final = ITERS % 2
    for l in range(layers):
        warmth_ref[l] = v_ref[final, l, 8 + HALO : 8 + HALO + cols, :rows]
        for c in range(0, cols, 16):
            at = 8 + HALO + c
            v = v_ref[final, l, at : at + 16, :]
            slopes = (
                0.5 * (v_ref[final, l, at + 1 : at + 17, :rows] - v_ref[final, l, at - 1 : at + 15, :rows]),
                0.5 * (next_r(v) - prev_r(v))[:, :rows],
            )
            for f, slope in enumerate(slopes):
                for part, piece in enumerate(pieces(slope)):
                    put = ((l * 2 + part) * 2 + f) * cols + c
                    slope_ref[put : put + 16, :] = piece.astype(BF16)


def pick(found, lc, first):
    cols = found.shape[0] // 4
    here = row_iota(cols, lc.shape[1]) == lc - first
    return [
        jnp.where(here, found[f * cols : (f + 1) * cols] + found[(2 + f) * cols : (3 + f) * cols], 0.0)
        for f in range(2)
    ]


def gather_unit(layers, slope_ref, code, lc, r):
    size = slope_ref.shape[0] // layers
    layer = lax.rem(code, layers)
    rows = slope_ref[pl.ds(pl.multiple_of(layer * size, size), size), :]
    found = dot(rows, onehot(r, slope_ref.shape[1]))
    first = (layer * (size // 4)).astype(F32)
    return [jnp.sum(part, axis=0, keepdims=True) for part in pick(found, lc, first)]


def gather_kernel(layers, sources, slope_ref, unit_ref, *refs):
    ins, out_ref = refs[:-1], refs[-1]
    rows = slope_ref.shape[1]
    for g, (which, at, line) in enumerate(sources):
        totals = [jnp.zeros((GROUP, WIDE), F32)] * 2
        for u in range(GROUP + layers - 1):
            code = unit_ref[line, u]
            row = lax.div(code, layers)
            slots = ins[which][pl.ds(at + row, 1), :]
            lc = jnp.floor(slots * (1.0 / rows))
            hit = row_iota(GROUP, WIDE) == row.astype(F32)
            for f, value in enumerate(gather_unit(layers, slope_ref, code, lc, slots - lc * rows)):
                totals[f] = totals[f] + jnp.where(hit, value, 0.0)
        for f in range(2):
            out_ref[(g * 2 + f) * GROUP : (g * 2 + f + 1) * GROUP, :] = totals[f]


def rank_kernel(layers, cols, table, field_ref, slot_ref, after_ref, place_ref, unit_ref, row_ref, lam_ref):
    size = slot_ref.shape[0]
    span = BLOCK * size // WIDE
    r_i = lax.broadcasted_iota(jnp.int32, (size, size), 0)
    c_i = lax.broadcasted_iota(jnp.int32, (size, size), 1)
    flag = lambda x: jnp.where(x, 1.0, 0.0).astype(BF16)
    upper, ones = flag(r_i < c_i), jnp.ones((size, size), BF16)
    same = (r_i // BLOCK) == (c_i // BLOCK)
    both = jnp.concatenate([flag(same & (r_i > c_i)), flag(same)], axis=1)
    layer = jnp.floor(field_ref[0] * (1.0 / cols))
    ahead = jnp.zeros((size, size), F32)
    rank = jnp.zeros((size, size), F32)
    lane = lax.broadcasted_iota(jnp.int32, (size, size), 1).astype(F32)
    passed = jnp.zeros((size, size), F32)
    for l in range(layers):
        mine = layer == float(l)
        mask = flag(mine)
        totals = dot(mask, ones)
        stack = jnp.concatenate([totals.astype(BF16), ahead.astype(BF16)], axis=0)
        rank = jnp.where(mine, dot(mask, upper) + dot(both, stack), rank)
        ahead = ahead + totals
        if l + 1 < layers:
            end = jnp.floor(dot(both[:, size:], ahead.astype(BF16)) * (1.0 / WIDE))
            passed = passed + jnp.where(jnp.minimum(end, span - 1.0) + l < lane, 1.0, 0.0)
    unit = ((lane - passed) * layers + passed).astype(jnp.int32)
    for k in range(size // BLOCK):
        unit_ref[k : k + 1, :] = unit[k * BLOCK : k * BLOCK + 1]
    row = jnp.floor(rank * (1.0 / WIDE))
    lam = rank - row * WIDE
    slot = slot_ref[...]
    place_ref[...] = jnp.where(slot >= 0.0, slot, (row + layer + table) * WIDE + lam)
    row_ref[...], lam_ref[...] = row, lam


def sort_kernel(field_ref, row_ref, lam_ref, after_ref, order_ref):
    size = row_ref.shape[0]
    span = BLOCK * size // WIDE
    row, lam = row_ref[...], lam_ref[...]
    for k in range(size // BLOCK):
        picks, marks = [], []
        for i in range(k * BLOCK, (k + 1) * BLOCK):
            hit = row_iota(span) == row[i : i + 1]
            picks.append(
                jnp.concatenate(
                    [jnp.where(hit, field_ref[f, i : i + 1, :], 0.0) for f in range(2)], axis=0
                ).astype(BF16)
            )
            marks.append(onehot(lam[i : i + 1], WIDE))
        sorted_rows = transposed_dot(lanes(picks), lanes(marks))
        for f in range(2):
            order_ref[f, k * span : (k + 1) * span, :] = sorted_rows[f * span : (f + 1) * span]


def stay_gather_kernel(layers, start, slope_ref, order_ref, unit_ref, out_ref):
    span = order_ref.shape[1] // unit_ref.shape[0]
    units = span + layers

    def body(j, carry):
        k = j + start
        for u in range(units - 1):
            code = unit_ref[k, u]
            at = k * span + lax.div(code, layers)
            lc, r = order_ref[0, pl.ds(at, 1), :], order_ref[1, pl.ds(at, 1), :]
            for f, value in enumerate(gather_unit(layers, slope_ref, code, lc, r)):
                out_ref[j, f * units + u : f * units + u + 1, :] = value
        for f in range(2):
            out_ref[j, (f + 1) * units - 1 : (f + 1) * units, :] = jnp.zeros((1, WIDE), F32)
        return carry

    lax.fori_loop(0, out_ref.shape[0], body, 0)


def reply_kernel(nyc, near_ref, after_ref, *refs):
    size = 2 * GROUP
    backs, (a_ref, b_ref) = refs[: nyc - 1], refs[nyc - 1 :]
    a_ref[:size, :] = near_ref[:size, :]
    b_ref[:size, :] = near_ref[size:, :]
    for y, ref in enumerate(backs):
        a_ref[(y + 1) * size : (y + 2) * size, :] = ref[size : 2 * size, :]
        b_ref[(y + 1) * size : (y + 2) * size, :] = ref[2 * size : 3 * size, :]


def unpack_kernel(nyc, backa_ref, backb_ref, *refs):
    backy = refs[: nyc - 1]
    early_ref, late_ref, place_ref, power_ref, out_ref, table_ref = refs[nyc - 1 :]
    groups = [(backa_ref, y) for y in range(nyc)] + [(backb_ref, y) for y in range(nyc)]
    groups += [(ref, 0) for ref in backy]
    sent, units = len(groups) * GROUP, early_ref.shape[1] // 2
    table = sent + units
    for f in range(2):
        whole = jnp.concatenate(
            [ref[(2 * at + f) * GROUP : (2 * at + f + 1) * GROUP, :] for ref, at in groups], axis=0
        )
        for part, piece in enumerate(pieces(whole)):
            at = (part * 2 + f) * table
            table_ref[at : at + sent, :] = piece

    def body(stay_ref, start, k, carry):
        base = pl.multiple_of((k + start) * BLOCK, BLOCK)
        for f in range(2):
            for part, piece in enumerate(pieces(stay_ref[k, f * units : (f + 1) * units, :])):
                at = (part * 2 + f) * table + sent
                table_ref[at : at + units, :] = piece
        source = table_ref[...].astype(BF16)
        places = place_ref[pl.ds(base, BLOCK), :]
        qs = jnp.floor(places * (1.0 / WIDE))
        lams = places - qs * WIDE
        powers = power_ref[pl.ds(base, BLOCK), :]
        for i in range(0, BLOCK, 8):
            many = lambda x: lanes([x[i + j : i + j + 1] for j in range(8)])
            at = pl.multiple_of(base * 128 + i * 128, 1024)
            found = dot(source, onehot(many(lams), WIDE))
            here = row_iota(table, 1024) == many(qs)
            for f in range(2):
                both = found[f * table : (f + 1) * table] + found[(2 + f) * table : (3 + f) * table]
                value = jnp.sum(jnp.where(here, both, 0.0), axis=0, keepdims=True)
                out_ref[f : f + 1, pl.ds(at, 1024)] = -many(powers) * value
        return carry

    early = early_ref.shape[0]
    lax.fori_loop(0, early, functools.partial(body, early_ref, 0), 0)
    lax.fori_loop(0, late_ref.shape[0], functools.partial(body, late_ref, early), 0)


def call(kernel, outs, scratch, *args, spaces={}):
    space = pl.BlockSpec(memory_space=pltpu.VMEM)
    specs = [pl.BlockSpec(memory_space=spaces.get(i, pltpu.VMEM)) for i in range(len(args))]
    shapes = [jax.ShapeDtypeStruct(shape, dtype) for shape, dtype in outs]
    return pl.pallas_call(
        kernel,
        out_shape=shapes,
        in_specs=specs,
        out_specs=[space] * len(shapes),
        scratch_shapes=scratch,
        compiler_params=pltpu.CompilerParams(vmem_limit_bytes=48 * 1024 * 1024),
    )(*args)


def shards(
    cell_bin, cell_layer, cell_offset, cell_power, spill_weight, conductivity, layer_coupling
):
    layers, cols, rows = conductivity.shape
    cells = cell_bin.shape[0]
    nyc = 2 if lax.axis_size("gy") == 2 else 3
    count = layers * cols
    groups = 3 * nyc - 1
    flat = lambda x: x.reshape(cells // 128, 128)
    bins, layer, off = flat(cell_bin), flat(cell_layer), flat(cell_offset)
    power, spill = flat(cell_power), flat(spill_weight)
    square = bins.shape
    split = square[0] * 3 // 4
    own = 3 * GROUP
    message = (nyc * own + layers * HALO, WIDE)
    vmem = lambda *shape: pltpu.VMEM(shape, F32)
    partial = functools.partial

    tile = conductivity.shape
    msg_a, msg_b, own_y, slot, fields, power = call(
        partial(pack_kernel, nyc, layers, cols, rows),
        [
            (message, F32), (message, F32), (((nyc - 1) * own, WIDE), F32),
            (square, F32), ((6, *square), F32), (square, F32),
        ],
        [pltpu.VMEM(square, jnp.int32)] * 3
        + [
            vmem(*square), vmem(2, layers, HALO, rows), pltpu.SemaphoreType.DMA((7,)),
            vmem(6 * groups * GROUP, WIDE),
        ],
        *[
            pltpu.with_memory_space_constraint(x, pltpu.HBM)
            for x in (bins, layer, off, power, spill, conductivity)
        ],
        spaces={i: pltpu.HBM for i in range(6)},
    )
    recv_a, recv_b = exchange(msg_a, 1, 0), exchange(msg_b, 2, 0)
    (stay_grid,) = call(
        partial(stay_deposit_kernel, cols, split),
        [((2 * count, rows), F32)],
        [],
        fields, slot,
    )
    msg_y = call(
        partial(forward_kernel, nyc),
        [((3 * own + 2 * HALO, WIDE), F32)] * (nyc - 1),
        [],
        recv_a, recv_b, own_y, conductivity, stay_grid,
        spaces={4: pl.ANY},
    )
    recv_y = [exchange(m, 0, i + 1) for i, m in enumerate(msg_y)]
    near_grid, near_unit = call(
        partial(near_deposit_kernel, cols, split),
        [((2 * count, rows), F32), ((8, 128), jnp.int32)],
        [],
        stay_grid, recv_a, recv_b, fields, slot,
    )
    table = groups * GROUP
    place, unit, row, lam = call(
        partial(rank_kernel, layers, cols, table),
        [(square, F32), ((square[0] // BLOCK, 128), jnp.int32), (square, F32), (square, F32)],
        [],
        fields, slot, near_grid,
        spaces={2: pl.ANY},
    )
    edge = (layers, HALO, rows)
    outer, edge_a, edge_b = call(
        partial(edge_deposit_kernel, cols),
        [((layers, cols // 2, rows), F32), (edge, F32), (edge, F32)],
        [],
        near_grid, row, *recv_y,
        spaces={1: pl.ANY},
    )
    from_a, from_b = exchange(edge_a, 1, 0), exchange(edge_b, 2, 0)
    (grid,) = call(
        partial(inner_deposit_kernel, cols), [(tile, F32)], [], near_grid, outer, *recv_y
    )
    (order,) = call(
        sort_kernel,
        [((2, cells // WIDE, WIDE), F32)],
        [],
        fields, row, lam, grid,
        spaces={3: pl.ANY},
    )
    edges = call(
        power_edge_kernel,
        [((2 * HALO, WIDE), F32)] * (nyc - 1),
        [],
        grid, from_a, from_b, order,
        spaces={3: pl.ANY},
    )
    from_y = [exchange(e, 0, i + 1) for i, e in enumerate(edges)]
    big = (layers, cols + 2 * HALO, rows + 128)
    *faces, far_unit = call(
        partial(face_kernel, nyc),
        [(big, F32)] * 5 + [((8, 128), jnp.int32)],
        [vmem(*big)],
        conductivity, recv_a, recv_b, layer_coupling, *recv_y,
        spaces={3: pltpu.SMEM},
    )
    final_warmth, slope = call(
        partial(solve_kernel, nyc),
        [(tile, F32), ((4 * count, rows), BF16)],
        [vmem(*big), vmem(2, layers, big[1] + 16, big[2]), vmem(*big)],
        grid, from_a, from_b, *faces, *from_y,
    )
    answer_y = [
        call(
            partial(gather_kernel, layers, [(0, own * i, 3 * y + i) for i in range(3)]),
            [((6 * GROUP, WIDE), F32)],
            [],
            slope, far_unit, r,
            spaces={1: pltpu.SMEM},
        )[0]
        for y, r in enumerate(recv_y)
    ]
    back_y = [exchange(m, 0, i + 1) for i, m in enumerate(answer_y)]
    (near_answer,) = call(
        partial(gather_kernel, layers, [(0, 0, 0), (1, 0, 1)]),
        [((4 * GROUP, WIDE), F32)],
        [],
        slope, near_unit, recv_a, recv_b,
        spaces={1: pltpu.SMEM},
    )
    blocks, early = square[0] // BLOCK, 1
    units = order.shape[1] // blocks + layers
    stay_values = [
        functools.partial(
            call,
            partial(stay_gather_kernel, layers, start),
            [((size, 2 * units, WIDE), F32)],
            [],
            slope, order, unit,
            spaces={2: pltpu.SMEM},
        )
        for start, size in ((0, early), (early, blocks - early))
    ]
    (early_value,) = stay_values[0]()
    answer_a, answer_b = call(
        partial(reply_kernel, nyc),
        [((2 * nyc * GROUP, WIDE), F32)] * 2,
        [],
        near_answer, early_value, *back_y,
        spaces={1: pl.ANY},
    )
    back_a, back_b = exchange(answer_a, 1, 0), exchange(answer_b, 2, 0)
    (late_value,) = stay_values[1]()
    (pull,) = call(
        partial(unpack_kernel, nyc),
        [((2, cells), F32)],
        [vmem(4 * (table + units), WIDE)],
        back_a, back_b, *back_y, early_value, late_value, place, power,
    )
    return final_warmth, pull


def solution(mesh):
    cell = P(("gx", "gy"))
    tile = P(None, "gx", "gy")
    return jax.shard_map(
        shards,
        mesh=mesh,
        in_specs=(cell, cell, cell, cell, cell, tile, P()),
        out_specs=(tile, P(None, ("gx", "gy"))),
        check_vma=False,
    )
```

```python
import functools

import jax
import jax.numpy as jnp
from jax import lax
from jax.experimental import pallas as pl
from jax.experimental.pallas import tpu as pltpu
from jax.sharding import PartitionSpec as P

ITERS = 4
CAP = 2048
SINK_RATE = 0.5
LOW_BOUND = 0.5
HIGH_BOUND = 33.0

WIDE = 256
GROUP = CAP // WIDE
BLOCK = 32
HALO = 8
F32, BF16 = jnp.float32, jnp.bfloat16


def partner(place, kind, count):
    if kind == 0:
        return place
    if kind == 1:
        return place ^ 1
    other = place - 1 if place % 2 == 0 else place + 1
    return other if 0 <= other < count else None


def exchange(value, x_kind, y_kind):
    nx, ny = lax.axis_size("gx"), lax.axis_size("gy")
    pairs = []
    for a in range(nx):
        for b in range(ny):
            x, y = partner(a, x_kind, nx), partner(b, y_kind, ny)
            if x is None:
                x, y = a, b ^ 1
            elif y is None:
                x, y = a ^ 1, b
            pairs.append((a * ny + b, x * ny + y))
    return lax.ppermute(value, ("gx", "gy"), pairs)


def pieces(value):
    high = value.astype(BF16).astype(F32)
    return high, value - high


def row_iota(count, width=128):
    return lax.broadcasted_iota(jnp.int32, (count, width), 0).astype(F32)


def onehot(row, count):
    return jnp.where(
        row_iota(count, row.shape[1]).astype(BF16) == row.astype(BF16),
        jnp.ones((), BF16),
        jnp.zeros((), BF16),
    )


def lanes(parts):
    return jnp.concatenate(parts, axis=1) if len(parts) > 1 else parts[0]


def transposed_dot(left, right):
    return lax.dot_general(left, right, (((1,), (1,)), ((), ())), preferred_element_type=F32)


def dot(left, right):
    return lax.dot_general(left, right, (((1,), (0,)), ((), ())), preferred_element_type=F32)


def kind_of(step, place):
    ahead = 1 - 2 * lax.rem(place, 2)
    return jnp.where(step == 0, 0, jnp.where(step == ahead, 1, 2))


def pack_kernel(
    nyc, layers, cols, rows,
    bin_hbm, layer_hbm, off_hbm, power_hbm, spill_hbm, cond_hbm,
    msga_ref, msgb_ref, owny_ref, slot_ref, field_ref, power_ref,
    bin_ref, layer_ref, off_ref, spill_ref, edge_ref, sems, acc_ref,
):
    a, b = lax.axis_index("gx"), lax.axis_index("gy")
    copies = [
        pltpu.make_async_copy(src, dst, sems.at[i])
        for i, (src, dst) in enumerate(
            [
                (off_hbm, off_ref), (layer_hbm, layer_ref), (bin_hbm, bin_ref),
                (power_hbm, power_ref), (spill_hbm, spill_ref),
                (cond_hbm.at[:, :HALO, :], edge_ref.at[0]),
                (cond_hbm.at[:, cols - HALO :, :], edge_ref.at[1]),
            ]
        )
    ]
    for copy in copies:
        copy.start()
    acc_ref[...] = jnp.zeros_like(acc_ref)
    groups = 3 * nyc - 1
    table = groups * GROUP
    copies[0].wait()
    copies[1].wait()
    off = off_ref[...]
    col_code = (off >= 3).astype(jnp.int32) + (off >= 6).astype(jnp.int32)
    x_kind = kind_of(col_code - 1, a)
    y_kind = kind_of(off - 3 * col_code - 1, b)
    group = jnp.where(x_kind > 0, (x_kind - 1) * nyc + y_kind, 2 * nyc - 1 + y_kind)
    key = jnp.where(off == 4, -1, group * layers + layer_ref[...])
    size = off.shape[0]
    r_i = lax.broadcasted_iota(jnp.int32, (size, size), 0)
    c_i = lax.broadcasted_iota(jnp.int32, (size, size), 1)
    flag = lambda x: jnp.where(x, 1.0, 0.0).astype(BF16)
    ones = jnp.ones((size, size), BF16)
    before = jnp.concatenate([flag(r_i < c_i), ones], axis=1)
    rank = jnp.zeros((size, size), F32)
    counts = jnp.zeros((size, size), F32)
    for g in range(groups):
        keys = range(g * layers, (g + 1) * layers)
        counted = dot(jnp.concatenate([flag(key == k) for k in keys], axis=0), before)
        for i, k in enumerate(keys):
            block = counted[i * size : (i + 1) * size]
            rank = jnp.where(key == k, block[:, :size], rank)
            counts = jnp.where(c_i == k, block[:, size:], counts)
    narrow = counts.astype(BF16)
    ahead = dot(narrow, flag((r_i // layers == c_i // layers) & (r_i < c_i))).astype(BF16)
    base = dot(
        jnp.concatenate([flag(r_i > c_i), ones], axis=1), jnp.concatenate([narrow, ahead], axis=0)
    )
    base = jnp.take_along_axis(base, jnp.maximum(key, 0), axis=1, mode="promise_in_bounds")
    slot = jnp.where(key >= 0, rank + base + (group * CAP).astype(F32), -1.0)
    slot_ref[...] = slot
    for copy in copies[2:]:
        copy.wait()
    code = layer_ref[...] * (cols * rows) + bin_ref[...]
    field_ref[0] = (code // rows).astype(F32)
    field_ref[1] = (code % rows).astype(F32)
    power = power_ref[...]
    spill = spill_ref[...]
    field_ref[2], field_ref[3] = pieces(power * (1.0 - spill))
    field_ref[4], field_ref[5] = pieces(power * spill)
    step = 64

    def body(j, carry):
        base = pl.multiple_of(j * step, step)
        slots = slot_ref[pl.ds(base, step), :]
        qs = jnp.floor(slots * (1.0 / WIDE))
        lams = slots - qs * WIDE
        vals = [field_ref[f, pl.ds(base, step), :] for f in range(6)]
        picks, marks = [], []
        for i in range(step):
            hit = row_iota(table) == qs[i : i + 1]
            picks.append(
                jnp.concatenate([jnp.where(hit, v[i : i + 1], 0.0) for v in vals], axis=0).astype(BF16)
            )
            marks.append(onehot(lams[i : i + 1], WIDE))
        acc_ref[...] += transposed_dot(lanes(picks), lanes(marks))
        return carry

    lax.fori_loop(0, size // step, body, 0)
    out = [acc_ref[f * table : (f + 1) * table, :] for f in range(6)]
    sent = [out[0] * float(rows) + out[1], out[2] + out[3], out[4] + out[5]]

    def put(ref, at, g):
        for f in range(3):
            ref[(at * 3 + f) * GROUP : (at * 3 + f + 1) * GROUP, :] = sent[f][
                g * GROUP : (g + 1) * GROUP
            ]

    for y in range(nyc):
        put(msga_ref, y, y)
        put(msgb_ref, y, nyc + y)
        if y:
            put(owny_ref, y - 1, 2 * nyc + y - 1)
    first, last = edge_ref[0], edge_ref[1]
    even = lax.rem(a, 2) == 0
    top = nyc * 3 * GROUP
    flat = (-1, rows)
    msga_ref[top:, :] = jnp.where(even, last, first).reshape(flat)
    msgb_ref[top:, :] = jnp.where(even, first, last).reshape(flat)


def deposit_block(lc, r, main, spill, cols, cells, part=None):
    picks, marks = [], []
    zero = jnp.zeros((), BF16)
    narrow = lambda x: x.astype(BF16)
    quarter = cols // 4
    count = cells if part is None else cells // 2
    for lc_i, r_i, (mh, ml), (sh, sl) in zip(lc, r, main, spill):
        spot = narrow(row_iota(count, lc_i.shape[1]))
        step = cols
        other = lambda at: jnp.where(lc_i >= float(cells - cols), at - step, at + step)
        if part is None:
            there_i = other(lc_i)
        else:
            step = cols // 2
            layer = jnp.floor(lc_i * (1.0 / cols))
            column = lc_i - layer * cols
            inner = (column >= quarter) & (column < 3 * quarter)
            if part == "inner":
                mine, at = inner, layer * step + (column - quarter)
            else:
                mine = jnp.logical_not(inner)
                at = layer * step + jnp.where(column < quarter, column, column - step)
            there_i = jnp.where(mine, other(at), -1.0)
            lc_i = jnp.where(mine, at, -1.0)
        here, there = spot == narrow(lc_i), spot == narrow(there_i)
        high = jnp.where(here, narrow(mh), jnp.where(there, narrow(sh), zero))
        low = jnp.where(here, narrow(ml), jnp.where(there, narrow(sl), zero))
        picks.append(jnp.concatenate([high, low], axis=0))
        marks.append(onehot(r_i, WIDE))
    return transposed_dot(lanes(picks), lanes(marks))


def deposit_stays(grid_ref, field_ref, slot_ref, first, last, cols):
    count, step = grid_ref.shape[0] // 2, 32
    stays = slot_ref[first:last, :] < 0.0
    vals = [jnp.where(stays, field_ref[2 + f, first:last, :], 0.0) for f in range(4)]
    lcs, rs = field_ref[0, first:last, :], field_ref[1, first:last, :]
    for base in range(0, last - first, step):
        rows_of = lambda x: [x[base + i : base + i + 1] for i in range(step)]
        parts = [rows_of(v) for v in vals]
        grid_ref[...] += deposit_block(
            rows_of(lcs), rows_of(rs), list(zip(parts[0], parts[1])),
            list(zip(parts[2], parts[3])), cols, count,
        )


def stay_deposit_kernel(cols, split, field_ref, slot_ref, grid_ref):
    grid_ref[...] = jnp.zeros_like(grid_ref)
    deposit_stays(grid_ref, field_ref, slot_ref, 0, split, cols)


def group_deposit(sources, cols, count, part=None):
    lc, r, main, spill = [], [], [], []
    for ref, at in sources:
        rows = ref.shape[1]
        for row in range(at, at + GROUP):
            code = ref[row : row + 1, :]
            lc_i = jnp.floor(code * (1.0 / rows))
            lc.append(lc_i)
            r.append(code - lc_i * rows)
            main.append(pieces(ref[row + GROUP : row + GROUP + 1, :]))
            spill.append(pieces(ref[row + 2 * GROUP : row + 2 * GROUP + 1, :]))
    return deposit_block(lc, r, main, spill, cols, count, part)


def count_units(unit_ref, sources, layers, cells):
    unit_ref[...] = jnp.zeros_like(unit_ref)
    lane = lax.broadcasted_iota(jnp.int32, (1, 128), 1).astype(F32)
    for g, (ref, at) in enumerate(sources):
        layer = jnp.floor(ref[at : at + GROUP, :] * (1.0 / cells))
        layer = jnp.where(ref[at + GROUP : at + 2 * GROUP, :] > 0.0, layer, float(layers))
        passed = jnp.zeros((1, 128), F32)
        for l in range(layers - 1):
            end = jnp.sum(jnp.where(layer <= l, 1.0, 0.0), axis=0, keepdims=True)
            end = jnp.floor(jnp.sum(end, axis=1, keepdims=True) * (1.0 / WIDE))
            passed = passed + jnp.where(jnp.minimum(end, GROUP - 1.0) + l < lane, 1.0, 0.0)
        unit_ref[g : g + 1, :] = ((lane - passed) * layers + passed).astype(jnp.int32)


def near_deposit_kernel(
    cols, split, stay_ref, recva_ref, recvb_ref, field_ref, slot_ref, grid_ref, unit_ref
):
    count, rows = grid_ref.shape[0] // 2, grid_ref.shape[1]
    count_units(unit_ref, [(recva_ref, 0), (recvb_ref, 0)], count // cols, cols * rows)
    grid_ref[...] = stay_ref[...]
    deposit_stays(grid_ref, field_ref, slot_ref, split, slot_ref.shape[0], cols)
    grid_ref[...] += group_deposit([(recva_ref, 0), (recvb_ref, 0)], cols, count)


def half_deposit(near_ref, recvy, cols, part):
    count, rows = near_ref.shape[0] // 2, near_ref.shape[1]
    layers = count // cols
    far = group_deposit([(ref, 3 * GROUP * i) for ref in recvy for i in range(3)], cols, count, part)
    far = far[: count // 2] + far[count // 2 :]
    near = (near_ref[:count, :] + near_ref[count:, :]).reshape(layers, cols, rows)
    quarter = cols // 4
    if part == "inner":
        near = near[:, quarter : 3 * quarter]
    else:
        near = jnp.concatenate([near[:, :quarter], near[:, 3 * quarter :]], axis=1)
    return near + far.reshape(layers, cols // 2, rows)


def edge_deposit_kernel(cols, near_ref, after_ref, *refs):
    recvy, (outer_ref, edgea_ref, edgeb_ref) = refs[:-3], refs[-3:]
    outer = half_deposit(near_ref, recvy, cols, "edge")
    outer_ref[...] = outer
    first, last = outer[:, :HALO], outer[:, cols // 2 - HALO :]
    even = lax.rem(lax.axis_index("gx"), 2) == 0
    edgea_ref[...] = jnp.where(even, last, first)
    edgeb_ref[...] = jnp.where(even, first, last)


def inner_deposit_kernel(cols, near_ref, outer_ref, *refs):
    recvy, grid_ref = refs[:-1], refs[-1]
    quarter = cols // 4
    grid_ref[:, :quarter, :] = outer_ref[:, :quarter, :]
    grid_ref[:, 3 * quarter :, :] = outer_ref[:, quarter:, :]
    grid_ref[:, quarter : 3 * quarter, :] = half_deposit(near_ref, recvy, cols, "inner")


def with_columns(own, from_a, from_b):
    a = lax.axis_index("gx")
    even = lax.rem(a, 2) == 0
    right = jnp.where(even, from_a, from_b)
    left = jnp.where(even, from_b, from_a)
    right = jnp.where(a < lax.axis_size("gx") - 1, right, 0.0)
    left = jnp.where(a > 0, left, 0.0)
    return jnp.concatenate([left, own, right], axis=1)


def row_edge(wide, last):
    rows = wide.shape[1]
    tile = jnp.where(last, wide[:, rows - 128 :], wide[:, :128]).T
    return jnp.where(last, tile[128 - HALO :], tile[:HALO])


def put_edges(ref, at, edge):
    extra = edge.shape[1] - WIDE
    ref[at : at + HALO, :] = edge[:, :WIDE]
    ref[at + HALO : at + 2 * HALO, :] = jnp.concatenate(
        [edge[:, WIDE:], jnp.zeros((HALO, WIDE - extra), F32)], axis=1
    )


def get_edges(ref, at, count):
    return jnp.concatenate(
        [ref[at : at + HALO, :], ref[at + HALO : at + 2 * HALO, : count - WIDE]], axis=1
    )


def y_edges(refs, at, wide):
    even = lax.rem(lax.axis_index("gy"), 2) == 0
    for kind, ref in enumerate(refs):
        put_edges(ref, at, row_edge(wide, even if kind == 0 else jnp.logical_not(even)))


def halo_of(ref, cols, layers, top):
    return ref[top:, :].reshape(layers, HALO, ref.shape[1])


def forward_kernel(nyc, recva_ref, recvb_ref, owny_ref, cond_ref, after_ref, *msgy_refs):
    layers, cols, rows = cond_ref.shape
    size, top = 3 * GROUP, nyc * 3 * GROUP
    for y, ref in enumerate(msgy_refs):
        ref[:size, :] = owny_ref[y * size : (y + 1) * size, :]
        ref[size : 2 * size, :] = recva_ref[(y + 1) * size : (y + 2) * size, :]
        ref[2 * size : 3 * size, :] = recvb_ref[(y + 1) * size : (y + 2) * size, :]
    wide = with_columns(
        cond_ref[...], halo_of(recva_ref, cols, layers, top), halo_of(recvb_ref, cols, layers, top)
    )
    y_edges(msgy_refs, 3 * size, wide.reshape(-1, rows))


def power_edge_kernel(grid_ref, froma_ref, fromb_ref, after_ref, *edge_refs):
    wide = with_columns(grid_ref[...], froma_ref[...], fromb_ref[...])
    y_edges(edge_refs, 0, wide.reshape(-1, grid_ref.shape[2]))


def with_rows(wide, edges):
    b, ny = lax.axis_index("gy"), lax.axis_size("gy")
    layers, span, rows = wide.shape
    count = layers * span
    even = lax.rem(b, 2) == 0
    one = edges[0]
    two = edges[1] if len(edges) > 1 else jnp.zeros_like(one)
    after = jnp.where(b < ny - 1, jnp.where(even, one, two), 0.0)
    before = jnp.where(b > 0, jnp.where(even, two, one), 0.0)
    tile = jnp.concatenate([after, jnp.zeros((128 - 2 * HALO, count), F32), before], axis=0).T
    return jnp.concatenate([wide, tile.reshape(layers, span, 128)], axis=2)


def face_kernel(nyc, cond_ref, recva_ref, recvb_ref, coupling_ref, *refs):
    recvy_refs = refs[: nyc - 1]
    cn_ref, cp_ref, rn_ref, fl_ref, d_ref, unit_ref, k_ref = refs[nyc - 1 :]
    layers, cols, rows = cond_ref.shape
    span, wide_rows = cols + 2 * HALO, rows + 128
    count = layers * span
    top = nyc * 3 * GROUP
    sources = [(ref, 3 * GROUP * i) for ref in recvy_refs for i in range(3)]
    count_units(unit_ref, sources, layers, cols * rows)
    a, b = lax.axis_index("gx"), lax.axis_index("gy")
    nx, ny = lax.axis_size("gx"), lax.axis_size("gy")
    k_ref[...] = with_rows(
        with_columns(
            cond_ref[...],
            halo_of(recva_ref, cols, layers, top),
            halo_of(recvb_ref, cols, layers, top),
        ),
        [get_edges(ref, 9 * GROUP, count) for ref in recvy_refs],
    )
    shape = (span, wide_rows)
    c_i = lax.broadcasted_iota(jnp.int32, shape, 0)
    r_i = lax.broadcasted_iota(jnp.int32, shape, 1)
    c_low = jnp.where(a > 0, 0, HALO)
    c_high = jnp.where(a < nx - 1, span, span - HALO)
    r_high = jnp.where(b < ny - 1, rows + HALO, rows)
    r_low = jnp.where(b > 0, wide_rows - HALO, wide_rows)
    inside = jnp.where((c_i >= c_low) & (c_i < c_high) & ((r_i < r_high) | (r_i >= r_low)), 1.0, 0.0)
    next_c = lambda x: pltpu.roll(x, span - 1, 0)
    prev_c = lambda x: pltpu.roll(x, 1, 0)
    next_r = lambda x: pltpu.roll(x, wide_rows - 1, 1)
    prev_r = lambda x: pltpu.roll(x, 1, 1)
    both_c, both_r = inside * next_c(inside), inside * next_r(inside)
    below = None
    for l in range(layers):
        k = k_ref[l]
        face_c, face_r = 0.5 * (k + next_c(k)), 0.5 * (k + next_r(k))
        kept_c, kept_r = face_c * both_c, face_r * both_r
        cn_ref[l], cp_ref[l] = kept_c, prev_c(kept_c)
        rn_ref[l] = kept_r
        total = SINK_RATE + ((face_c + prev_c(face_c)) + (face_r + prev_r(face_r)))
        if below is not None:
            total = total + below
        if l + 1 < layers:
            below = coupling_ref[l] * (0.5 * (k + k_ref[l + 1]))
            fl_ref[l] = below * inside
            total = total + below
        d_ref[l] = total


def solve_kernel(
    nyc, grid_ref, froma_ref, fromb_ref, cn_ref, cp_ref, rn_ref, fl_ref, d_ref, *refs
):
    edge_refs, (warmth_ref, slope_ref, p_ref, v_ref, u_ref) = refs[: nyc - 1], refs[nyc - 1 :]
    layers, cols, rows = grid_ref.shape
    span, wide_rows = cols + 2 * HALO, rows + 128
    p_ref[...] = with_rows(
        with_columns(grid_ref[...], froma_ref[...], fromb_ref[...]),
        [get_edges(ref, 0, layers * span) for ref in edge_refs],
    )
    next_r = lambda x: pltpu.roll(x, wide_rows - 1, 1)
    prev_r = lambda x: pltpu.roll(x, 1, 1)
    middle = 0.5 * (HIGH_BOUND + LOW_BOUND)
    spread = 0.5 * (HIGH_BOUND - LOW_BOUND)
    sigma = middle / spread
    now = 1.0 / sigma
    blank = jnp.zeros((8, wide_rows), F32)
    for l in range(layers):
        for side in range(2):
            v_ref[side, l, :8, :] = blank
            v_ref[side, l, 8 + span :, :] = blank
        v_ref[0, l, 8 : 8 + span, :] = p_ref[l] * (1.0 / middle)
    for sweep in range(ITERS):
        later = 1.0 / (2.0 * sigma - now)
        keep, gain = later * now, 2.0 * later / spread
        old, new = sweep % 2, (sweep + 1) % 2
        for c in range(0, span, 8):
            at, here = slice(c, c + 8), slice(c + 8, c + 16)
            vs = [v_ref[old, l, here, :] for l in range(layers)]
            for l in range(layers):
                v = vs[l]
                rest = p_ref[l, at, :] - d_ref[l, at, :] * v
                rest = rest + cn_ref[l, at, :] * v_ref[old, l, c + 9 : c + 17, :]
                rest = rest + cp_ref[l, at, :] * v_ref[old, l, c + 7 : c + 15, :]
                after = rn_ref[l, at, :]
                rest = rest + (after * next_r(v) + prev_r(after * v))
                if l + 1 < layers:
                    rest = rest + fl_ref[l, at, :] * vs[l + 1]
                if l:
                    rest = rest + fl_ref[l - 1, at, :] * vs[l - 1]
                advance = keep * (u_ref[l, at, :] if sweep else v) + gain * rest
                if sweep + 1 < ITERS:
                    u_ref[l, at, :] = advance
                v_ref[new, l, here, :] = v + advance
        now = later
    final = ITERS % 2
    for l in range(layers):
        warmth_ref[l] = v_ref[final, l, 8 + HALO : 8 + HALO + cols, :rows]
        for c in range(0, cols, 16):
            at = 8 + HALO + c
            v = v_ref[final, l, at : at + 16, :]
            slopes = (
                0.5 * (v_ref[final, l, at + 1 : at + 17, :rows] - v_ref[final, l, at - 1 : at + 15, :rows]),
                0.5 * (next_r(v) - prev_r(v))[:, :rows],
            )
            for f, slope in enumerate(slopes):
                for part, piece in enumerate(pieces(slope)):
                    put = ((l * 2 + part) * 2 + f) * cols + c
                    slope_ref[put : put + 16, :] = piece.astype(BF16)


def pick(found, lc, first):
    cols = found.shape[0] // 4
    here = row_iota(cols, lc.shape[1]) == lc - first
    return [
        jnp.where(here, found[f * cols : (f + 1) * cols] + found[(2 + f) * cols : (3 + f) * cols], 0.0)
        for f in range(2)
    ]


def gather_unit(layers, slope_ref, code, lc, r):
    size = slope_ref.shape[0] // layers
    layer = lax.rem(code, layers)
    rows = slope_ref[pl.ds(pl.multiple_of(layer * size, size), size), :]
    found = dot(rows, onehot(r, slope_ref.shape[1]))
    first = (layer * (size // 4)).astype(F32)
    return [jnp.sum(part, axis=0, keepdims=True) for part in pick(found, lc, first)]


def gather_kernel(layers, sources, slope_ref, unit_ref, *refs):
    ins, out_ref = refs[:-1], refs[-1]
    rows = slope_ref.shape[1]
    for g, (which, at, line) in enumerate(sources):
        totals = [jnp.zeros((GROUP, WIDE), F32)] * 2
        for u in range(GROUP + layers - 1):
            code = unit_ref[line, u]
            row = lax.div(code, layers)
            slots = ins[which][pl.ds(at + row, 1), :]
            lc = jnp.floor(slots * (1.0 / rows))
            hit = row_iota(GROUP, WIDE) == row.astype(F32)
            for f, value in enumerate(gather_unit(layers, slope_ref, code, lc, slots - lc * rows)):
                totals[f] = totals[f] + jnp.where(hit, value, 0.0)
        for f in range(2):
            out_ref[(g * 2 + f) * GROUP : (g * 2 + f + 1) * GROUP, :] = totals[f]


def rank_kernel(layers, cols, table, field_ref, slot_ref, after_ref, place_ref, unit_ref, row_ref, lam_ref):
    size = slot_ref.shape[0]
    span = BLOCK * size // WIDE
    r_i = lax.broadcasted_iota(jnp.int32, (size, size), 0)
    c_i = lax.broadcasted_iota(jnp.int32, (size, size), 1)
    flag = lambda x: jnp.where(x, 1.0, 0.0).astype(BF16)
    upper, ones = flag(r_i < c_i), jnp.ones((size, size), BF16)
    same = (r_i // BLOCK) == (c_i // BLOCK)
    both = jnp.concatenate([flag(same & (r_i > c_i)), flag(same)], axis=1)
    layer = jnp.floor(field_ref[0] * (1.0 / cols))
    ahead = jnp.zeros((size, size), F32)
    rank = jnp.zeros((size, size), F32)
    lane = lax.broadcasted_iota(jnp.int32, (size, size), 1).astype(F32)
    passed = jnp.zeros((size, size), F32)
    for l in range(layers):
        mine = layer == float(l)
        mask = flag(mine)
        totals = dot(mask, ones)
        stack = jnp.concatenate([totals.astype(BF16), ahead.astype(BF16)], axis=0)
        rank = jnp.where(mine, dot(mask, upper) + dot(both, stack), rank)
        ahead = ahead + totals
        if l + 1 < layers:
            end = jnp.floor(dot(both[:, size:], ahead.astype(BF16)) * (1.0 / WIDE))
            passed = passed + jnp.where(jnp.minimum(end, span - 1.0) + l < lane, 1.0, 0.0)
    unit = ((lane - passed) * layers + passed).astype(jnp.int32)
    for k in range(size // BLOCK):
        unit_ref[k : k + 1, :] = unit[k * BLOCK : k * BLOCK + 1]
    row = jnp.floor(rank * (1.0 / WIDE))
    lam = rank - row * WIDE
    slot = slot_ref[...]
    place_ref[...] = jnp.where(slot >= 0.0, slot, (row + layer + table) * WIDE + lam)
    row_ref[...], lam_ref[...] = row, lam


def sort_kernel(field_ref, row_ref, lam_ref, after_ref, order_ref):
    size = row_ref.shape[0]
    span = BLOCK * size // WIDE
    row, lam = row_ref[...], lam_ref[...]
    for k in range(size // BLOCK):
        picks, marks = [], []
        for i in range(k * BLOCK, (k + 1) * BLOCK):
            hit = row_iota(span) == row[i : i + 1]
            picks.append(
                jnp.concatenate(
                    [jnp.where(hit, field_ref[f, i : i + 1, :], 0.0) for f in range(2)], axis=0
                ).astype(BF16)
            )
            marks.append(onehot(lam[i : i + 1], WIDE))
        sorted_rows = transposed_dot(lanes(picks), lanes(marks))
        for f in range(2):
            order_ref[f, k * span : (k + 1) * span, :] = sorted_rows[f * span : (f + 1) * span]


def stay_gather_kernel(layers, start, slope_ref, order_ref, unit_ref, out_ref):
    span = order_ref.shape[1] // unit_ref.shape[0]
    units = span + layers

    def body(j, carry):
        k = j + start
        for u in range(units - 1):
            code = unit_ref[k, u]
            at = k * span + lax.div(code, layers)
            lc, r = order_ref[0, pl.ds(at, 1), :], order_ref[1, pl.ds(at, 1), :]
            for f, value in enumerate(gather_unit(layers, slope_ref, code, lc, r)):
                out_ref[j, f * units + u : f * units + u + 1, :] = value
        for f in range(2):
            out_ref[j, (f + 1) * units - 1 : (f + 1) * units, :] = jnp.zeros((1, WIDE), F32)
        return carry

    lax.fori_loop(0, out_ref.shape[0], body, 0)


def late_gather_kernel(layers, start, slope_ref, order_ref, unit_ref, value_ref, out_ref, value_hbm, sem):
    copy = pltpu.make_async_copy(value_ref, value_hbm, sem)
    copy.start()
    stay_gather_kernel(layers, start, slope_ref, order_ref, unit_ref, out_ref)
    copy.wait()


def reply_kernel(nyc, near_ref, after_ref, *refs):
    size = 2 * GROUP
    backs, (a_ref, b_ref) = refs[: nyc - 1], refs[nyc - 1 :]
    a_ref[:size, :] = near_ref[:size, :]
    b_ref[:size, :] = near_ref[size:, :]
    for y, ref in enumerate(backs):
        a_ref[(y + 1) * size : (y + 2) * size, :] = ref[size : 2 * size, :]
        b_ref[(y + 1) * size : (y + 2) * size, :] = ref[2 * size : 3 * size, :]


def unpack_kernel(nyc, backa_ref, backb_ref, *refs):
    backy = refs[: nyc - 1]
    early_ref, late_ref, place_ref, power_ref, out_ref, table_ref = refs[nyc - 1 :]
    groups = [(backa_ref, y) for y in range(nyc)] + [(backb_ref, y) for y in range(nyc)]
    groups += [(ref, 0) for ref in backy]
    sent, units = len(groups) * GROUP, early_ref.shape[1] // 2
    table = sent + units
    for f in range(2):
        whole = jnp.concatenate(
            [ref[(2 * at + f) * GROUP : (2 * at + f + 1) * GROUP, :] for ref, at in groups], axis=0
        )
        for part, piece in enumerate(pieces(whole)):
            at = (part * 2 + f) * table
            table_ref[at : at + sent, :] = piece

    def body(stay_ref, start, k, carry):
        base = pl.multiple_of((k + start) * BLOCK, BLOCK)
        for f in range(2):
            for part, piece in enumerate(pieces(stay_ref[k, f * units : (f + 1) * units, :])):
                at = (part * 2 + f) * table + sent
                table_ref[at : at + units, :] = piece
        source = table_ref[...].astype(BF16)
        places = place_ref[pl.ds(base, BLOCK), :]
        qs = jnp.floor(places * (1.0 / WIDE))
        lams = places - qs * WIDE
        powers = power_ref[pl.ds(base, BLOCK), :]
        for i in range(0, BLOCK, 8):
            many = lambda x: lanes([x[i + j : i + j + 1] for j in range(8)])
            at = pl.multiple_of(base * 128 + i * 128, 1024)
            found = dot(source, onehot(many(lams), WIDE))
            here = row_iota(table, 1024) == many(qs)
            for f in range(2):
                both = found[f * table : (f + 1) * table] + found[(2 + f) * table : (3 + f) * table]
                value = jnp.sum(jnp.where(here, both, 0.0), axis=0, keepdims=True)
                out_ref[f : f + 1, pl.ds(at, 1024)] = -many(powers) * value
        return carry

    early = early_ref.shape[0]
    lax.fori_loop(0, early, functools.partial(body, early_ref, 0), 0)
    lax.fori_loop(0, late_ref.shape[0], functools.partial(body, late_ref, early), 0)


def call(kernel, outs, scratch, *args, spaces={}, out_spaces={}):
    specs = [pl.BlockSpec(memory_space=spaces.get(i, pltpu.VMEM)) for i in range(len(args))]
    shapes = [jax.ShapeDtypeStruct(shape, dtype) for shape, dtype in outs]
    return pl.pallas_call(
        kernel,
        out_shape=shapes,
        in_specs=specs,
        out_specs=[
            pl.BlockSpec(memory_space=out_spaces.get(i, pltpu.VMEM)) for i in range(len(shapes))
        ],
        scratch_shapes=scratch,
        compiler_params=pltpu.CompilerParams(vmem_limit_bytes=48 * 1024 * 1024),
    )(*args)


def shards(
    cell_bin, cell_layer, cell_offset, cell_power, spill_weight, conductivity, layer_coupling
):
    layers, cols, rows = conductivity.shape
    cells = cell_bin.shape[0]
    nyc = 2 if lax.axis_size("gy") == 2 else 3
    count = layers * cols
    groups = 3 * nyc - 1
    flat = lambda x: x.reshape(cells // 128, 128)
    bins, layer, off = flat(cell_bin), flat(cell_layer), flat(cell_offset)
    power, spill = flat(cell_power), flat(spill_weight)
    square = bins.shape
    split = square[0] * 3 // 4
    own = 3 * GROUP
    message = (nyc * own + layers * HALO, WIDE)
    vmem = lambda *shape: pltpu.VMEM(shape, F32)
    partial = functools.partial

    tile = conductivity.shape
    msg_a, msg_b, own_y, slot, fields, power = call(
        partial(pack_kernel, nyc, layers, cols, rows),
        [
            (message, F32), (message, F32), (((nyc - 1) * own, WIDE), F32),
            (square, F32), ((6, *square), F32), (square, F32),
        ],
        [pltpu.VMEM(square, jnp.int32)] * 3
        + [
            vmem(*square), vmem(2, layers, HALO, rows), pltpu.SemaphoreType.DMA((7,)),
            vmem(6 * groups * GROUP, WIDE),
        ],
        *[
            pltpu.with_memory_space_constraint(x, pltpu.HBM)
            for x in (bins, layer, off, power, spill, conductivity)
        ],
        spaces={i: pltpu.HBM for i in range(6)},
    )
    recv_a, recv_b = exchange(msg_a, 1, 0), exchange(msg_b, 2, 0)
    (stay_grid,) = call(
        partial(stay_deposit_kernel, cols, split),
        [((2 * count, rows), F32)],
        [],
        fields, slot,
    )
    msg_y = call(
        partial(forward_kernel, nyc),
        [((3 * own + 2 * HALO, WIDE), F32)] * (nyc - 1),
        [],
        recv_a, recv_b, own_y, conductivity, stay_grid,
        spaces={4: pl.ANY},
    )
    recv_y = [exchange(m, 0, i + 1) for i, m in enumerate(msg_y)]
    near_grid, near_unit = call(
        partial(near_deposit_kernel, cols, split),
        [((2 * count, rows), F32), ((8, 128), jnp.int32)],
        [],
        stay_grid, recv_a, recv_b, fields, slot,
    )
    table = groups * GROUP
    place, unit, row, lam = call(
        partial(rank_kernel, layers, cols, table),
        [(square, F32), ((square[0] // BLOCK, 128), jnp.int32), (square, F32), (square, F32)],
        [],
        fields, slot, near_grid,
        spaces={2: pl.ANY},
    )
    edge = (layers, HALO, rows)
    outer, edge_a, edge_b = call(
        partial(edge_deposit_kernel, cols),
        [((layers, cols // 2, rows), F32), (edge, F32), (edge, F32)],
        [],
        near_grid, row, *recv_y,
        spaces={1: pl.ANY},
    )
    from_a, from_b = exchange(edge_a, 1, 0), exchange(edge_b, 2, 0)
    (grid,) = call(
        partial(inner_deposit_kernel, cols), [(tile, F32)], [], near_grid, outer, *recv_y
    )
    (order,) = call(
        sort_kernel,
        [((2, cells // WIDE, WIDE), F32)],
        [],
        fields, row, lam, grid,
        spaces={3: pl.ANY},
    )
    edges = call(
        power_edge_kernel,
        [((2 * HALO, WIDE), F32)] * (nyc - 1),
        [],
        grid, from_a, from_b, order,
        spaces={3: pl.ANY},
    )
    from_y = [exchange(e, 0, i + 1) for i, e in enumerate(edges)]
    big = (layers, cols + 2 * HALO, rows + 128)
    *faces, far_unit = call(
        partial(face_kernel, nyc),
        [(big, F32)] * 5 + [((8, 128), jnp.int32)],
        [vmem(*big)],
        conductivity, recv_a, recv_b, layer_coupling, *recv_y,
        spaces={3: pltpu.SMEM},
    )
    warmth, slope = call(
        partial(solve_kernel, nyc),
        [(tile, F32), ((4 * count, rows), BF16)],
        [vmem(*big), vmem(2, layers, big[1] + 16, big[2]), vmem(*big)],
        grid, from_a, from_b, *faces, *from_y,
    )
    answer_y = [
        call(
            partial(gather_kernel, layers, [(0, own * i, 3 * y + i) for i in range(3)]),
            [((6 * GROUP, WIDE), F32)],
            [],
            slope, far_unit, r,
            spaces={1: pltpu.SMEM},
        )[0]
        for y, r in enumerate(recv_y)
    ]
    back_y = [exchange(m, 0, i + 1) for i, m in enumerate(answer_y)]
    (near_answer,) = call(
        partial(gather_kernel, layers, [(0, 0, 0), (1, 0, 1)]),
        [((4 * GROUP, WIDE), F32)],
        [],
        slope, near_unit, recv_a, recv_b,
        spaces={1: pltpu.SMEM},
    )
    blocks, early = square[0] // BLOCK, 1
    units = order.shape[1] // blocks + layers
    (early_value,) = call(
        partial(stay_gather_kernel, layers, 0),
        [((early, 2 * units, WIDE), F32)],
        [],
        slope, order, unit,
        spaces={2: pltpu.SMEM},
    )
    answer_a, answer_b = call(
        partial(reply_kernel, nyc),
        [((2 * nyc * GROUP, WIDE), F32)] * 2,
        [],
        near_answer, early_value, *back_y,
        spaces={1: pl.ANY},
    )
    back_a, back_b = exchange(answer_a, 1, 0), exchange(answer_b, 2, 0)
    late_value, final_warmth = call(
        partial(late_gather_kernel, layers, early),
        [((blocks - early, 2 * units, WIDE), F32), (tile, F32)],
        [pltpu.SemaphoreType.DMA(())],
        slope, order, unit, warmth,
        spaces={2: pltpu.SMEM},
        out_spaces={1: pltpu.HBM},
    )
    (pull,) = call(
        partial(unpack_kernel, nyc),
        [((2, cells), F32)],
        [vmem(4 * (table + units), WIDE)],
        back_a, back_b, *back_y, early_value, late_value, place, power,
    )
    return final_warmth, pull


def solution(mesh):
    cell = P(("gx", "gy"))
    tile = P(None, "gx", "gy")
    return jax.shard_map(
        shards,
        mesh=mesh,
        in_specs=(cell, cell, cell, cell, cell, tile, P()),
        out_specs=(tile, P(None, ("gx", "gy"))),
        check_vma=False,
    )
```

```python
import functools

import jax
import jax.numpy as jnp
from jax import lax
from jax.experimental import pallas as pl
from jax.experimental.pallas import tpu as pltpu
from jax.sharding import PartitionSpec as P

ITERS = 4
CAP = 2048
SINK_RATE = 0.5
LOW_BOUND = 0.5
HIGH_BOUND = 33.0

WIDE = 256
GROUP = CAP // WIDE
BLOCK = 32
HALO = 8
F32, BF16 = jnp.float32, jnp.bfloat16


def partner(place, kind, count):
    if kind == 0:
        return place
    if kind == 1:
        return place ^ 1
    other = place - 1 if place % 2 == 0 else place + 1
    return other if 0 <= other < count else None


def exchange(value, x_kind, y_kind):
    nx, ny = lax.axis_size("gx"), lax.axis_size("gy")
    pairs = []
    for a in range(nx):
        for b in range(ny):
            x, y = partner(a, x_kind, nx), partner(b, y_kind, ny)
            if x is None:
                x, y = a, b ^ 1
            elif y is None:
                x, y = a ^ 1, b
            pairs.append((a * ny + b, x * ny + y))
    return lax.ppermute(value, ("gx", "gy"), pairs)


def pieces(value):
    high = value.astype(BF16).astype(F32)
    return high, value - high


def row_iota(count, width=128):
    return lax.broadcasted_iota(jnp.int32, (count, width), 0).astype(F32)


def onehot(row, count):
    return jnp.where(
        row_iota(count, row.shape[1]).astype(BF16) == row.astype(BF16),
        jnp.ones((), BF16),
        jnp.zeros((), BF16),
    )


def lanes(parts):
    return jnp.concatenate(parts, axis=1) if len(parts) > 1 else parts[0]


def transposed_dot(left, right):
    return lax.dot_general(left, right, (((1,), (1,)), ((), ())), preferred_element_type=F32)


def dot(left, right):
    return lax.dot_general(left, right, (((1,), (0,)), ((), ())), preferred_element_type=F32)


def kind_of(step, place):
    ahead = 1 - 2 * lax.rem(place, 2)
    return jnp.where(step == 0, 0, jnp.where(step == ahead, 1, 2))


def pack_kernel(
    nyc, layers, cols, rows,
    bin_hbm, layer_hbm, off_hbm, power_hbm, spill_hbm, cond_hbm,
    msga_ref, msgb_ref, owny_ref, slot_ref, field_ref, power_ref,
    bin_ref, layer_ref, off_ref, spill_ref, edge_ref, sems, acc_ref,
):
    a, b = lax.axis_index("gx"), lax.axis_index("gy")
    copies = [
        pltpu.make_async_copy(src, dst, sems.at[i])
        for i, (src, dst) in enumerate(
            [
                (off_hbm, off_ref), (layer_hbm, layer_ref), (bin_hbm, bin_ref),
                (power_hbm, power_ref), (spill_hbm, spill_ref),
                (cond_hbm.at[:, :HALO, :], edge_ref.at[0]),
                (cond_hbm.at[:, cols - HALO :, :], edge_ref.at[1]),
            ]
        )
    ]
    for copy in copies:
        copy.start()
    acc_ref[...] = jnp.zeros_like(acc_ref)
    groups = 3 * nyc - 1
    table = groups * GROUP
    copies[0].wait()
    copies[1].wait()
    off = off_ref[...]
    col_code = (off >= 3).astype(jnp.int32) + (off >= 6).astype(jnp.int32)
    x_kind = kind_of(col_code - 1, a)
    y_kind = kind_of(off - 3 * col_code - 1, b)
    group = jnp.where(x_kind > 0, (x_kind - 1) * nyc + y_kind, 2 * nyc - 1 + y_kind)
    key = jnp.where(off == 4, -1, group * layers + layer_ref[...])
    size = off.shape[0]
    r_i = lax.broadcasted_iota(jnp.int32, (size, size), 0)
    c_i = lax.broadcasted_iota(jnp.int32, (size, size), 1)
    flag = lambda x: jnp.where(x, 1.0, 0.0).astype(BF16)
    ones = jnp.ones((size, size), BF16)
    before = jnp.concatenate([flag(r_i < c_i), ones], axis=1)
    rank = jnp.zeros((size, size), F32)
    counts = jnp.zeros((size, size), F32)
    for g in range(groups):
        keys = range(g * layers, (g + 1) * layers)
        counted = dot(jnp.concatenate([flag(key == k) for k in keys], axis=0), before)
        for i, k in enumerate(keys):
            block = counted[i * size : (i + 1) * size]
            rank = jnp.where(key == k, block[:, :size], rank)
            counts = jnp.where(c_i == k, block[:, size:], counts)
    narrow = counts.astype(BF16)
    ahead = dot(narrow, flag((r_i // layers == c_i // layers) & (r_i < c_i))).astype(BF16)
    base = dot(
        jnp.concatenate([flag(r_i > c_i), ones], axis=1), jnp.concatenate([narrow, ahead], axis=0)
    )
    base = jnp.take_along_axis(base, jnp.maximum(key, 0), axis=1, mode="promise_in_bounds")
    slot = jnp.where(key >= 0, rank + base + (group * CAP).astype(F32), -1.0)
    slot_ref[...] = slot
    for copy in copies[2:]:
        copy.wait()
    code = layer_ref[...] * (cols * rows) + bin_ref[...]
    field_ref[0] = (code // rows).astype(F32)
    field_ref[1] = (code % rows).astype(F32)
    power = power_ref[...]
    spill = spill_ref[...]
    field_ref[2], field_ref[3] = pieces(power * (1.0 - spill))
    field_ref[4], field_ref[5] = pieces(power * spill)
    step = 64

    def body(j, carry):
        base = pl.multiple_of(j * step, step)
        slots = slot_ref[pl.ds(base, step), :]
        qs = jnp.floor(slots * (1.0 / WIDE))
        lams = slots - qs * WIDE
        vals = [field_ref[f, pl.ds(base, step), :] for f in range(6)]
        picks, marks = [], []
        for i in range(step):
            hit = row_iota(table) == qs[i : i + 1]
            picks.append(
                jnp.concatenate([jnp.where(hit, v[i : i + 1], 0.0) for v in vals], axis=0).astype(BF16)
            )
            marks.append(onehot(lams[i : i + 1], WIDE))
        acc_ref[...] += transposed_dot(lanes(picks), lanes(marks))
        return carry

    lax.fori_loop(0, size // step, body, 0)
    out = [acc_ref[f * table : (f + 1) * table, :] for f in range(6)]
    sent = [out[0] * float(rows) + out[1], out[2] + out[3], out[4] + out[5]]

    def put(ref, at, g):
        for f in range(3):
            ref[(at * 3 + f) * GROUP : (at * 3 + f + 1) * GROUP, :] = sent[f][
                g * GROUP : (g + 1) * GROUP
            ]

    for y in range(nyc):
        put(msga_ref, y, y)
        put(msgb_ref, y, nyc + y)
        if y:
            put(owny_ref, y - 1, 2 * nyc + y - 1)
    first, last = edge_ref[0], edge_ref[1]
    even = lax.rem(a, 2) == 0
    top = nyc * 3 * GROUP
    flat = (-1, rows)
    msga_ref[top:, :] = jnp.where(even, last, first).reshape(flat)
    msgb_ref[top:, :] = jnp.where(even, first, last).reshape(flat)


def deposit_block(lc, r, main, spill, cols, cells, part=None):
    picks, marks = [], []
    zero = jnp.zeros((), BF16)
    narrow = lambda x: x.astype(BF16)
    quarter = cols // 4
    count = cells if part is None else cells // 2
    for lc_i, r_i, (mh, ml), (sh, sl) in zip(lc, r, main, spill):
        spot = narrow(row_iota(count, lc_i.shape[1]))
        step = cols
        other = lambda at: jnp.where(lc_i >= float(cells - cols), at - step, at + step)
        if part is None:
            there_i = other(lc_i)
        else:
            step = cols // 2
            layer = jnp.floor(lc_i * (1.0 / cols))
            column = lc_i - layer * cols
            inner = (column >= quarter) & (column < 3 * quarter)
            if part == "inner":
                mine, at = inner, layer * step + (column - quarter)
            else:
                mine = jnp.logical_not(inner)
                at = layer * step + jnp.where(column < quarter, column, column - step)
            there_i = jnp.where(mine, other(at), -1.0)
            lc_i = jnp.where(mine, at, -1.0)
        here, there = spot == narrow(lc_i), spot == narrow(there_i)
        high = jnp.where(here, narrow(mh), jnp.where(there, narrow(sh), zero))
        low = jnp.where(here, narrow(ml), jnp.where(there, narrow(sl), zero))
        picks.append(jnp.concatenate([high, low], axis=0))
        marks.append(onehot(r_i, WIDE))
    return transposed_dot(lanes(picks), lanes(marks))


def deposit_stays(grid_ref, field_ref, slot_ref, first, last, cols):
    count, step = grid_ref.shape[0] // 2, last - first
    stays = slot_ref[first:last, :] < 0.0
    vals = [jnp.where(stays, field_ref[2 + f, first:last, :], 0.0) for f in range(4)]
    lcs, rs = field_ref[0, first:last, :], field_ref[1, first:last, :]
    for base in range(0, last - first, step):
        rows_of = lambda x: [x[base + i : base + i + 1] for i in range(step)]
        parts = [rows_of(v) for v in vals]
        grid_ref[...] += deposit_block(
            rows_of(lcs), rows_of(rs), list(zip(parts[0], parts[1])),
            list(zip(parts[2], parts[3])), cols, count,
        )


def stay_deposit_kernel(cols, split, field_ref, slot_ref, grid_ref):
    grid_ref[...] = jnp.zeros_like(grid_ref)
    deposit_stays(grid_ref, field_ref, slot_ref, 0, split, cols)


def group_deposit(sources, cols, count, part=None):
    lc, r, main, spill = [], [], [], []
    for ref, at in sources:
        rows = ref.shape[1]
        for row in range(at, at + GROUP):
            code = ref[row : row + 1, :]
            lc_i = jnp.floor(code * (1.0 / rows))
            lc.append(lc_i)
            r.append(code - lc_i * rows)
            main.append(pieces(ref[row + GROUP : row + GROUP + 1, :]))
            spill.append(pieces(ref[row + 2 * GROUP : row + 2 * GROUP + 1, :]))
    return deposit_block(lc, r, main, spill, cols, count, part)


def count_units(unit_ref, sources, layers, cells):
    unit_ref[...] = jnp.zeros_like(unit_ref)
    lane = lax.broadcasted_iota(jnp.int32, (1, 128), 1).astype(F32)
    for g, (ref, at) in enumerate(sources):
        layer = jnp.floor(ref[at : at + GROUP, :] * (1.0 / cells))
        layer = jnp.where(ref[at + GROUP : at + 2 * GROUP, :] > 0.0, layer, float(layers))
        passed = jnp.zeros((1, 128), F32)
        for l in range(layers - 1):
            end = jnp.sum(jnp.where(layer <= l, 1.0, 0.0), axis=0, keepdims=True)
            end = jnp.floor(jnp.sum(end, axis=1, keepdims=True) * (1.0 / WIDE))
            passed = passed + jnp.where(jnp.minimum(end, GROUP - 1.0) + l < lane, 1.0, 0.0)
        unit_ref[g : g + 1, :] = ((lane - passed) * layers + passed).astype(jnp.int32)


def near_deposit_kernel(
    cols, split, stay_ref, recva_ref, recvb_ref, field_ref, slot_ref, grid_ref, unit_ref
):
    count, rows = grid_ref.shape[0] // 2, grid_ref.shape[1]
    count_units(unit_ref, [(recva_ref, 0), (recvb_ref, 0)], count // cols, cols * rows)
    grid_ref[...] = stay_ref[...]
    deposit_stays(grid_ref, field_ref, slot_ref, split, slot_ref.shape[0], cols)
    grid_ref[...] += group_deposit([(recva_ref, 0), (recvb_ref, 0)], cols, count)


def half_deposit(near_ref, recvy, cols, part):
    count, rows = near_ref.shape[0] // 2, near_ref.shape[1]
    layers = count // cols
    far = group_deposit([(ref, 3 * GROUP * i) for ref in recvy for i in range(3)], cols, count, part)
    far = far[: count // 2] + far[count // 2 :]
    near = (near_ref[:count, :] + near_ref[count:, :]).reshape(layers, cols, rows)
    quarter = cols // 4
    if part == "inner":
        near = near[:, quarter : 3 * quarter]
    else:
        near = jnp.concatenate([near[:, :quarter], near[:, 3 * quarter :]], axis=1)
    return near + far.reshape(layers, cols // 2, rows)


def edge_deposit_kernel(cols, near_ref, after_ref, *refs):
    recvy, (outer_ref, edgea_ref, edgeb_ref) = refs[:-3], refs[-3:]
    outer = half_deposit(near_ref, recvy, cols, "edge")
    outer_ref[...] = outer
    first, last = outer[:, :HALO], outer[:, cols // 2 - HALO :]
    even = lax.rem(lax.axis_index("gx"), 2) == 0
    edgea_ref[...] = jnp.where(even, last, first)
    edgeb_ref[...] = jnp.where(even, first, last)


def inner_deposit_kernel(cols, near_ref, outer_ref, *refs):
    recvy, grid_ref = refs[:-1], refs[-1]
    quarter = cols // 4
    grid_ref[:, :quarter, :] = outer_ref[:, :quarter, :]
    grid_ref[:, 3 * quarter :, :] = outer_ref[:, quarter:, :]
    grid_ref[:, quarter : 3 * quarter, :] = half_deposit(near_ref, recvy, cols, "inner")


def with_columns(own, from_a, from_b):
    a = lax.axis_index("gx")
    even = lax.rem(a, 2) == 0
    right = jnp.where(even, from_a, from_b)
    left = jnp.where(even, from_b, from_a)
    right = jnp.where(a < lax.axis_size("gx") - 1, right, 0.0)
    left = jnp.where(a > 0, left, 0.0)
    return jnp.concatenate([left, own, right], axis=1)


def row_edge(wide, last):
    rows = wide.shape[1]
    tile = jnp.where(last, wide[:, rows - 128 :], wide[:, :128]).T
    return jnp.where(last, tile[128 - HALO :], tile[:HALO])


def put_edges(ref, at, edge):
    extra = edge.shape[1] - WIDE
    ref[at : at + HALO, :] = edge[:, :WIDE]
    ref[at + HALO : at + 2 * HALO, :] = jnp.concatenate(
        [edge[:, WIDE:], jnp.zeros((HALO, WIDE - extra), F32)], axis=1
    )


def get_edges(ref, at, count):
    return jnp.concatenate(
        [ref[at : at + HALO, :], ref[at + HALO : at + 2 * HALO, : count - WIDE]], axis=1
    )


def y_edges(refs, at, wide):
    even = lax.rem(lax.axis_index("gy"), 2) == 0
    for kind, ref in enumerate(refs):
        put_edges(ref, at, row_edge(wide, even if kind == 0 else jnp.logical_not(even)))


def halo_of(ref, cols, layers, top):
    return ref[top:, :].reshape(layers, HALO, ref.shape[1])


def forward_kernel(nyc, recva_ref, recvb_ref, owny_ref, cond_ref, after_ref, *msgy_refs):
    layers, cols, rows = cond_ref.shape
    size, top = 3 * GROUP, nyc * 3 * GROUP
    for y, ref in enumerate(msgy_refs):
        ref[:size, :] = owny_ref[y * size : (y + 1) * size, :]
        ref[size : 2 * size, :] = recva_ref[(y + 1) * size : (y + 2) * size, :]
        ref[2 * size : 3 * size, :] = recvb_ref[(y + 1) * size : (y + 2) * size, :]
    wide = with_columns(
        cond_ref[...], halo_of(recva_ref, cols, layers, top), halo_of(recvb_ref, cols, layers, top)
    )
    y_edges(msgy_refs, 3 * size, wide.reshape(-1, rows))


def power_edge_kernel(grid_ref, froma_ref, fromb_ref, after_ref, *edge_refs):
    wide = with_columns(grid_ref[...], froma_ref[...], fromb_ref[...])
    y_edges(edge_refs, 0, wide.reshape(-1, grid_ref.shape[2]))


def with_rows(wide, edges):
    b, ny = lax.axis_index("gy"), lax.axis_size("gy")
    layers, span, rows = wide.shape
    count = layers * span
    even = lax.rem(b, 2) == 0
    one = edges[0]
    two = edges[1] if len(edges) > 1 else jnp.zeros_like(one)
    after = jnp.where(b < ny - 1, jnp.where(even, one, two), 0.0)
    before = jnp.where(b > 0, jnp.where(even, two, one), 0.0)
    tile = jnp.concatenate([after, jnp.zeros((128 - 2 * HALO, count), F32), before], axis=0).T
    return jnp.concatenate([wide, tile.reshape(layers, span, 128)], axis=2)


def face_kernel(nyc, cond_ref, recva_ref, recvb_ref, coupling_ref, *refs):
    recvy_refs = refs[: nyc - 1]
    cn_ref, cp_ref, rn_ref, fl_ref, d_ref, unit_ref, k_ref = refs[nyc - 1 :]
    layers, cols, rows = cond_ref.shape
    span, wide_rows = cols + 2 * HALO, rows + 128
    count = layers * span
    top = nyc * 3 * GROUP
    sources = [(ref, 3 * GROUP * i) for ref in recvy_refs for i in range(3)]
    count_units(unit_ref, sources, layers, cols * rows)
    a, b = lax.axis_index("gx"), lax.axis_index("gy")
    nx, ny = lax.axis_size("gx"), lax.axis_size("gy")
    k_ref[...] = with_rows(
        with_columns(
            cond_ref[...],
            halo_of(recva_ref, cols, layers, top),
            halo_of(recvb_ref, cols, layers, top),
        ),
        [get_edges(ref, 9 * GROUP, count) for ref in recvy_refs],
    )
    shape = (span, wide_rows)
    c_i = lax.broadcasted_iota(jnp.int32, shape, 0)
    r_i = lax.broadcasted_iota(jnp.int32, shape, 1)
    c_low = jnp.where(a > 0, 0, HALO)
    c_high = jnp.where(a < nx - 1, span, span - HALO)
    r_high = jnp.where(b < ny - 1, rows + HALO, rows)
    r_low = jnp.where(b > 0, wide_rows - HALO, wide_rows)
    inside = jnp.where((c_i >= c_low) & (c_i < c_high) & ((r_i < r_high) | (r_i >= r_low)), 1.0, 0.0)
    next_c = lambda x: pltpu.roll(x, span - 1, 0)
    prev_c = lambda x: pltpu.roll(x, 1, 0)
    next_r = lambda x: pltpu.roll(x, wide_rows - 1, 1)
    prev_r = lambda x: pltpu.roll(x, 1, 1)
    both_c, both_r = inside * next_c(inside), inside * next_r(inside)
    below = None
    for l in range(layers):
        k = k_ref[l]
        face_c, face_r = 0.5 * (k + next_c(k)), 0.5 * (k + next_r(k))
        kept_c, kept_r = face_c * both_c, face_r * both_r
        cn_ref[l], cp_ref[l] = kept_c, prev_c(kept_c)
        rn_ref[l] = kept_r
        total = SINK_RATE + ((face_c + prev_c(face_c)) + (face_r + prev_r(face_r)))
        if below is not None:
            total = total + below
        if l + 1 < layers:
            below = coupling_ref[l] * (0.5 * (k + k_ref[l + 1]))
            fl_ref[l] = below * inside
            total = total + below
        d_ref[l] = total


def solve_kernel(
    nyc, grid_ref, froma_ref, fromb_ref, cn_ref, cp_ref, rn_ref, fl_ref, d_ref, *refs
):
    edge_refs, (warmth_ref, slope_ref, p_ref, v_ref, u_ref) = refs[: nyc - 1], refs[nyc - 1 :]
    layers, cols, rows = grid_ref.shape
    span, wide_rows = cols + 2 * HALO, rows + 128
    p_ref[...] = with_rows(
        with_columns(grid_ref[...], froma_ref[...], fromb_ref[...]),
        [get_edges(ref, 0, layers * span) for ref in edge_refs],
    )
    next_r = lambda x: pltpu.roll(x, wide_rows - 1, 1)
    prev_r = lambda x: pltpu.roll(x, 1, 1)
    middle = 0.5 * (HIGH_BOUND + LOW_BOUND)
    spread = 0.5 * (HIGH_BOUND - LOW_BOUND)
    sigma = middle / spread
    now = 1.0 / sigma
    blank = jnp.zeros((8, wide_rows), F32)
    for l in range(layers):
        for side in range(2):
            v_ref[side, l, :8, :] = blank
            v_ref[side, l, 8 + span :, :] = blank
        v_ref[0, l, 8 : 8 + span, :] = p_ref[l] * (1.0 / middle)
    for sweep in range(ITERS):
        later = 1.0 / (2.0 * sigma - now)
        keep, gain = later * now, 2.0 * later / spread
        old, new = sweep % 2, (sweep + 1) % 2
        for c in range(0, span, 8):
            at, here = slice(c, c + 8), slice(c + 8, c + 16)
            vs = [v_ref[old, l, here, :] for l in range(layers)]
            for l in range(layers):
                v = vs[l]
                rest = p_ref[l, at, :] - d_ref[l, at, :] * v
                rest = rest + cn_ref[l, at, :] * v_ref[old, l, c + 9 : c + 17, :]
                rest = rest + cp_ref[l, at, :] * v_ref[old, l, c + 7 : c + 15, :]
                after = rn_ref[l, at, :]
                rest = rest + (after * next_r(v) + prev_r(after * v))
                if l + 1 < layers:
                    rest = rest + fl_ref[l, at, :] * vs[l + 1]
                if l:
                    rest = rest + fl_ref[l - 1, at, :] * vs[l - 1]
                advance = keep * (u_ref[l, at, :] if sweep else v) + gain * rest
                if sweep + 1 < ITERS:
                    u_ref[l, at, :] = advance
                v_ref[new, l, here, :] = v + advance
        now = later
    final = ITERS % 2
    for l in range(layers):
        warmth_ref[l] = v_ref[final, l, 8 + HALO : 8 + HALO + cols, :rows]
        for c in range(0, cols, 16):
            at = 8 + HALO + c
            v = v_ref[final, l, at : at + 16, :]
            slopes = (
                0.5 * (v_ref[final, l, at + 1 : at + 17, :rows] - v_ref[final, l, at - 1 : at + 15, :rows]),
                0.5 * (next_r(v) - prev_r(v))[:, :rows],
            )
            for f, slope in enumerate(slopes):
                for part, piece in enumerate(pieces(slope)):
                    put = ((l * 2 + part) * 2 + f) * cols + c
                    slope_ref[put : put + 16, :] = piece.astype(BF16)


def pick(found, lc, first):
    cols = found.shape[0] // 4
    here = row_iota(cols, lc.shape[1]) == lc - first
    return [
        jnp.where(here, found[f * cols : (f + 1) * cols] + found[(2 + f) * cols : (3 + f) * cols], 0.0)
        for f in range(2)
    ]


def gather_unit(layers, slope_ref, code, lc, r):
    size = slope_ref.shape[0] // layers
    layer = lax.rem(code, layers)
    rows = slope_ref[pl.ds(pl.multiple_of(layer * size, size), size), :]
    found = dot(rows, onehot(r, slope_ref.shape[1]))
    first = (layer * (size // 4)).astype(F32)
    return [jnp.sum(part, axis=0, keepdims=True) for part in pick(found, lc, first)]


def gather_kernel(layers, sources, slope_ref, unit_ref, *refs):
    ins, out_ref = refs[:-1], refs[-1]
    rows = slope_ref.shape[1]
    for g, (which, at, line) in enumerate(sources):
        totals = [jnp.zeros((GROUP, WIDE), F32)] * 2
        for u in range(GROUP + layers - 1):
            code = unit_ref[line, u]
            row = lax.div(code, layers)
            slots = ins[which][pl.ds(at + row, 1), :]
            lc = jnp.floor(slots * (1.0 / rows))
            hit = row_iota(GROUP, WIDE) == row.astype(F32)
            for f, value in enumerate(gather_unit(layers, slope_ref, code, lc, slots - lc * rows)):
                totals[f] = totals[f] + jnp.where(hit, value, 0.0)
        for f in range(2):
            out_ref[(g * 2 + f) * GROUP : (g * 2 + f + 1) * GROUP, :] = totals[f]


def rank_kernel(layers, cols, table, field_ref, slot_ref, after_ref, place_ref, unit_ref, row_ref, lam_ref):
    size = slot_ref.shape[0]
    span = BLOCK * size // WIDE
    r_i = lax.broadcasted_iota(jnp.int32, (size, size), 0)
    c_i = lax.broadcasted_iota(jnp.int32, (size, size), 1)
    flag = lambda x: jnp.where(x, 1.0, 0.0).astype(BF16)
    upper, ones = flag(r_i < c_i), jnp.ones((size, size), BF16)
    same = (r_i // BLOCK) == (c_i // BLOCK)
    both = jnp.concatenate([flag(same & (r_i > c_i)), flag(same)], axis=1)
    layer = jnp.floor(field_ref[0] * (1.0 / cols))
    ahead = jnp.zeros((size, size), F32)
    rank = jnp.zeros((size, size), F32)
    lane = lax.broadcasted_iota(jnp.int32, (size, size), 1).astype(F32)
    passed = jnp.zeros((size, size), F32)
    for l in range(layers):
        mine = layer == float(l)
        mask = flag(mine)
        totals = dot(mask, ones)
        stack = jnp.concatenate([totals.astype(BF16), ahead.astype(BF16)], axis=0)
        rank = jnp.where(mine, dot(mask, upper) + dot(both, stack), rank)
        ahead = ahead + totals
        if l + 1 < layers:
            end = jnp.floor(dot(both[:, size:], ahead.astype(BF16)) * (1.0 / WIDE))
            passed = passed + jnp.where(jnp.minimum(end, span - 1.0) + l < lane, 1.0, 0.0)
    unit = ((lane - passed) * layers + passed).astype(jnp.int32)
    for k in range(size // BLOCK):
        unit_ref[k : k + 1, :] = unit[k * BLOCK : k * BLOCK + 1]
    row = jnp.floor(rank * (1.0 / WIDE))
    lam = rank - row * WIDE
    slot = slot_ref[...]
    place_ref[...] = jnp.where(slot >= 0.0, slot, (row + layer + table) * WIDE + lam)
    row_ref[...], lam_ref[...] = row, lam


def sort_kernel(field_ref, row_ref, lam_ref, after_ref, order_ref):
    size = row_ref.shape[0]
    span = BLOCK * size // WIDE
    row, lam = row_ref[...], lam_ref[...]
    for k in range(size // BLOCK):
        picks, marks = [], []
        for i in range(k * BLOCK, (k + 1) * BLOCK):
            hit = row_iota(span) == row[i : i + 1]
            picks.append(
                jnp.concatenate(
                    [jnp.where(hit, field_ref[f, i : i + 1, :], 0.0) for f in range(2)], axis=0
                ).astype(BF16)
            )
            marks.append(onehot(lam[i : i + 1], WIDE))
        sorted_rows = transposed_dot(lanes(picks), lanes(marks))
        for f in range(2):
            order_ref[f, k * span : (k + 1) * span, :] = sorted_rows[f * span : (f + 1) * span]


def stay_gather_kernel(layers, start, slope_ref, order_ref, unit_ref, out_ref):
    span = order_ref.shape[1] // unit_ref.shape[0]
    units = span + layers

    def body(j, carry):
        k = j + start
        for u in range(units - 1):
            code = unit_ref[k, u]
            at = k * span + lax.div(code, layers)
            lc, r = order_ref[0, pl.ds(at, 1), :], order_ref[1, pl.ds(at, 1), :]
            for f, value in enumerate(gather_unit(layers, slope_ref, code, lc, r)):
                out_ref[j, f * units + u : f * units + u + 1, :] = value
        for f in range(2):
            out_ref[j, (f + 1) * units - 1 : (f + 1) * units, :] = jnp.zeros((1, WIDE), F32)
        return carry

    lax.fori_loop(0, out_ref.shape[0], body, 0)


def late_gather_kernel(layers, start, slope_ref, order_ref, unit_ref, value_ref, out_ref, value_hbm, sem):
    copy = pltpu.make_async_copy(value_ref, value_hbm, sem)
    copy.start()
    stay_gather_kernel(layers, start, slope_ref, order_ref, unit_ref, out_ref)
    copy.wait()


def reply_kernel(nyc, near_ref, after_ref, *refs):
    size = 2 * GROUP
    backs, (a_ref, b_ref) = refs[: nyc - 1], refs[nyc - 1 :]
    a_ref[:size, :] = near_ref[:size, :]
    b_ref[:size, :] = near_ref[size:, :]
    for y, ref in enumerate(backs):
        a_ref[(y + 1) * size : (y + 2) * size, :] = ref[size : 2 * size, :]
        b_ref[(y + 1) * size : (y + 2) * size, :] = ref[2 * size : 3 * size, :]


def unpack_kernel(nyc, backa_ref, backb_ref, *refs):
    backy = refs[: nyc - 1]
    early_ref, late_ref, place_ref, power_ref, out_ref, table_ref = refs[nyc - 1 :]
    groups = [(backa_ref, y) for y in range(nyc)] + [(backb_ref, y) for y in range(nyc)]
    groups += [(ref, 0) for ref in backy]
    sent, units = len(groups) * GROUP, early_ref.shape[1] // 2
    table = sent + units
    for f in range(2):
        whole = jnp.concatenate(
            [ref[(2 * at + f) * GROUP : (2 * at + f + 1) * GROUP, :] for ref, at in groups], axis=0
        )
        for part, piece in enumerate(pieces(whole)):
            at = (part * 2 + f) * table
            table_ref[at : at + sent, :] = piece

    def body(stay_ref, start, k, carry):
        base = pl.multiple_of((k + start) * BLOCK, BLOCK)
        for f in range(2):
            for part, piece in enumerate(pieces(stay_ref[k, f * units : (f + 1) * units, :])):
                at = (part * 2 + f) * table + sent
                table_ref[at : at + units, :] = piece
        source = table_ref[...].astype(BF16)
        places = place_ref[pl.ds(base, BLOCK), :]
        qs = jnp.floor(places * (1.0 / WIDE))
        lams = places - qs * WIDE
        powers = power_ref[pl.ds(base, BLOCK), :]
        for i in range(0, BLOCK, 8):
            many = lambda x: lanes([x[i + j : i + j + 1] for j in range(8)])
            at = pl.multiple_of(base * 128 + i * 128, 1024)
            found = dot(source, onehot(many(lams), WIDE))
            here = row_iota(table, 1024) == many(qs)
            for f in range(2):
                both = found[f * table : (f + 1) * table] + found[(2 + f) * table : (3 + f) * table]
                value = jnp.sum(jnp.where(here, both, 0.0), axis=0, keepdims=True)
                out_ref[f : f + 1, pl.ds(at, 1024)] = -many(powers) * value
        return carry

    early = early_ref.shape[0]
    lax.fori_loop(0, early, functools.partial(body, early_ref, 0), 0)
    lax.fori_loop(0, late_ref.shape[0], functools.partial(body, late_ref, early), 0)


def call(kernel, outs, scratch, *args, spaces={}, out_spaces={}):
    specs = [pl.BlockSpec(memory_space=spaces.get(i, pltpu.VMEM)) for i in range(len(args))]
    shapes = [jax.ShapeDtypeStruct(shape, dtype) for shape, dtype in outs]
    return pl.pallas_call(
        kernel,
        out_shape=shapes,
        in_specs=specs,
        out_specs=[
            pl.BlockSpec(memory_space=out_spaces.get(i, pltpu.VMEM)) for i in range(len(shapes))
        ],
        scratch_shapes=scratch,
        compiler_params=pltpu.CompilerParams(vmem_limit_bytes=48 * 1024 * 1024),
    )(*args)


def shards(
    cell_bin, cell_layer, cell_offset, cell_power, spill_weight, conductivity, layer_coupling
):
    layers, cols, rows = conductivity.shape
    cells = cell_bin.shape[0]
    nyc = 2 if lax.axis_size("gy") == 2 else 3
    count = layers * cols
    groups = 3 * nyc - 1
    flat = lambda x: x.reshape(cells // 128, 128)
    bins, layer, off = flat(cell_bin), flat(cell_layer), flat(cell_offset)
    power, spill = flat(cell_power), flat(spill_weight)
    square = bins.shape
    split = square[0] * 13 // 16
    own = 3 * GROUP
    message = (nyc * own + layers * HALO, WIDE)
    vmem = lambda *shape: pltpu.VMEM(shape, F32)
    partial = functools.partial

    tile = conductivity.shape
    msg_a, msg_b, own_y, slot, fields, power = call(
        partial(pack_kernel, nyc, layers, cols, rows),
        [
            (message, F32), (message, F32), (((nyc - 1) * own, WIDE), F32),
            (square, F32), ((6, *square), F32), (square, F32),
        ],
        [pltpu.VMEM(square, jnp.int32)] * 3
        + [
            vmem(*square), vmem(2, layers, HALO, rows), pltpu.SemaphoreType.DMA((7,)),
            vmem(6 * groups * GROUP, WIDE),
        ],
        *[
            pltpu.with_memory_space_constraint(x, pltpu.HBM)
            for x in (bins, layer, off, power, spill, conductivity)
        ],
        spaces={i: pltpu.HBM for i in range(6)},
    )
    recv_a, recv_b = exchange(msg_a, 1, 0), exchange(msg_b, 2, 0)
    (stay_grid,) = call(
        partial(stay_deposit_kernel, cols, split),
        [((2 * count, rows), F32)],
        [],
        fields, slot,
    )
    msg_y = call(
        partial(forward_kernel, nyc),
        [((3 * own + 2 * HALO, WIDE), F32)] * (nyc - 1),
        [],
        recv_a, recv_b, own_y, conductivity, stay_grid,
        spaces={4: pl.ANY},
    )
    recv_y = [exchange(m, 0, i + 1) for i, m in enumerate(msg_y)]
    near_grid, near_unit = call(
        partial(near_deposit_kernel, cols, split),
        [((2 * count, rows), F32), ((8, 128), jnp.int32)],
        [],
        stay_grid, recv_a, recv_b, fields, slot,
    )
    table = groups * GROUP
    place, unit, row, lam = call(
        partial(rank_kernel, layers, cols, table),
        [(square, F32), ((square[0] // BLOCK, 128), jnp.int32), (square, F32), (square, F32)],
        [],
        fields, slot, near_grid,
        spaces={2: pl.ANY},
    )
    edge = (layers, HALO, rows)
    outer, edge_a, edge_b = call(
        partial(edge_deposit_kernel, cols),
        [((layers, cols // 2, rows), F32), (edge, F32), (edge, F32)],
        [],
        near_grid, row, *recv_y,
        spaces={1: pl.ANY},
    )
    from_a, from_b = exchange(edge_a, 1, 0), exchange(edge_b, 2, 0)
    (grid,) = call(
        partial(inner_deposit_kernel, cols), [(tile, F32)], [], near_grid, outer, *recv_y
    )
    (order,) = call(
        sort_kernel,
        [((2, cells // WIDE, WIDE), F32)],
        [],
        fields, row, lam, grid,
        spaces={3: pl.ANY},
    )
    edges = call(
        power_edge_kernel,
        [((2 * HALO, WIDE), F32)] * (nyc - 1),
        [],
        grid, from_a, from_b, order,
        spaces={3: pl.ANY},
    )
    from_y = [exchange(e, 0, i + 1) for i, e in enumerate(edges)]
    big = (layers, cols + 2 * HALO, rows + 128)
    *faces, far_unit = call(
        partial(face_kernel, nyc),
        [(big, F32)] * 5 + [((8, 128), jnp.int32)],
        [vmem(*big)],
        conductivity, recv_a, recv_b, layer_coupling, *recv_y,
        spaces={3: pltpu.SMEM},
    )
    warmth, slope = call(
        partial(solve_kernel, nyc),
        [(tile, F32), ((4 * count, rows), BF16)],
        [vmem(*big), vmem(2, layers, big[1] + 16, big[2]), vmem(*big)],
        grid, from_a, from_b, *faces, *from_y,
    )
    answer_y = [
        call(
            partial(gather_kernel, layers, [(0, own * i, 3 * y + i) for i in range(3)]),
            [((6 * GROUP, WIDE), F32)],
            [],
            slope, far_unit, r,
            spaces={1: pltpu.SMEM},
        )[0]
        for y, r in enumerate(recv_y)
    ]
    back_y = [exchange(m, 0, i + 1) for i, m in enumerate(answer_y)]
    (near_answer,) = call(
        partial(gather_kernel, layers, [(0, 0, 0), (1, 0, 1)]),
        [((4 * GROUP, WIDE), F32)],
        [],
        slope, near_unit, recv_a, recv_b,
        spaces={1: pltpu.SMEM},
    )
    blocks, early = square[0] // BLOCK, 1
    units = order.shape[1] // blocks + layers
    (early_value,) = call(
        partial(stay_gather_kernel, layers, 0),
        [((early, 2 * units, WIDE), F32)],
        [],
        slope, order, unit,
        spaces={2: pltpu.SMEM},
    )
    answer_a, answer_b = call(
        partial(reply_kernel, nyc),
        [((2 * nyc * GROUP, WIDE), F32)] * 2,
        [],
        near_answer, early_value, *back_y,
        spaces={1: pl.ANY},
    )
    back_a, back_b = exchange(answer_a, 1, 0), exchange(answer_b, 2, 0)
    late_value, final_warmth = call(
        partial(late_gather_kernel, layers, early),
        [((blocks - early, 2 * units, WIDE), F32), (tile, F32)],
        [pltpu.SemaphoreType.DMA(())],
        slope, order, unit, warmth,
        spaces={2: pltpu.SMEM},
        out_spaces={1: pltpu.HBM},
    )
    (pull,) = call(
        partial(unpack_kernel, nyc),
        [((2, cells), F32)],
        [vmem(4 * (table + units), WIDE)],
        back_a, back_b, *back_y, early_value, late_value, place, power,
    )
    return final_warmth, pull


def solution(mesh):
    cell = P(("gx", "gy"))
    tile = P(None, "gx", "gy")
    return jax.shard_map(
        shards,
        mesh=mesh,
        in_specs=(cell, cell, cell, cell, cell, tile, P()),
        out_specs=(tile, P(None, ("gx", "gy"))),
        check_vma=False,
    )
```

```python
import functools

import jax
import jax.numpy as jnp
from jax import lax
from jax.experimental import pallas as pl
from jax.experimental.pallas import tpu as pltpu
from jax.sharding import PartitionSpec as P

ITERS = 4
CAP = 2048
SINK_RATE = 0.5
LOW_BOUND = 0.5
HIGH_BOUND = 33.0

WIDE = 256
GROUP = CAP // WIDE
BLOCK = 32
HALO = 8
F32, BF16 = jnp.float32, jnp.bfloat16


def partner(place, kind, count):
    if kind == 0:
        return place
    if kind == 1:
        return place ^ 1
    other = place - 1 if place % 2 == 0 else place + 1
    return other if 0 <= other < count else None


def exchange(value, x_kind, y_kind):
    nx, ny = lax.axis_size("gx"), lax.axis_size("gy")
    pairs = []
    for a in range(nx):
        for b in range(ny):
            x, y = partner(a, x_kind, nx), partner(b, y_kind, ny)
            if x is None:
                x, y = a, b ^ 1
            elif y is None:
                x, y = a ^ 1, b
            pairs.append((a * ny + b, x * ny + y))
    return lax.ppermute(value, ("gx", "gy"), pairs)


def pieces(value):
    high = value.astype(BF16).astype(F32)
    return high, value - high


def row_iota(count, width=128):
    return lax.broadcasted_iota(jnp.int32, (count, width), 0).astype(F32)


def onehot(row, count):
    return jnp.where(
        row_iota(count, row.shape[1]).astype(BF16) == row.astype(BF16),
        jnp.ones((), BF16),
        jnp.zeros((), BF16),
    )


def lanes(parts):
    return jnp.concatenate(parts, axis=1) if len(parts) > 1 else parts[0]


def transposed_dot(left, right):
    return lax.dot_general(left, right, (((1,), (1,)), ((), ())), preferred_element_type=F32)


def dot(left, right):
    return lax.dot_general(left, right, (((1,), (0,)), ((), ())), preferred_element_type=F32)


def kind_of(step, place):
    ahead = 1 - 2 * lax.rem(place, 2)
    return jnp.where(step == 0, 0, jnp.where(step == ahead, 1, 2))


def pack_kernel(
    nyc, layers, cols, rows,
    bin_hbm, layer_hbm, off_hbm, power_hbm, spill_hbm, cond_hbm,
    msga_ref, msgb_ref, owny_ref, slot_ref, field_ref, power_ref,
    bin_ref, layer_ref, off_ref, spill_ref, edge_ref, sems, acc_ref,
):
    a, b = lax.axis_index("gx"), lax.axis_index("gy")
    copies = [
        pltpu.make_async_copy(src, dst, sems.at[i])
        for i, (src, dst) in enumerate(
            [
                (off_hbm, off_ref), (layer_hbm, layer_ref), (bin_hbm, bin_ref),
                (power_hbm, power_ref), (spill_hbm, spill_ref),
                (cond_hbm.at[:, :HALO, :], edge_ref.at[0]),
                (cond_hbm.at[:, cols - HALO :, :], edge_ref.at[1]),
            ]
        )
    ]
    for copy in copies:
        copy.start()
    acc_ref[...] = jnp.zeros_like(acc_ref)
    groups = 3 * nyc - 1
    table = groups * GROUP
    copies[0].wait()
    copies[1].wait()
    off = off_ref[...]
    col_code = (off >= 3).astype(jnp.int32) + (off >= 6).astype(jnp.int32)
    x_kind = kind_of(col_code - 1, a)
    y_kind = kind_of(off - 3 * col_code - 1, b)
    group = jnp.where(x_kind > 0, (x_kind - 1) * nyc + y_kind, 2 * nyc - 1 + y_kind)
    key = jnp.where(off == 4, -1, group * layers + layer_ref[...])
    size = off.shape[0]
    r_i = lax.broadcasted_iota(jnp.int32, (size, size), 0)
    c_i = lax.broadcasted_iota(jnp.int32, (size, size), 1)
    flag = lambda x: jnp.where(x, 1.0, 0.0).astype(BF16)
    ones = jnp.ones((size, size), BF16)
    before = jnp.concatenate([flag(r_i < c_i), ones], axis=1)
    rank = jnp.zeros((size, size), F32)
    counts = jnp.zeros((size, size), F32)
    for g in range(groups):
        keys = range(g * layers, (g + 1) * layers)
        counted = dot(jnp.concatenate([flag(key == k) for k in keys], axis=0), before)
        for i, k in enumerate(keys):
            block = counted[i * size : (i + 1) * size]
            rank = jnp.where(key == k, block[:, :size], rank)
            counts = jnp.where(c_i == k, block[:, size:], counts)
    narrow = counts.astype(BF16)
    ahead = dot(narrow, flag((r_i // layers == c_i // layers) & (r_i < c_i))).astype(BF16)
    base = dot(
        jnp.concatenate([flag(r_i > c_i), ones], axis=1), jnp.concatenate([narrow, ahead], axis=0)
    )
    base = jnp.take_along_axis(base, jnp.maximum(key, 0), axis=1, mode="promise_in_bounds")
    slot = jnp.where(key >= 0, rank + base + (group * CAP).astype(F32), -1.0)
    slot_ref[...] = slot
    for copy in copies[2:]:
        copy.wait()
    code = layer_ref[...] * (cols * rows) + bin_ref[...]
    field_ref[0] = (code // rows).astype(F32)
    field_ref[1] = (code % rows).astype(F32)
    power = power_ref[...]
    spill = spill_ref[...]
    field_ref[2], field_ref[3] = pieces(power * (1.0 - spill))
    field_ref[4], field_ref[5] = pieces(power * spill)
    step = 64

    def body(j, carry):
        base = pl.multiple_of(j * step, step)
        slots = slot_ref[pl.ds(base, step), :]
        qs = jnp.floor(slots * (1.0 / WIDE))
        lams = slots - qs * WIDE
        vals = [field_ref[f, pl.ds(base, step), :] for f in range(6)]
        picks, marks = [], []
        for i in range(step):
            hit = row_iota(table) == qs[i : i + 1]
            picks.append(
                jnp.concatenate([jnp.where(hit, v[i : i + 1], 0.0) for v in vals], axis=0).astype(BF16)
            )
            marks.append(onehot(lams[i : i + 1], WIDE))
        acc_ref[...] += transposed_dot(lanes(picks), lanes(marks))
        return carry

    lax.fori_loop(0, size // step, body, 0)
    out = [acc_ref[f * table : (f + 1) * table, :] for f in range(6)]
    sent = [out[0] * float(rows) + out[1], out[2] + out[3], out[4] + out[5]]

    def put(ref, at, g):
        for f in range(3):
            ref[(at * 3 + f) * GROUP : (at * 3 + f + 1) * GROUP, :] = sent[f][
                g * GROUP : (g + 1) * GROUP
            ]

    for y in range(nyc):
        put(msga_ref, y, y)
        put(msgb_ref, y, nyc + y)
        if y:
            put(owny_ref, y - 1, 2 * nyc + y - 1)
    first, last = edge_ref[0], edge_ref[1]
    even = lax.rem(a, 2) == 0
    top = nyc * 3 * GROUP
    flat = (-1, rows)
    msga_ref[top:, :] = jnp.where(even, last, first).reshape(flat)
    msgb_ref[top:, :] = jnp.where(even, first, last).reshape(flat)


def deposit_block(lc, r, main, spill, cols, cells, part=None):
    picks, marks = [], []
    zero = jnp.zeros((), BF16)
    narrow = lambda x: x.astype(BF16)
    quarter = cols // 4
    count = cells if part is None else cells // 2
    for lc_i, r_i, (mh, ml), (sh, sl) in zip(lc, r, main, spill):
        spot = narrow(row_iota(count, lc_i.shape[1]))
        step = cols
        other = lambda at: jnp.where(lc_i >= float(cells - cols), at - step, at + step)
        if part is None:
            there_i = other(lc_i)
        else:
            step = cols // 2
            layer = jnp.floor(lc_i * (1.0 / cols))
            column = lc_i - layer * cols
            inner = (column >= quarter) & (column < 3 * quarter)
            if part == "inner":
                mine, at = inner, layer * step + (column - quarter)
            else:
                mine = jnp.logical_not(inner)
                at = layer * step + jnp.where(column < quarter, column, column - step)
            there_i = jnp.where(mine, other(at), -1.0)
            lc_i = jnp.where(mine, at, -1.0)
        here, there = spot == narrow(lc_i), spot == narrow(there_i)
        high = jnp.where(here, narrow(mh), jnp.where(there, narrow(sh), zero))
        low = jnp.where(here, narrow(ml), jnp.where(there, narrow(sl), zero))
        picks.append(jnp.concatenate([high, low], axis=0))
        marks.append(onehot(r_i, WIDE))
    return transposed_dot(lanes(picks), lanes(marks))


def deposit_stays(grid_ref, field_ref, slot_ref, first, last, cols):
    count, step = grid_ref.shape[0] // 2, 32
    stays = slot_ref[first:last, :] < 0.0
    vals = [jnp.where(stays, field_ref[2 + f, first:last, :], 0.0) for f in range(4)]
    lcs, rs = field_ref[0, first:last, :], field_ref[1, first:last, :]
    for base in range(0, last - first, step):
        rows_of = lambda x: [x[base + i : base + i + 1] for i in range(step)]
        parts = [rows_of(v) for v in vals]
        grid_ref[...] += deposit_block(
            rows_of(lcs), rows_of(rs), list(zip(parts[0], parts[1])),
            list(zip(parts[2], parts[3])), cols, count,
        )


def stay_deposit_kernel(cols, split, field_ref, slot_ref, grid_ref):
    grid_ref[...] = jnp.zeros_like(grid_ref)
    deposit_stays(grid_ref, field_ref, slot_ref, 0, split, cols)


def group_deposit(sources, cols, count, part=None):
    lc, r, main, spill = [], [], [], []
    for ref, at in sources:
        rows = ref.shape[1]
        for row in range(at, at + GROUP):
            code = ref[row : row + 1, :]
            lc_i = jnp.floor(code * (1.0 / rows))
            lc.append(lc_i)
            r.append(code - lc_i * rows)
            main.append(pieces(ref[row + GROUP : row + GROUP + 1, :]))
            spill.append(pieces(ref[row + 2 * GROUP : row + 2 * GROUP + 1, :]))
    return deposit_block(lc, r, main, spill, cols, count, part)


def count_units(unit_ref, sources, layers, cells):
    unit_ref[...] = jnp.zeros_like(unit_ref)
    lane = lax.broadcasted_iota(jnp.int32, (1, 128), 1).astype(F32)
    for g, (ref, at) in enumerate(sources):
        layer = jnp.floor(ref[at : at + GROUP, :] * (1.0 / cells))
        layer = jnp.where(ref[at + GROUP : at + 2 * GROUP, :] > 0.0, layer, float(layers))
        passed = jnp.zeros((1, 128), F32)
        for l in range(layers - 1):
            end = jnp.sum(jnp.where(layer <= l, 1.0, 0.0), axis=0, keepdims=True)
            end = jnp.floor(jnp.sum(end, axis=1, keepdims=True) * (1.0 / WIDE))
            passed = passed + jnp.where(jnp.minimum(end, GROUP - 1.0) + l < lane, 1.0, 0.0)
        unit_ref[g : g + 1, :] = ((lane - passed) * layers + passed).astype(jnp.int32)


def near_deposit_kernel(
    cols, split, stay_ref, recva_ref, recvb_ref, field_ref, slot_ref, grid_ref, unit_ref
):
    count, rows = grid_ref.shape[0] // 2, grid_ref.shape[1]
    count_units(unit_ref, [(recva_ref, 0), (recvb_ref, 0)], count // cols, cols * rows)
    grid_ref[...] = stay_ref[...]
    deposit_stays(grid_ref, field_ref, slot_ref, split, slot_ref.shape[0], cols)
    grid_ref[...] += group_deposit([(recva_ref, 0), (recvb_ref, 0)], cols, count)


def half_deposit(near_ref, recvy, cols, part):
    count, rows = near_ref.shape[0] // 2, near_ref.shape[1]
    layers = count // cols
    far = group_deposit([(ref, 3 * GROUP * i) for ref in recvy for i in range(3)], cols, count, part)
    far = far[: count // 2] + far[count // 2 :]
    near = (near_ref[:count, :] + near_ref[count:, :]).reshape(layers, cols, rows)
    quarter = cols // 4
    if part == "inner":
        near = near[:, quarter : 3 * quarter]
    else:
        near = jnp.concatenate([near[:, :quarter], near[:, 3 * quarter :]], axis=1)
    return near + far.reshape(layers, cols // 2, rows)


def edge_deposit_kernel(cols, near_ref, after_ref, *refs):
    recvy, (outer_ref, edgea_ref, edgeb_ref) = refs[:-3], refs[-3:]
    outer = half_deposit(near_ref, recvy, cols, "edge")
    outer_ref[...] = outer
    first, last = outer[:, :HALO], outer[:, cols // 2 - HALO :]
    even = lax.rem(lax.axis_index("gx"), 2) == 0
    edgea_ref[...] = jnp.where(even, last, first)
    edgeb_ref[...] = jnp.where(even, first, last)


def inner_deposit_kernel(cols, near_ref, outer_ref, *refs):
    recvy, grid_ref = refs[:-1], refs[-1]
    quarter = cols // 4
    grid_ref[:, :quarter, :] = outer_ref[:, :quarter, :]
    grid_ref[:, 3 * quarter :, :] = outer_ref[:, quarter:, :]
    grid_ref[:, quarter : 3 * quarter, :] = half_deposit(near_ref, recvy, cols, "inner")


def with_columns(own, from_a, from_b):
    a = lax.axis_index("gx")
    even = lax.rem(a, 2) == 0
    right = jnp.where(even, from_a, from_b)
    left = jnp.where(even, from_b, from_a)
    right = jnp.where(a < lax.axis_size("gx") - 1, right, 0.0)
    left = jnp.where(a > 0, left, 0.0)
    return jnp.concatenate([left, own, right], axis=1)


def row_edge(wide, last):
    rows = wide.shape[1]
    tile = jnp.where(last, wide[:, rows - 128 :], wide[:, :128]).T
    return jnp.where(last, tile[128 - HALO :], tile[:HALO])


def put_edges(ref, at, edge):
    extra = edge.shape[1] - WIDE
    ref[at : at + HALO, :] = edge[:, :WIDE]
    ref[at + HALO : at + 2 * HALO, :] = jnp.concatenate(
        [edge[:, WIDE:], jnp.zeros((HALO, WIDE - extra), F32)], axis=1
    )


def get_edges(ref, at, count):
    return jnp.concatenate(
        [ref[at : at + HALO, :], ref[at + HALO : at + 2 * HALO, : count - WIDE]], axis=1
    )


def y_edges(refs, at, wide):
    even = lax.rem(lax.axis_index("gy"), 2) == 0
    for kind, ref in enumerate(refs):
        put_edges(ref, at, row_edge(wide, even if kind == 0 else jnp.logical_not(even)))


def halo_of(ref, cols, layers, top):
    return ref[top:, :].reshape(layers, HALO, ref.shape[1])


def forward_kernel(nyc, recva_ref, recvb_ref, owny_ref, cond_ref, after_ref, *msgy_refs):
    layers, cols, rows = cond_ref.shape
    size, top = 3 * GROUP, nyc * 3 * GROUP
    for y, ref in enumerate(msgy_refs):
        ref[:size, :] = owny_ref[y * size : (y + 1) * size, :]
        ref[size : 2 * size, :] = recva_ref[(y + 1) * size : (y + 2) * size, :]
        ref[2 * size : 3 * size, :] = recvb_ref[(y + 1) * size : (y + 2) * size, :]
    wide = with_columns(
        cond_ref[...], halo_of(recva_ref, cols, layers, top), halo_of(recvb_ref, cols, layers, top)
    )
    y_edges(msgy_refs, 3 * size, wide.reshape(-1, rows))


def power_edge_kernel(grid_ref, froma_ref, fromb_ref, after_ref, *edge_refs):
    wide = with_columns(grid_ref[...], froma_ref[...], fromb_ref[...])
    y_edges(edge_refs, 0, wide.reshape(-1, grid_ref.shape[2]))


def with_rows(wide, edges):
    b, ny = lax.axis_index("gy"), lax.axis_size("gy")
    layers, span, rows = wide.shape
    count = layers * span
    even = lax.rem(b, 2) == 0
    one = edges[0]
    two = edges[1] if len(edges) > 1 else jnp.zeros_like(one)
    after = jnp.where(b < ny - 1, jnp.where(even, one, two), 0.0)
    before = jnp.where(b > 0, jnp.where(even, two, one), 0.0)
    tile = jnp.concatenate([after, jnp.zeros((128 - 2 * HALO, count), F32), before], axis=0).T
    return jnp.concatenate([wide, tile.reshape(layers, span, 128)], axis=2)


def face_kernel(nyc, cond_ref, recva_ref, recvb_ref, coupling_ref, *refs):
    recvy_refs = refs[: nyc - 1]
    cn_ref, cp_ref, rn_ref, fl_ref, d_ref, unit_ref, k_ref = refs[nyc - 1 :]
    layers, cols, rows = cond_ref.shape
    span, wide_rows = cols + 2 * HALO, rows + 128
    count = layers * span
    top = nyc * 3 * GROUP
    sources = [(ref, 3 * GROUP * i) for ref in recvy_refs for i in range(3)]
    count_units(unit_ref, sources, layers, cols * rows)
    a, b = lax.axis_index("gx"), lax.axis_index("gy")
    nx, ny = lax.axis_size("gx"), lax.axis_size("gy")
    k_ref[...] = with_rows(
        with_columns(
            cond_ref[...],
            halo_of(recva_ref, cols, layers, top),
            halo_of(recvb_ref, cols, layers, top),
        ),
        [get_edges(ref, 9 * GROUP, count) for ref in recvy_refs],
    )
    shape = (span, wide_rows)
    c_i = lax.broadcasted_iota(jnp.int32, shape, 0)
    r_i = lax.broadcasted_iota(jnp.int32, shape, 1)
    c_low = jnp.where(a > 0, 0, HALO)
    c_high = jnp.where(a < nx - 1, span, span - HALO)
    r_high = jnp.where(b < ny - 1, rows + HALO, rows)
    r_low = jnp.where(b > 0, wide_rows - HALO, wide_rows)
    inside = jnp.where((c_i >= c_low) & (c_i < c_high) & ((r_i < r_high) | (r_i >= r_low)), 1.0, 0.0)
    next_c = lambda x: pltpu.roll(x, span - 1, 0)
    prev_c = lambda x: pltpu.roll(x, 1, 0)
    next_r = lambda x: pltpu.roll(x, wide_rows - 1, 1)
    prev_r = lambda x: pltpu.roll(x, 1, 1)
    both_c, both_r = inside * next_c(inside), inside * next_r(inside)
    below = None
    for l in range(layers):
        k = k_ref[l]
        face_c, face_r = 0.5 * (k + next_c(k)), 0.5 * (k + next_r(k))
        kept_c, kept_r = face_c * both_c, face_r * both_r
        cn_ref[l], cp_ref[l] = kept_c, prev_c(kept_c)
        rn_ref[l] = kept_r
        total = SINK_RATE + ((face_c + prev_c(face_c)) + (face_r + prev_r(face_r)))
        if below is not None:
            total = total + below
        if l + 1 < layers:
            below = coupling_ref[l] * (0.5 * (k + k_ref[l + 1]))
            fl_ref[l] = below * inside
            total = total + below
        d_ref[l] = total


def solve_kernel(
    nyc, grid_ref, froma_ref, fromb_ref, cn_ref, cp_ref, rn_ref, fl_ref, d_ref, *refs
):
    edge_refs, (warmth_ref, slope_ref, p_ref, v_ref, u_ref) = refs[: nyc - 1], refs[nyc - 1 :]
    layers, cols, rows = grid_ref.shape
    span, wide_rows = cols + 2 * HALO, rows + 128
    p_ref[...] = with_rows(
        with_columns(grid_ref[...], froma_ref[...], fromb_ref[...]),
        [get_edges(ref, 0, layers * span) for ref in edge_refs],
    )
    next_r = lambda x: pltpu.roll(x, wide_rows - 1, 1)
    prev_r = lambda x: pltpu.roll(x, 1, 1)
    middle = 0.5 * (HIGH_BOUND + LOW_BOUND)
    spread = 0.5 * (HIGH_BOUND - LOW_BOUND)
    sigma = middle / spread
    now = 1.0 / sigma
    blank = jnp.zeros((8, wide_rows), F32)
    for l in range(layers):
        for side in range(2):
            v_ref[side, l, :8, :] = blank
            v_ref[side, l, 8 + span :, :] = blank
        v_ref[0, l, 8 : 8 + span, :] = p_ref[l] * (1.0 / middle)
    for sweep in range(ITERS):
        later = 1.0 / (2.0 * sigma - now)
        keep, gain = later * now, 2.0 * later / spread
        old, new = sweep % 2, (sweep + 1) % 2
        for c in range(0, span, 8):
            at, here = slice(c, c + 8), slice(c + 8, c + 16)
            vs = [v_ref[old, l, here, :] for l in range(layers)]
            for l in range(layers):
                v = vs[l]
                rest = p_ref[l, at, :] - d_ref[l, at, :] * v
                rest = rest + cn_ref[l, at, :] * v_ref[old, l, c + 9 : c + 17, :]
                rest = rest + cp_ref[l, at, :] * v_ref[old, l, c + 7 : c + 15, :]
                after = rn_ref[l, at, :]
                rest = rest + (after * next_r(v) + prev_r(after * v))
                if l + 1 < layers:
                    rest = rest + fl_ref[l, at, :] * vs[l + 1]
                if l:
                    rest = rest + fl_ref[l - 1, at, :] * vs[l - 1]
                advance = keep * (u_ref[l, at, :] if sweep else v) + gain * rest
                if sweep + 1 < ITERS:
                    u_ref[l, at, :] = advance
                v_ref[new, l, here, :] = v + advance
        now = later
    final = ITERS % 2
    for l in range(layers):
        warmth_ref[l] = v_ref[final, l, 8 + HALO : 8 + HALO + cols, :rows]
        for c in range(0, cols, 16):
            at = 8 + HALO + c
            v = v_ref[final, l, at : at + 16, :]
            slopes = (
                0.5 * (v_ref[final, l, at + 1 : at + 17, :rows] - v_ref[final, l, at - 1 : at + 15, :rows]),
                0.5 * (next_r(v) - prev_r(v))[:, :rows],
            )
            for f, slope in enumerate(slopes):
                for part, piece in enumerate(pieces(slope)):
                    put = ((l * 2 + part) * 2 + f) * cols + c
                    slope_ref[put : put + 16, :] = piece.astype(BF16)


def pick(found, lc, first):
    cols = found.shape[0] // 4
    here = row_iota(cols, lc.shape[1]) == lc - first
    return [
        jnp.where(here, found[f * cols : (f + 1) * cols] + found[(2 + f) * cols : (3 + f) * cols], 0.0)
        for f in range(2)
    ]


def gather_unit(layers, slope_ref, code, lc, r):
    size = slope_ref.shape[0] // layers
    layer = lax.rem(code, layers)
    rows = slope_ref[pl.ds(pl.multiple_of(layer * size, size), size), :]
    found = dot(rows, onehot(r, slope_ref.shape[1]))
    first = (layer * (size // 4)).astype(F32)
    return [jnp.sum(part, axis=0, keepdims=True) for part in pick(found, lc, first)]


def gather_kernel(layers, sources, slope_ref, unit_ref, *refs):
    ins, out_ref = refs[:-1], refs[-1]
    rows = slope_ref.shape[1]
    for g, (which, at, line) in enumerate(sources):
        totals = [jnp.zeros((GROUP, WIDE), F32)] * 2
        for u in range(GROUP + layers - 1):
            code = unit_ref[line, u]
            row = lax.div(code, layers)
            slots = ins[which][pl.ds(at + row, 1), :]
            lc = jnp.floor(slots * (1.0 / rows))
            hit = row_iota(GROUP, WIDE) == row.astype(F32)
            for f, value in enumerate(gather_unit(layers, slope_ref, code, lc, slots - lc * rows)):
                totals[f] = totals[f] + jnp.where(hit, value, 0.0)
        for f in range(2):
            out_ref[(g * 2 + f) * GROUP : (g * 2 + f + 1) * GROUP, :] = totals[f]


def rank_kernel(layers, cols, table, field_ref, slot_ref, after_ref, place_ref, unit_ref, row_ref, lam_ref):
    size = slot_ref.shape[0]
    span = BLOCK * size // WIDE
    r_i = lax.broadcasted_iota(jnp.int32, (size, size), 0)
    c_i = lax.broadcasted_iota(jnp.int32, (size, size), 1)
    flag = lambda x: jnp.where(x, 1.0, 0.0).astype(BF16)
    upper, ones = flag(r_i < c_i), jnp.ones((size, size), BF16)
    same = (r_i // BLOCK) == (c_i // BLOCK)
    both = jnp.concatenate([flag(same & (r_i > c_i)), flag(same)], axis=1)
    layer = jnp.floor(field_ref[0] * (1.0 / cols))
    ahead = jnp.zeros((size, size), F32)
    rank = jnp.zeros((size, size), F32)
    lane = lax.broadcasted_iota(jnp.int32, (size, size), 1).astype(F32)
    passed = jnp.zeros((size, size), F32)
    for l in range(layers):
        mine = layer == float(l)
        mask = flag(mine)
        totals = dot(mask, ones)
        stack = jnp.concatenate([totals.astype(BF16), ahead.astype(BF16)], axis=0)
        rank = jnp.where(mine, dot(mask, upper) + dot(both, stack), rank)
        ahead = ahead + totals
        if l + 1 < layers:
            end = jnp.floor(dot(both[:, size:], ahead.astype(BF16)) * (1.0 / WIDE))
            passed = passed + jnp.where(jnp.minimum(end, span - 1.0) + l < lane, 1.0, 0.0)
    unit = ((lane - passed) * layers + passed).astype(jnp.int32)
    for k in range(size // BLOCK):
        unit_ref[k : k + 1, :] = unit[k * BLOCK : k * BLOCK + 1]
    row = jnp.floor(rank * (1.0 / WIDE))
    lam = rank - row * WIDE
    slot = slot_ref[...]
    place_ref[...] = jnp.where(slot >= 0.0, slot, (row + layer + table) * WIDE + lam)
    row_ref[...], lam_ref[...] = row, lam


def sort_kernel(field_ref, row_ref, lam_ref, after_ref, order_ref):
    size = row_ref.shape[0]
    span = BLOCK * size // WIDE
    row, lam = row_ref[...], lam_ref[...]
    for k in range(size // BLOCK):
        picks, marks = [], []
        for i in range(k * BLOCK, (k + 1) * BLOCK):
            hit = row_iota(span) == row[i : i + 1]
            picks.append(
                jnp.concatenate(
                    [jnp.where(hit, field_ref[f, i : i + 1, :], 0.0) for f in range(2)], axis=0
                ).astype(BF16)
            )
            marks.append(onehot(lam[i : i + 1], WIDE))
        sorted_rows = transposed_dot(lanes(picks), lanes(marks))
        for f in range(2):
            order_ref[f, k * span : (k + 1) * span, :] = sorted_rows[f * span : (f + 1) * span]


def stay_gather_kernel(layers, start, slope_ref, order_ref, unit_ref, out_ref):
    span = order_ref.shape[1] // unit_ref.shape[0]
    units = span + layers

    def body(j, carry):
        k = j + start
        for u in range(units - 1):
            code = unit_ref[k, u]
            at = k * span + lax.div(code, layers)
            lc, r = order_ref[0, pl.ds(at, 1), :], order_ref[1, pl.ds(at, 1), :]
            for f, value in enumerate(gather_unit(layers, slope_ref, code, lc, r)):
                out_ref[j, f * units + u : f * units + u + 1, :] = value
        for f in range(2):
            out_ref[j, (f + 1) * units - 1 : (f + 1) * units, :] = jnp.zeros((1, WIDE), F32)
        return carry

    lax.fori_loop(0, out_ref.shape[0], body, 0)


def late_gather_kernel(layers, start, slope_ref, order_ref, unit_ref, value_ref, out_ref, value_hbm, sem):
    copy = pltpu.make_async_copy(value_ref, value_hbm, sem)
    copy.start()
    stay_gather_kernel(layers, start, slope_ref, order_ref, unit_ref, out_ref)
    copy.wait()


def reply_kernel(nyc, near_ref, after_ref, *refs):
    size = 2 * GROUP
    backs, (a_ref, b_ref) = refs[: nyc - 1], refs[nyc - 1 :]
    a_ref[:size, :] = near_ref[:size, :]
    b_ref[:size, :] = near_ref[size:, :]
    for y, ref in enumerate(backs):
        a_ref[(y + 1) * size : (y + 2) * size, :] = ref[size : 2 * size, :]
        b_ref[(y + 1) * size : (y + 2) * size, :] = ref[2 * size : 3 * size, :]


def unpack_kernel(nyc, backa_ref, backb_ref, *refs):
    backy = refs[: nyc - 1]
    early_ref, late_ref, place_ref, power_ref, out_ref, table_ref = refs[nyc - 1 :]
    groups = [(backa_ref, y) for y in range(nyc)] + [(backb_ref, y) for y in range(nyc)]
    groups += [(ref, 0) for ref in backy]
    sent, units = len(groups) * GROUP, early_ref.shape[1] // 2
    table = sent + units
    for f in range(2):
        whole = jnp.concatenate(
            [ref[(2 * at + f) * GROUP : (2 * at + f + 1) * GROUP, :] for ref, at in groups], axis=0
        )
        for part, piece in enumerate(pieces(whole)):
            at = (part * 2 + f) * table
            table_ref[at : at + sent, :] = piece

    def body(stay_ref, start, k, carry):
        base = pl.multiple_of((k + start) * BLOCK, BLOCK)
        for f in range(2):
            for part, piece in enumerate(pieces(stay_ref[k, f * units : (f + 1) * units, :])):
                at = (part * 2 + f) * table + sent
                table_ref[at : at + units, :] = piece
        source = table_ref[...].astype(BF16)
        places = place_ref[pl.ds(base, BLOCK), :]
        qs = jnp.floor(places * (1.0 / WIDE))
        lams = places - qs * WIDE
        powers = power_ref[pl.ds(base, BLOCK), :]
        for i in range(0, BLOCK, 8):
            many = lambda x: lanes([x[i + j : i + j + 1] for j in range(8)])
            at = pl.multiple_of(base * 128 + i * 128, 1024)
            found = dot(source, onehot(many(lams), WIDE))
            here = row_iota(table, 1024) == many(qs)
            for f in range(2):
                both = found[f * table : (f + 1) * table] + found[(2 + f) * table : (3 + f) * table]
                value = jnp.sum(jnp.where(here, both, 0.0), axis=0, keepdims=True)
                out_ref[f : f + 1, pl.ds(at, 1024)] = -many(powers) * value
        return carry

    early = early_ref.shape[0]
    lax.fori_loop(0, early, functools.partial(body, early_ref, 0), 0)
    lax.fori_loop(0, late_ref.shape[0], functools.partial(body, late_ref, early), 0)


def call(kernel, outs, scratch, *args, spaces={}, out_spaces={}):
    specs = [pl.BlockSpec(memory_space=spaces.get(i, pltpu.VMEM)) for i in range(len(args))]
    shapes = [jax.ShapeDtypeStruct(shape, dtype) for shape, dtype in outs]
    return pl.pallas_call(
        kernel,
        out_shape=shapes,
        in_specs=specs,
        out_specs=[
            pl.BlockSpec(memory_space=out_spaces.get(i, pltpu.VMEM)) for i in range(len(shapes))
        ],
        scratch_shapes=scratch,
        compiler_params=pltpu.CompilerParams(vmem_limit_bytes=48 * 1024 * 1024),
    )(*args)


def shards(
    cell_bin, cell_layer, cell_offset, cell_power, spill_weight, conductivity, layer_coupling
):
    layers, cols, rows = conductivity.shape
    cells = cell_bin.shape[0]
    nyc = 2 if lax.axis_size("gy") == 2 else 3
    count = layers * cols
    groups = 3 * nyc - 1
    flat = lambda x: x.reshape(cells // 128, 128)
    bins, layer, off = flat(cell_bin), flat(cell_layer), flat(cell_offset)
    power, spill = flat(cell_power), flat(spill_weight)
    square = bins.shape
    split = square[0] * 3 // 4
    own = 3 * GROUP
    message = (nyc * own + layers * HALO, WIDE)
    vmem = lambda *shape: pltpu.VMEM(shape, F32)
    partial = functools.partial

    tile = conductivity.shape
    msg_a, msg_b, own_y, slot, fields, power = call(
        partial(pack_kernel, nyc, layers, cols, rows),
        [
            (message, F32), (message, F32), (((nyc - 1) * own, WIDE), F32),
            (square, F32), ((6, *square), F32), (square, F32),
        ],
        [pltpu.VMEM(square, jnp.int32)] * 3
        + [
            vmem(*square), vmem(2, layers, HALO, rows), pltpu.SemaphoreType.DMA((7,)),
            vmem(6 * groups * GROUP, WIDE),
        ],
        *[
            pltpu.with_memory_space_constraint(x, pltpu.HBM)
            for x in (bins, layer, off, power, spill, conductivity)
        ],
        spaces={i: pltpu.HBM for i in range(6)},
    )
    recv_a, recv_b = exchange(msg_a, 1, 0), exchange(msg_b, 2, 0)
    (stay_grid,) = call(
        partial(stay_deposit_kernel, cols, split),
        [((2 * count, rows), F32)],
        [],
        fields, slot,
    )
    msg_y = call(
        partial(forward_kernel, nyc),
        [((3 * own + 2 * HALO, WIDE), F32)] * (nyc - 1),
        [],
        recv_a, recv_b, own_y, conductivity, stay_grid,
        spaces={4: pl.ANY},
    )
    recv_y = [exchange(m, 0, i + 1) for i, m in enumerate(msg_y)]
    near_grid, near_unit = call(
        partial(near_deposit_kernel, cols, split),
        [((2 * count, rows), F32), ((8, 128), jnp.int32)],
        [],
        stay_grid, recv_a, recv_b, fields, slot,
    )
    table = groups * GROUP
    place, unit, row, lam = call(
        partial(rank_kernel, layers, cols, table),
        [(square, F32), ((square[0] // BLOCK, 128), jnp.int32), (square, F32), (square, F32)],
        [],
        fields, slot, near_grid,
        spaces={2: pl.ANY},
    )
    edge = (layers, HALO, rows)
    outer, edge_a, edge_b = call(
        partial(edge_deposit_kernel, cols),
        [((layers, cols // 2, rows), F32), (edge, F32), (edge, F32)],
        [],
        near_grid, row, *recv_y,
        spaces={1: pl.ANY},
    )
    from_a, from_b = exchange(edge_a, 1, 0), exchange(edge_b, 2, 0)
    (grid,) = call(
        partial(inner_deposit_kernel, cols), [(tile, F32)], [], near_grid, outer, *recv_y
    )
    (order,) = call(
        sort_kernel,
        [((2, cells // WIDE, WIDE), F32)],
        [],
        fields, row, lam, grid,
        spaces={3: pl.ANY},
    )
    edges = call(
        power_edge_kernel,
        [((2 * HALO, WIDE), F32)] * (nyc - 1),
        [],
        grid, from_a, from_b, order,
        spaces={3: pl.ANY},
    )
    from_y = [exchange(e, 0, i + 1) for i, e in enumerate(edges)]
    big = (layers, cols + 2 * HALO, rows + 128)
    *faces, far_unit = call(
        partial(face_kernel, nyc),
        [(big, F32)] * 5 + [((8, 128), jnp.int32)],
        [vmem(*big)],
        conductivity, recv_a, recv_b, layer_coupling, *recv_y,
        spaces={3: pltpu.SMEM},
    )
    warmth, slope = call(
        partial(solve_kernel, nyc),
        [(tile, F32), ((4 * count, rows), BF16)],
        [vmem(*big), vmem(2, layers, big[1] + 16, big[2]), vmem(*big)],
        grid, from_a, from_b, *faces, *from_y,
    )
    answer_y = [
        call(
            partial(gather_kernel, layers, [(0, own * i, 3 * y + i) for i in range(3)]),
            [((6 * GROUP, WIDE), F32)],
            [],
            slope, far_unit, r,
            spaces={1: pltpu.SMEM},
        )[0]
        for y, r in enumerate(recv_y)
    ]
    back_y = [exchange(m, 0, i + 1) for i, m in enumerate(answer_y)]
    (near_answer,) = call(
        partial(gather_kernel, layers, [(0, 0, 0), (1, 0, 1)]),
        [((4 * GROUP, WIDE), F32)],
        [],
        slope, near_unit, recv_a, recv_b,
        spaces={1: pltpu.SMEM},
    )
    blocks, early = square[0] // BLOCK, 2
    units = order.shape[1] // blocks + layers
    (early_value,) = call(
        partial(stay_gather_kernel, layers, 0),
        [((early, 2 * units, WIDE), F32)],
        [],
        slope, order, unit,
        spaces={2: pltpu.SMEM},
    )
    answer_a, answer_b = call(
        partial(reply_kernel, nyc),
        [((2 * nyc * GROUP, WIDE), F32)] * 2,
        [],
        near_answer, early_value, *back_y,
        spaces={1: pl.ANY},
    )
    back_a, back_b = exchange(answer_a, 1, 0), exchange(answer_b, 2, 0)
    late_value, final_warmth = call(
        partial(late_gather_kernel, layers, early),
        [((blocks - early, 2 * units, WIDE), F32), (tile, F32)],
        [pltpu.SemaphoreType.DMA(())],
        slope, order, unit, warmth,
        spaces={2: pltpu.SMEM},
        out_spaces={1: pltpu.HBM},
    )
    (pull,) = call(
        partial(unpack_kernel, nyc),
        [((2, cells), F32)],
        [vmem(4 * (table + units), WIDE)],
        back_a, back_b, *back_y, early_value, late_value, place, power,
    )
    return final_warmth, pull


def solution(mesh):
    cell = P(("gx", "gy"))
    tile = P(None, "gx", "gy")
    return jax.shard_map(
        shards,
        mesh=mesh,
        in_specs=(cell, cell, cell, cell, cell, tile, P()),
        out_specs=(tile, P(None, ("gx", "gy"))),
        check_vma=False,
    )
```
